32 devices in a mesh: line: 4 (over y, core), block: 8 (over z, x).
Axes of the slice: x: 2, y: 2, z: 4, core: 2. Of those that a mesh axis runs over, the one named last changes fastest.
Arguments:
- residual: float32 [6, 32, 15, 1024], P(None, 'line', None, 'block'), may hold values from -6 to 6
- adjoint: float32 [6, 32, 15, 1024], P(None, 'line', None, 'block'), may hold values from -6 to 6
- i_factors: float32 [8, 2, 6, 32, 8], P('block', None, None, 'line'), as said below
- k_factors: float32 [4, 2, 6, 1024, 128], P('line', None, None, 'block'), as said below
- couplings: float32 [4, 8, 4, 3, 6], P('line', 'block')
- receptor_cell: int32 [4, 8, 8, 2048], P('line', 'block'), may hold values from 0 to 15359
- send_count: int32 [4, 8, 8], P('line', 'block'), may hold values from 512 to 2048, as said below
- donor_cell: int32 [4, 8, 8, 2048], P('line', 'block'), may hold values from 0 to 13310, as said below
- donor_weight: float32 [4, 8, 3, 8, 2048], P('line', 'block'), may hold values from 0 to 1
Outputs:
- update: float32 [6, 32, 15, 1024], P(None, 'line', None, 'block')
The draws below stay inside these ranges and needn't reach their ends.
Inputs may be any that keep to these rules, and one draw needn't show every extreme that they name: The first send_count slots of each device for each donor owner are live. In each group along block one donor owner receives exactly 2048 live slots from every source device of the group; every other owner receives at most 1280 live slots from each source, and some source sends exactly that many to some owner. `donor_cell`: numbered within the owner's block; its base cell has i < 7, j < 14 and k < 127 in the block, so that all eight donor cells lie in the block. `receptor_cell`: numbered within the sending device's block; entries of slots that are not live are arbitrary. `i_factors`: each segment matrix is lower triangular with a diagonal between 0.8 and 1.2. `k_factors`: each segment matrix is lower triangular with a diagonal between 0.8 and 1.2.
All inputs are finite; a program needn't handle non-finite values.
Results may differ from the reference program's by a relative error of at most 0.00022.
Values sent between devices are 32-bit elements; how exact they have to be, the bound alone decides.
No kernel may reach another device: no remote copies, remote signals or barrier semaphores. Data moves between devices by JAX's collectives and lax.ppermute only.
A program may use at most 320 MiB of HBM per device.

```python
import jax
import jax.numpy as jnp
from jax import lax

FIELD_COUNT = 6
CI = 8
CJ = 15
CK = 128
CAP = 2048
NI = 32
NJ = 15
NK = 1024
N_LINE = 4
N_BLOCK = 8


def make_factor(key, leading, segments, length, chain_count):
    lookup_keys = jax.random.split(key, 6)
    slow_count = 3
    ranks = jnp.stack([jax.random.permutation(lookup_keys[0], FIELD_COUNT), jax.random.permutation(lookup_keys[1], FIELD_COUNT)])
    slow_field = (ranks < slow_count)[None, :, :, None, None, None]
    rate_shape = (leading, 2, FIELD_COUNT, segments, 1, 1)
    slow_rate = jnp.exp(jax.random.uniform(lookup_keys[2], rate_shape, jnp.float32, jnp.log(0.3), jnp.log(1.2))) / (length * chain_count)
    fast_rate = jnp.exp(jax.random.uniform(lookup_keys[3], rate_shape, jnp.float32, jnp.log(1.5), jnp.log(2.5))) / min(length, 40)
    rate = jnp.where(slow_field, slow_rate, fast_rate)
    row_index = jnp.arange(length)[:, None]
    col_index = jnp.arange(length)[None, :]
    distance = jnp.maximum(row_index - col_index, 0).astype(jnp.float32)
    full_shape = (leading, 2, FIELD_COUNT, segments, length, length)
    jitter = jax.random.uniform(lookup_keys[4], full_shape, jnp.float32, 0.85, 1.15)
    below = jnp.exp(-rate * distance) * jitter / jnp.sqrt(jnp.float32(length))
    diagonal = jax.random.uniform(lookup_keys[5], full_shape, jnp.float32, 0.8, 1.2)
    matrix = jnp.where(row_index > col_index, below, jnp.where(row_index == col_index, diagonal, 0.0))
    return matrix.reshape(leading, 2, FIELD_COUNT, segments * length, length)


def draw_i_factors(key, part):
    return make_factor(key, N_BLOCK, N_LINE, CI, N_LINE)


def draw_k_factors(key, part):
    return make_factor(key, N_LINE, N_BLOCK, CK, N_BLOCK)


def draw_couplings(key, part):
    lookup_keys = jax.random.split(key, 3)
    lowest = jnp.array([0.4, 0.05, 0.3], jnp.float32).reshape(1, 1, 1, 3, 1)
    highest = jnp.array([0.55, 0.12, 0.45], jnp.float32).reshape(1, 1, 1, 3, 1)
    shape = (N_LINE, N_BLOCK, 4, 3, FIELD_COUNT)
    spread = jax.random.uniform(lookup_keys[0], shape, jnp.float32)
    table_entries = lowest + (highest - lowest) * spread
    chain_lengths = jnp.array([CI, CI, CK, CK], jnp.float32).reshape(1, 1, 4, 1, 1)
    group_selection = jax.random.uniform(lookup_keys[1], (N_LINE, N_BLOCK, 4, 1, FIELD_COUNT), jnp.float32)
    group_length = jax.random.uniform(lookup_keys[2], (N_LINE, N_BLOCK, 4, 1, FIELD_COUNT), jnp.float32, 0.5, 0.8)
    donor_group = jnp.where(group_selection < 0.15, group_length, 1.0)
    return table_entries * jnp.sqrt(chain_lengths) * donor_group


def draw_send_count(key, part):
    lookup_keys = jax.random.split(key, 2)
    head_most = 5 * CAP // 8
    background = jax.random.randint(lookup_keys[0], (N_LINE, N_BLOCK, N_BLOCK), CAP // 4, head_most + 1)
    hottest = jax.random.randint(lookup_keys[1], (N_LINE, 1, 1), 0, N_BLOCK)
    owners = jnp.arange(N_BLOCK, dtype=jnp.int32)[None, None, :]
    second = (hottest + 1) % N_BLOCK
    background = jnp.where(owners == second, head_most, background)
    return jnp.where(owners == hottest, CAP, background).astype(jnp.int32)


def draw_donor_cell(key, part):
    lookup_keys = jax.random.split(key, 3)
    shape = (N_LINE, N_BLOCK, N_BLOCK, CAP)
    along_i = jax.random.randint(lookup_keys[0], shape, 0, CI - 1)
    along_j = jax.random.randint(lookup_keys[1], shape, 0, NJ - 1)
    along_k = jax.random.randint(lookup_keys[2], shape, 0, CK - 1)
    return (along_i * NJ * CK + along_j * CK + along_k).astype(jnp.int32)


def place_ends(drawn, stream_key, low, high):
    longest = drawn.shape.index(max(drawn.shape))
    spots = []
    for shift in (0, 1):
        where = [jax.random.randint(jax.random.fold_in(stream_key, axis), (), 0, length) for axis, length in enumerate(drawn.shape)]
        where[longest] = (where[longest] + shift) % drawn.shape[longest]
        spots.append(tuple(where))
    return drawn.at[spots[0]].set(low).at[spots[1]].set(high)


def block_levels(stream_key, shape, cuts, low, largest):
    gain, own = 1.0, jax.random.fold_in(stream_key, 6)
    for position, blocks in cuts:
        draws = jnp.exp(jax.random.uniform(jax.random.fold_in(own, position), (blocks,), jnp.float32, low / len(cuts), largest / len(cuts)))
        gain = gain * jnp.repeat(draws, shape[position] // blocks).reshape([-1 if axis == position else 1 for axis in range(len(shape))])
    return gain


def gaussian(stream_key, dims, width, most, cuts=(), held_as=jnp.bfloat16):
    drawn = jax.random.normal(stream_key, dims, jnp.float32) * width
    if len(cuts) > 0:
        drawn = block_levels(stream_key, dims, cuts, -0.22, 0.18) * drawn
    return jnp.clip(drawn, min=-most, max=most).astype(held_as)


def setup_inputs(seed: int = 0) -> dict:
    arg_keys = jax.random.split(jax.random.key(seed), 10)
    residual = gaussian(arg_keys[0], (FIELD_COUNT, NI, NJ, NK), 1.0, 6.0, ((1, 4), (3, 8)), jnp.float32)
    adjoint = gaussian(arg_keys[1], (FIELD_COUNT, NI, NJ, NK), 1.0, 6.0, ((1, 4), (3, 8)), jnp.float32)
    i_factors = draw_i_factors(jax.random.fold_in(arg_keys[9], 71), 0)
    k_factors = draw_k_factors(jax.random.fold_in(arg_keys[9], 71), 0)
    couplings = draw_couplings(jax.random.fold_in(arg_keys[9], 71), 0)
    receptor_cell = place_ends(jax.random.randint(arg_keys[5], (N_LINE, N_BLOCK, N_BLOCK, CAP), 0, CI * CJ * CK), jax.random.fold_in(arg_keys[5], 1), 0, (CI * CJ * CK) - 1).astype(jnp.int32)
    send_count = draw_send_count(jax.random.fold_in(arg_keys[9], 71), 0)
    donor_cell = draw_donor_cell(jax.random.fold_in(arg_keys[9], 71), 0)
    donor_weight = jnp.clip(1.0 * jax.random.uniform(arg_keys[8], (N_LINE, N_BLOCK, 3, N_BLOCK, CAP), jnp.float32) ** block_levels(arg_keys[8], (N_LINE, N_BLOCK, 3, N_BLOCK, CAP), ((0, 4), (1, 8)), -0.2, 0.2), 0.0, 1.0)
    return dict(residual=residual, adjoint=adjoint, i_factors=i_factors, k_factors=k_factors, couplings=couplings, receptor_cell=receptor_cell, send_count=send_count, donor_cell=donor_cell, donor_weight=donor_weight)


def coupling_matrix(triple):
    zeros_part = jnp.zeros_like(triple[..., 0, :])
    upper_row = jnp.stack([triple[..., 0, :], triple[..., 1, :]], axis=-1)
    lower_row = jnp.stack([triple[..., 2, :], zeros_part], axis=-1)
    return jnp.stack([upper_row, lower_row], axis=-2)


def chain_solve(columns, factors, couplings):
    fields = columns.shape[0]
    segments = factors.shape[0]
    length = factors.shape[2]
    incoming = jnp.zeros((fields, 2, columns.shape[2]), jnp.float32)
    pieces = []
    for segment in range(segments):
        block_data = columns[:, segment * length:(segment + 1) * length]
        homogeneous = jnp.einsum('fpq,fql->fpl', factors[segment], block_data, precision=lax.Precision.HIGHEST)
        influence = jnp.einsum('fpa,fab->fpb', factors[segment][:, :, 0:2], couplings[segment], precision=lax.Precision.HIGHEST)
        solved = homogeneous - jnp.einsum('fpa,fal->fpl', influence, incoming, precision=lax.Precision.HIGHEST)
        incoming = jnp.stack([solved[:, -1], solved[:, -2]], axis=1)
        pieces.append(solved)
    return jnp.concatenate(pieces, axis=1)


def both_ways(columns, lower, upper, couple_lower, couple_upper):
    forward = chain_solve(columns, lower, couple_lower)
    return jnp.flip(chain_solve(jnp.flip(forward, 1), upper[::-1], couple_upper[::-1]), 1)


def spread_donors(right_side, incoming, donor_cell, donor_weight, cells_j, cells_k):
    fields = right_side.shape[0]
    base_cell = donor_cell.reshape(-1)
    fractions = donor_weight.reshape(3, -1)
    values = incoming.reshape(fields, -1)
    index_list = []
    weight_list = []
    for corner in range(8):
        step_i = corner // 4
        step_j = (corner // 2) % 2
        step_k = corner % 2
        along_i = fractions[0] if step_i else 1.0 - fractions[0]
        along_j = fractions[1] if step_j else 1.0 - fractions[1]
        along_k = fractions[2] if step_k else 1.0 - fractions[2]
        weight_list.append(along_i * along_j * along_k)
        index_list.append(base_cell + step_i * cells_j * cells_k + step_j * cells_k + step_k)
    targets = jnp.concatenate(index_list)
    weights = jnp.concatenate(weight_list)
    spread = jnp.tile(values, (1, 8)) * weights[None, :]
    return right_side.at[:, targets].add(spread)


def to_blocks(grid):
    shaped = grid.reshape(FIELD_COUNT, N_LINE, CI, NJ, N_BLOCK, CK).transpose(1, 4, 0, 2, 3, 5)
    return shaped.reshape(N_LINE * N_BLOCK, FIELD_COUNT, CI * NJ * CK)


def from_blocks(blocks):
    shaped = blocks.reshape(N_LINE, N_BLOCK, FIELD_COUNT, CI, NJ, CK).transpose(2, 0, 3, 4, 1, 5)
    return shaped.reshape(FIELD_COUNT, NI, NJ, NK)


def reference(residual, adjoint, i_factors, k_factors, couplings, receptor_cell, send_count, donor_cell, donor_weight):
    adjoint_blocks = to_blocks(adjoint)
    receptors = receptor_cell.reshape(N_LINE * N_BLOCK, N_BLOCK * CAP)
    picked = lax.map(lambda pair: pair[0][:, pair[1]], (adjoint_blocks, receptors))
    picked = picked.reshape(N_LINE, N_BLOCK, FIELD_COUNT, N_BLOCK, CAP)
    active = jnp.arange(CAP, dtype=jnp.int32)[None, None, None, :] < send_count[:, :, :, None]
    outgoing = jnp.where(active[:, :, None], picked, 0.0)
    incoming = outgoing.transpose(0, 3, 2, 1, 4).reshape(N_LINE * N_BLOCK, FIELD_COUNT, N_BLOCK, CAP)
    residual_blocks = to_blocks(residual)
    combined = lax.map(
        lambda group: spread_donors(group[0], group[1], group[2], group[3], NJ, CK),
        (residual_blocks, incoming, donor_cell.reshape(N_LINE * N_BLOCK, N_BLOCK, CAP),
         donor_weight.reshape(N_LINE * N_BLOCK, 3, N_BLOCK, CAP)))
    right_side = from_blocks(combined)

    i_parts = []
    for block_index in range(N_BLOCK):
        columns = right_side[:, :, :, block_index * CK:(block_index + 1) * CK].reshape(FIELD_COUNT, NI, NJ * CK)
        lower = i_factors[block_index, 0].reshape(FIELD_COUNT, N_LINE, CI, CI).transpose(1, 0, 2, 3)
        upper = i_factors[block_index, 1].reshape(FIELD_COUNT, N_LINE, CI, CI).transpose(1, 0, 2, 3)
        couple_lower = coupling_matrix(couplings[:, block_index, 0])
        couple_upper = coupling_matrix(couplings[:, block_index, 1])
        solved = both_ways(columns, lower, upper, couple_lower, couple_upper)
        i_parts.append(solved.reshape(FIELD_COUNT, NI, NJ, CK))
    after_i = jnp.concatenate(i_parts, axis=3)

    k_parts = []
    for line_index in range(N_LINE):
        columns = after_i[:, line_index * CI:(line_index + 1) * CI].reshape(FIELD_COUNT, CI * NJ, NK).transpose(0, 2, 1)
        lower = k_factors[line_index, 0].reshape(FIELD_COUNT, N_BLOCK, CK, CK).transpose(1, 0, 2, 3)
        upper = k_factors[line_index, 1].reshape(FIELD_COUNT, N_BLOCK, CK, CK).transpose(1, 0, 2, 3)
        couple_lower = coupling_matrix(couplings[line_index, :, 2])
        couple_upper = coupling_matrix(couplings[line_index, :, 3])
        solved = both_ways(columns, lower, upper, couple_lower, couple_upper)
        k_parts.append(solved.transpose(0, 2, 1).reshape(FIELD_COUNT, CI, NJ, NK))
    return jnp.concatenate(k_parts, axis=1)
```

```python
import functools

import jax
import jax.numpy as jnp
from jax import lax
from jax.experimental import pallas as pl
from jax.experimental.pallas import tpu as pltpu
from jax.sharding import PartitionSpec as P

LANES = 128
HIGHEST = lax.Precision.HIGHEST
F32 = jnp.float32
BF16 = jnp.bfloat16


def split(x):
    high = x.astype(BF16)
    return high, (x - high.astype(F32)).astype(BF16)


def dot_nt(a, b, precision=None):
    return lax.dot_general(
        a, b, (((1,), (1,)), ((), ())), precision=precision, preferred_element_type=F32
    )


def dot_nn(a, b, precision=None):
    return lax.dot_general(
        a, b, (((1,), (0,)), ((), ())), precision=precision, preferred_element_type=F32
    )


def dot_tn(a, b, precision=None):
    return lax.dot_general(
        a, b, (((0,), (0,)), ((), ())), precision=precision, preferred_element_type=F32
    )


def split_cell(cell, cells_i, cells_j):
    row = lax.shift_right_logical(cell, 7)
    k = lax.bitwise_and(cell, LANES - 1)
    i = jnp.zeros_like(row)
    for m in range(1, cells_i):
        i = i + (row >= m * cells_j).astype(jnp.int32)
    return i, row - i * cells_j, k


def col(x, c):
    return jnp.broadcast_to(x[:, c : c + 1], x.shape)


def gather_kernel(count_ref, cell_ref, field_ref, out_ref, high_ref, low_ref, *, chunk):
    fields, cells_i, cells_j, _ = field_ref.shape
    owners, capacity = cell_ref.shape
    rows_j = 16
    half_i = cells_i // 2
    rows = half_i * rows_j
    for f in range(fields):
        for i in range(cells_i):
            part = jnp.concatenate(
                [field_ref[f, i], jnp.zeros((rows_j - cells_j, LANES), F32)], axis=0
            )
            high, low = split(part)
            at = (f * half_i + i // 2) * rows_j
            lane = (i % 2) * LANES
            high_ref[at : at + rows_j, lane : lane + LANES] = high
            low_ref[at : at + rows_j, lane : lane + LANES] = low
    out_ref[...] = jnp.zeros(out_ref.shape, F32)
    per = chunk // LANES
    slot_rows = capacity // LANES

    def owner_body(d, carry):
        count = count_ref[d]

        def chunk_body(c, carry):
            start = pl.multiple_of(c * chunk, chunk)
            cell = cell_ref[pl.ds(d, 1), pl.ds(start, chunk)]
            i, j, k = split_cell(cell, cells_i, cells_j)
            slot = start + lax.broadcasted_iota(jnp.int32, cell.shape, 1)
            row = lax.shift_right_logical(i, 1) * rows_j + j
            row = jnp.where(slot < count, row, -1)
            column = lax.bitwise_and(i, 1) * LANES + k
            hot = lax.broadcasted_iota(jnp.int32, (2 * LANES, chunk), 0) == column
            hot = jnp.where(hot, 1.0, 0.0).astype(BF16)
            found = dot_nn(high_ref[...], hot) + dot_nn(low_ref[...], hot)
            pick = lax.broadcasted_iota(jnp.int32, (rows, chunk), 0) == row
            for f in range(fields):
                value = jnp.where(pick, found[f * rows : (f + 1) * rows], 0.0)
                value = jnp.sum(value, axis=0, keepdims=True)
                for q in range(per):
                    out_ref[d, pl.ds(f * slot_rows + c * per + q, 1), :] = value[
                        :, q * LANES : (q + 1) * LANES
                    ]
            return carry

        return lax.fori_loop(0, lax.div(count + (chunk - 1), chunk), chunk_body, carry)

    lax.fori_loop(0, owners, owner_body, 0)


def gather(count, cell, field, chunk=512):
    fields, cells_i, _, _ = field.shape
    owners, capacity = cell.shape
    table = (fields * cells_i // 2 * 16, 2 * LANES)
    return pl.pallas_call(
        functools.partial(gather_kernel, chunk=chunk),
        out_shape=jax.ShapeDtypeStruct((owners, fields * capacity // LANES, LANES), F32),
        in_specs=[
            pl.BlockSpec(memory_space=pltpu.SMEM),
            pl.BlockSpec(memory_space=pltpu.VMEM),
            pl.BlockSpec(memory_space=pltpu.VMEM),
        ],
        out_specs=pl.BlockSpec(memory_space=pltpu.VMEM),
        scratch_shapes=[pltpu.VMEM(table, BF16), pltpu.VMEM(table, BF16)],
        name="gather",
    )(count, cell, field)


def prepare_kernel(
    couple_ref, i_ref, k_ref, i_out, k_tile, k_map, k_rows, k_carry, f_ref, *, cells_i
):
    fields, length = k_ref.shape[1], k_ref.shape[2]
    lower, upper, edge = i_ref[0], i_ref[1], i_ref[2]
    lane = lax.broadcasted_iota(jnp.int32, (8, LANES), 1)

    def edges(matrix, at):
        e0, e1, e2 = col(edge, at), col(edge, at + 1), col(edge, at + 2)
        table = []
        for p in range(cells_i):
            first, second = col(matrix, p * cells_i), col(matrix, p * cells_i + 1)
            table.append((first * e0 + second * e2, first * e1))
        return table

    low_edge = edges(lower, 0)
    up_edge = edges(upper, 3)
    through = []
    for p in range(cells_i):
        total = [jnp.zeros((8, LANES), F32), jnp.zeros((8, LANES), F32)]
        for q in range(p + 1):
            factor = col(upper, p * cells_i + q)
            for a in range(2):
                total[a] = total[a] + factor * low_edge[cells_i - 1 - q][a]
        through.append(total)
    last, prior = cells_i - 1, cells_i - 2
    entries = []
    for table in (through, up_edge):
        for p in range(cells_i):
            entries += [table[p][0], table[p][1]]
    entries += [-low_edge[last][0], -low_edge[last][1], -low_edge[prior][0], -low_edge[prior][1]]
    entries += [-up_edge[last][0], -up_edge[last][1], -up_edge[prior][0], -up_edge[prior][1]]
    entries += [through[last][0], through[last][1], through[prior][0], through[prior][1]]
    tile = jnp.zeros((8, LANES), F32)
    for at, entry in enumerate(entries):
        tile = jnp.where(lane == at, entry, tile)
    i_out[...] = tile

    row8 = lax.broadcasted_iota(jnp.int32, (8, LANES), 0)
    row_n = lax.broadcasted_iota(jnp.int32, (length, length), 0)
    lane_n = lax.broadcasted_iota(jnp.int32, (length, length), 1)
    turn = jnp.where(row_n + lane_n == length - 1, 1.0, 0.0).astype(F32)

    def edge_rows(direction, f):
        e0 = couple_ref[direction, 0, f]
        e1 = couple_ref[direction, 1, f]
        e2 = couple_ref[direction, 2, f]
        first = jnp.where((row8 == 0) & (lane == 0), e0, 0.0)
        first = jnp.where((row8 == 0) & (lane == 1), e2, first)
        return jnp.where((row8 == 1) & (lane == 0), e1, first)

    f_ref[...] = jnp.zeros(f_ref.shape, F32)
    k_carry[...] = jnp.zeros(k_carry.shape, F32)
    for f in range(fields):
        low, up = k_ref[0, f], k_ref[1, f]
        whole = dot_nn(up, dot_nn(turn, low, HIGHEST), HIGHEST)
        whole = dot_nn(turn, whole, HIGHEST)
        k_map[f] = whole
        k_rows[f, 0:1, :] = low[length - 1 : length]
        k_rows[f, 1:2, :] = low[length - 2 : length - 1]
        k_rows[f, 2:4, :] = whole[0:2]
        k_rows[f, 4:8, :] = jnp.zeros((4, length), F32)
        low_rows = dot_nt(edge_rows(2, f), low, HIGHEST)
        flipped = dot_nn(low_rows, turn, HIGHEST)
        across = dot_nt(flipped, up, HIGHEST)
        up_rows = dot_nt(edge_rows(3, f), up, HIGHEST)
        both = jnp.concatenate([across[0:2], up_rows[0:2], jnp.zeros((4, length), F32)], axis=0)
        both = dot_nn(both, turn, HIGHEST)
        for a in range(4):
            k_carry[a, f : f + 1, :] = both[a : a + 1]
        for a in range(2):
            f_ref[a, f : f + 1, :] = low_rows[a : a + 1]
    end = length - 1
    entries = [
        -col(f_ref[0], end),
        -col(f_ref[1], end),
        -col(f_ref[0], end - 1),
        -col(f_ref[1], end - 1),
        -col(k_carry[2], 0),
        -col(k_carry[3], 0),
        -col(k_carry[2], 1),
        -col(k_carry[3], 1),
        col(k_carry[0], 0),
        col(k_carry[1], 0),
        col(k_carry[0], 1),
        col(k_carry[1], 1),
    ]
    tile = jnp.zeros((8, LANES), F32)
    for at, entry in enumerate(entries):
        tile = jnp.where(lane == at, entry, tile)
    k_tile[...] = tile


def prepare(couplings, i_tiles, k_factors, cells_i):
    fields, length = k_factors.shape[1], k_factors.shape[2]
    return pl.pallas_call(
        functools.partial(prepare_kernel, cells_i=cells_i),
        out_shape=(
            jax.ShapeDtypeStruct((8, LANES), F32),
            jax.ShapeDtypeStruct((8, LANES), F32),
            jax.ShapeDtypeStruct((fields, length, length), F32),
            jax.ShapeDtypeStruct((fields, 8, length), F32),
            jax.ShapeDtypeStruct((4, 8, length), F32),
        ),
        in_specs=[
            pl.BlockSpec(memory_space=pltpu.SMEM),
            pl.BlockSpec(memory_space=pltpu.VMEM),
            pl.BlockSpec(memory_space=pltpu.VMEM),
        ],
        out_specs=(pl.BlockSpec(memory_space=pltpu.VMEM),) * 5,
        scratch_shapes=[pltpu.VMEM((2, 8, length), F32)],
        name="prepare",
    )(couplings, i_tiles, k_factors)


def mat2(a, b):
    return [
        a[0] * b[0] + a[1] * b[2],
        a[0] * b[1] + a[1] * b[3],
        a[2] * b[0] + a[3] * b[2],
        a[2] * b[1] + a[3] * b[3],
    ]


def downstream_map(tiles, base, mine):
    peers = len(tiles)
    total = [jnp.zeros((8, LANES), F32)] * 4
    for m in range(1, peers):
        entry = [col(tiles[m], base + c) for c in range(12)]
        step = mat2(mat2(entry[4:8], total), entry[0:4])
        total = [
            jnp.where(m > mine, new - back, old) for new, back, old in zip(step, entry[8:12], total)
        ]
    return total


def scatter_kernel(*refs, peers, chunk, base):
    mine_ref, solve_ref, got_ref, cell_ref, weight_ref, residual_ref = refs[:6]
    tile_refs = refs[6 : 6 + peers]
    start_ref = refs[6 + peers]
    send_refs = refs[7 + peers : 7 + 2 * peers]
    total_ref = refs[7 + 2 * peers]
    fields, cells_i, cells_j, _ = residual_ref.shape
    sources, capacity = cell_ref.shape
    rows_j = 16
    per = chunk // LANES
    slot_rows = capacity // LANES
    total_ref[...] = jnp.zeros(total_ref.shape, F32)

    def source_body(b, carry):
        def chunk_body(c, carry):
            start = pl.multiple_of(c * chunk, chunk)
            cell = cell_ref[pl.ds(b, 1), pl.ds(start, chunk)]
            x = weight_ref[0, pl.ds(b, 1), pl.ds(start, chunk)]
            y = weight_ref[1, pl.ds(b, 1), pl.ds(start, chunk)]
            z = weight_ref[2, pl.ds(b, 1), pl.ds(start, chunk)]
            i, j, k = split_cell(cell, cells_i, cells_j)

            def hat(size, at, t):
                place = lax.broadcasted_iota(jnp.int32, (size, chunk), 0)
                return jnp.where(place == at, 1.0 - t, jnp.where(place == at + 1, t, 0.0))

            along_i = hat(8, i, x)
            along_j = hat(rows_j, j, y)
            k_high, k_low = split(hat(LANES, k, z))
            along_k = jnp.concatenate([k_high, k_low], axis=0)
            highs = []
            lows = []
            for f in range(fields):
                value = jnp.concatenate(
                    [
                        got_ref[b, pl.ds(f * slot_rows + c * per + q, 1), :]
                        for q in range(per)
                    ],
                    axis=1,
                )
                scaled = along_i * value
                for p in range(cells_i):
                    high, low = split(scaled[p : p + 1] * along_j)
                    highs.append(high)
                    lows.append(low)
            high = jnp.concatenate(highs, axis=0)
            low = jnp.concatenate(lows, axis=0)
            total_ref[...] += dot_nt(high, along_k) + dot_nt(low, along_k)
            return carry

        return lax.fori_loop(0, capacity // chunk, chunk_body, carry)

    lax.fori_loop(0, sources, source_body, 0)

    mine = mine_ref[0]
    tiles = [ref[...] for ref in tile_refs]
    onward = downstream_map(tiles, base, mine)
    turned = mat2([col(tiles[0], base + 4 + c) for c in range(4)], onward)
    pad = jnp.zeros((rows_j - cells_j, LANES), F32)
    for f in range(fields):
        data = []
        for i in range(cells_i):
            at = (f * cells_i + i) * rows_j
            spread = total_ref[at : at + rows_j]
            spread = spread[:, :LANES] + spread[:, LANES:]
            data.append(spread + jnp.concatenate([residual_ref[f, i], pad], axis=0))

        def solve(direction, columns):
            result = []
            for p in range(cells_i):
                value = solve_ref[direction, f, p * cells_i] * columns[0]
                for q in range(1, p + 1):
                    value = value + solve_ref[direction, f, p * cells_i + q] * columns[q]
                result.append(value)
            return result

        first = solve(0, data)
        second = solve(1, first[::-1])
        e0, e1 = first[-1], first[-2]
        g0, g1 = second[-1], second[-2]
        m = [jnp.broadcast_to(entry[f : f + 1], (rows_j, LANES)) for entry in turned]
        h0 = g0 + m[0] * e0 + m[1] * e1
        h1 = g1 + m[2] * e0 + m[3] * e1
        for i in range(cells_i):
            at = (f * cells_i + i) * rows_j
            start_ref[at : at + rows_j] = second[cells_i - 1 - i]
        for shift in range(peers):
            ahead = mine + shift < peers
            at = f * rows_j
            send_refs[shift][at : at + rows_j] = jnp.where(ahead, e0, h0)
            at = (fields + f) * rows_j
            send_refs[shift][at : at + rows_j] = jnp.where(ahead, e1, h1)


def scatter(mine, solve_tiles, got, cell, weight, residual, tiles, base, chunk=512):
    fields, cells_i, _, _ = residual.shape
    peers = len(tiles)
    rows = fields * cells_i * 16
    vmem = pl.BlockSpec(memory_space=pltpu.VMEM)
    smem = pl.BlockSpec(memory_space=pltpu.SMEM)
    return pl.pallas_call(
        functools.partial(scatter_kernel, peers=peers, chunk=chunk, base=base),
        out_shape=(jax.ShapeDtypeStruct((rows, LANES), F32),)
        + (jax.ShapeDtypeStruct((2 * fields * 16, LANES), F32),) * peers,
        in_specs=[smem, smem, vmem, vmem, vmem, vmem] + [vmem] * peers,
        out_specs=(vmem,) * (1 + peers),
        scratch_shapes=[pltpu.VMEM((rows, 2 * LANES), F32)],
        name="scatter",
    )(mine, solve_tiles, got, cell, weight, residual, *tiles)


def middle_kernel(*refs, peers, base, fields, cells_i):
    mine_ref, own_ref, start_ref, map_ref, rows_ref, k_tile_ref = refs[:6]
    tile_refs = refs[6 : 6 + peers]
    got_refs = refs[6 + peers : 6 + 2 * peers]
    out_ref, send_ref, field_ref, end_ref = refs[6 + 2 * peers :]
    rows_j = 16
    mine = mine_ref[0]
    tiles = [ref[...] for ref in tile_refs]
    onward = downstream_map(tiles, base, mine)
    forward = [[col(tile, base + c) for c in range(4)] for tile in tiles]
    backward = [[col(tile, base + 4 + c) for c in range(4)] for tile in tiles]
    end_ref[...] = jnp.zeros(end_ref.shape, F32)
    rows = cells_i * rows_j
    for f in range(fields):

        def wide(entry):
            return jnp.broadcast_to(entry[f : f + 1], (rows_j, LANES))

        def advance(matrix, state, add):
            m = [wide(entry) for entry in matrix]
            return [
                m[0] * state[0] + m[1] * state[1] + add[0],
                m[2] * state[0] + m[3] * state[1] + add[1],
            ]

        got = []
        for shift in range(peers):
            low = got_refs[shift][f * rows_j : (f + 1) * rows_j]
            high = got_refs[shift][(fields + f) * rows_j : (fields + f + 1) * rows_j]
            got.append((low, high))
        zero = jnp.zeros((rows_j, LANES), F32)
        before = [zero, zero]
        for shift in range(peers - 1, 0, -1):
            new = advance(forward[shift], before, got[shift])
            before = [jnp.where(shift <= mine, n, o) for n, o in zip(new, before)]
        after = [zero, zero]
        for shift in range(1, peers):
            new = advance(backward[shift], after, got[shift])
            after = [jnp.where(shift > mine, n, o) for n, o in zip(new, after)]
        onto = advance(forward[0], before, got[0])
        after = advance(onward, onto, after)
        for p in range(cells_i):
            at = (f * cells_i + cells_i - 1 - p) * rows_j
            value = start_ref[at : at + rows_j]
            value = value - own_ref[f, 2 * p] * before[0] - own_ref[f, 2 * p + 1] * before[1]
            shift = 2 * cells_i
            value = value - own_ref[f, shift + 2 * p] * after[0]
            value = value - own_ref[f, shift + 2 * p + 1] * after[1]
            field_ref[at : at + rows_j] = value
        block = field_ref[f * rows : (f + 1) * rows]
        out_ref[f * rows : (f + 1) * rows] = dot_nt(block, map_ref[f], HIGHEST)
        ends = dot_nt(rows_ref[f], block, HIGHEST)
        for a in range(4):
            end_ref[a * 8 + f : a * 8 + f + 1, :] = ends[a : a + 1]
    end_ref[32:40] = k_tile_ref[...]
    for d in range(send_ref.shape[0]):
        send_ref[d] = end_ref[...]


def middle(mine, own, start, k_map, k_rows, k_tile, tiles, got, base, owners, fields, cells_i):
    peers = len(tiles)
    vmem = pl.BlockSpec(memory_space=pltpu.VMEM)
    smem = pl.BlockSpec(memory_space=pltpu.SMEM)
    return pl.pallas_call(
        functools.partial(middle_kernel, peers=peers, base=base, fields=fields, cells_i=cells_i),
        out_shape=(
            jax.ShapeDtypeStruct(start.shape, F32),
            jax.ShapeDtypeStruct((owners, 40, LANES), F32),
        ),
        in_specs=[smem, smem] + [vmem] * (4 + 2 * peers),
        out_specs=(vmem, vmem),
        scratch_shapes=[pltpu.VMEM(start.shape, F32), pltpu.VMEM((40, LANES), F32)],
        name="middle",
    )(mine, own, start, k_map, k_rows, k_tile, *tiles, *got)


def finish_kernel(mine_ref, start_ref, got_ref, carry_ref, out_ref):
    fields, cells_i, cells_j, _ = out_ref.shape
    rows_j = 16
    rows = cells_i * rows_j
    blocks = got_ref.shape[0]
    mine = mine_ref[0]
    zero = jnp.zeros((8, LANES), F32)
    entry = [[col(got_ref[m, 32:40], c) for c in range(12)] for m in range(blocks)]
    part = [[got_ref[m, 8 * a : 8 * a + 8] for a in range(4)] for m in range(blocks)]
    states = []
    state = [zero, zero]
    for m in range(blocks):
        states.append(state)
        p = entry[m]
        state = [
            p[0] * state[0] + p[1] * state[1] + part[m][0],
            p[2] * state[0] + p[3] * state[1] + part[m][1],
        ]
    before = [zero, zero]
    after = [zero, zero]
    state = [zero, zero]
    for m in range(blocks - 1, -1, -1):
        here = m == mine
        before = [jnp.where(here, n, o) for n, o in zip(states[m], before)]
        after = [jnp.where(here, n, o) for n, o in zip(state, after)]
        q, b = entry[m][4:8], entry[m][8:12]
        old = states[m]
        state = [
            q[0] * state[0] + q[1] * state[1] + part[m][2] - b[0] * old[0] - b[1] * old[1],
            q[2] * state[0] + q[3] * state[1] + part[m][3] - b[2] * old[0] - b[3] * old[1],
        ]
    for f in range(fields):
        carried = jnp.concatenate(
            [x[f : f + 1] for x in (before[0], before[1], after[0], after[1])]
            + [jnp.zeros((4, LANES), F32)],
            axis=0,
        )
        response = jnp.concatenate(
            [carry_ref[a, f : f + 1, :] for a in range(4)] + [jnp.zeros((4, LANES), F32)], axis=0
        )
        change = dot_tn(carried, response, HIGHEST)
        value = start_ref[f * rows : (f + 1) * rows] - change
        for i in range(cells_i):
            out_ref[f, i] = value[i * rows_j : i * rows_j + cells_j]


def finish(mine, start, got, carry, shape):
    vmem = pl.BlockSpec(memory_space=pltpu.VMEM)
    smem = pl.BlockSpec(memory_space=pltpu.SMEM)
    return pl.pallas_call(
        finish_kernel,
        out_shape=jax.ShapeDtypeStruct(shape, F32),
        in_specs=[smem, vmem, vmem, vmem],
        out_specs=vmem,
        name="finish",
    )(mine, start, got, carry)


def per_device(
    residual,
    adjoint,
    i_factors,
    k_factors,
    couplings,
    receptor_cell,
    send_count,
    donor_cell,
    donor_weight,
):
    fields, cells_i, cells_j, cells_k = adjoint.shape
    owners = receptor_cell.shape[2]
    peers = lax.axis_size("line")
    line = lax.axis_index("line").astype(jnp.int32).reshape(1)
    block = lax.axis_index("block").astype(jnp.int32).reshape(1)
    base = 4 * cells_i

    outgoing = gather(send_count.reshape(owners), receptor_cell[0, 0], adjoint)
    incoming = lax.all_to_all(outgoing, "block", split_axis=0, concat_axis=0, tiled=True)

    square = i_factors[0].reshape(2, fields, cells_i * cells_i)
    square = jnp.pad(square, ((0, 0), (0, 8 - fields), (0, LANES - cells_i * cells_i)))
    edge = couplings[0, 0, 0:2].reshape(6, fields).T
    edge = jnp.pad(edge, ((0, 8 - fields), (0, LANES - 6)))
    i_tiles = jnp.concatenate([square, edge[None]], axis=0)
    own, k_tile, k_map, k_rows, k_carry = prepare(couplings[0, 0], i_tiles, k_factors[0], cells_i)

    def shifted(value, shift):
        return lax.ppermute(value, "line", [(s, (s + shift) % peers) for s in range(peers)])

    tiles = [own] + [shifted(own, m) for m in range(1, peers)]
    start, *ends = scatter(
        line, i_tiles, incoming, donor_cell[0, 0], donor_weight[0, 0], residual, tiles, base
    )
    got = [ends[0]] + [shifted(ends[m], m) for m in range(1, peers)]
    start, message = middle(
        line, own, start, k_map, k_rows, k_tile, tiles, got, base, owners, fields, cells_i
    )
    message = lax.all_to_all(message, "block", split_axis=0, concat_axis=0, tiled=True)
    return finish(block, start, message, k_carry, residual.shape)


def solution(mesh):
    return jax.shard_map(
        per_device,
        mesh=mesh,
        in_specs=(
            P(None, "line", None, "block"),
            P(None, "line", None, "block"),
            P("block", None, None, "line", None),
            P("line", None, None, "block", None),
            P("line", "block", None, None, None),
            P("line", "block", None, None),
            P("line", "block", None),
            P("line", "block", None, None),
            P("line", "block", None, None, None),
        ),
        out_specs=P(None, "line", None, "block"),
        check_vma=False,
    )
```

```python
import functools

import jax
import jax.numpy as jnp
from jax import lax
from jax.experimental import pallas as pl
from jax.experimental.pallas import tpu as pltpu
from jax.sharding import PartitionSpec as P

LANES = 128
HIGHEST = lax.Precision.HIGHEST
F32 = jnp.float32
BF16 = jnp.bfloat16


def split(x):
    high = x.astype(BF16)
    return high, (x - high.astype(F32)).astype(BF16)


def dot_nt(a, b, precision=None):
    return lax.dot_general(
        a, b, (((1,), (1,)), ((), ())), precision=precision, preferred_element_type=F32
    )


def dot_nn(a, b, precision=None):
    return lax.dot_general(
        a, b, (((1,), (0,)), ((), ())), precision=precision, preferred_element_type=F32
    )


def dot_tn(a, b, precision=None):
    return lax.dot_general(
        a, b, (((0,), (0,)), ((), ())), precision=precision, preferred_element_type=F32
    )


def dot3(dot, a, b, axis_a, axis_b):
    a_high, a_low = split(a)
    b_high, b_low = split(b)
    left = jnp.concatenate([a_high, a_high, a_low], axis=axis_a)
    right = jnp.concatenate([b_high, b_low, b_high], axis=axis_b)
    return dot(left, right)


def product_nt(a, b):
    return dot3(dot_nt, a, b, 1, 1)


def product_nn(a, b):
    return dot3(dot_nn, a, b, 1, 0)


def turn_lanes(x, turn):
    return dot_nn(jnp.concatenate(split(x), axis=1), jnp.concatenate([turn, turn], axis=0))


def turn_rows(x, turn):
    return dot_nn(jnp.concatenate([turn, turn], axis=1), jnp.concatenate(split(x), axis=0))


def rows_of(value, count, dtype):
    return jnp.broadcast_to(value, (count, value.shape[1])).astype(dtype)


def places(size, width):
    place = lax.broadcasted_iota(jnp.int32, (size, width), 0)
    return place.astype(F32).astype(BF16)


def split_cell(cell, cells_i, cells_j):
    row = lax.shift_right_logical(cell, 7)
    k = lax.bitwise_and(cell, LANES - 1)
    i = jnp.zeros_like(row)
    for m in range(1, cells_i):
        i = i + (row >= m * cells_j).astype(jnp.int32)
    return i, row - i * cells_j, k


def col(x, c):
    return jnp.broadcast_to(x[:, c : c + 1], x.shape)


def gather_kernel(
    count_ref, cell_ref, field_ref, out_ref, high_ref, low_ref, place_ref, *, chunk
):
    fields, cells_j, cells_i, _ = field_ref.shape
    owners, capacity = cell_ref.shape
    rows_j = 16
    half_i = cells_i // 2
    rows = half_i * rows_j
    pad = jnp.zeros((rows_j - cells_j, LANES), F32)
    for f in range(fields):
        for i in range(cells_i):
            high, low = split(jnp.concatenate([field_ref[f, :, i, :], pad], axis=0))
            at = (f * half_i + i // 2) * rows_j
            lane = (i % 2) * LANES
            high_ref[at : at + rows_j, lane : lane + LANES] = high
            low_ref[at : at + rows_j, lane : lane + LANES] = low
    out_ref[...] = jnp.zeros(out_ref.shape, F32)
    place_ref[...] = places(2 * LANES, LANES)
    per = chunk // LANES
    slot_rows = capacity // LANES

    def owner_body(d, carry):
        count = count_ref[d]

        def chunk_body(c, carry):
            start = pl.multiple_of(c * chunk, chunk)
            cell = cell_ref[pl.ds(d, 1), pl.ds(start, chunk)]
            i, j, k = split_cell(cell, cells_i, cells_j)
            slot = start + lax.broadcasted_iota(jnp.int32, cell.shape, 1)
            row = lax.shift_right_logical(i, 1) * rows_j + j
            row = jnp.where(slot < count, row, -1)
            column = (lax.bitwise_and(i, 1) * LANES + k).astype(F32)
            column = rows_of(column, 16, BF16)
            place = place_ref[...]
            hot = []
            for r in range(2 * LANES // 16):
                here = jnp.concatenate([place[16 * r : 16 * r + 16]] * per, axis=1)
                hot.append(jnp.where(here == column, jnp.asarray(1, BF16), jnp.asarray(0, BF16)))
            hot = jnp.concatenate(hot, axis=0)
            found = dot_nn(high_ref[...], hot) + dot_nn(low_ref[...], hot)
            pick = lax.broadcasted_iota(jnp.int32, (rows, chunk), 0) == row
            for f in range(fields):
                value = jnp.where(pick, found[f * rows : (f + 1) * rows], 0.0)
                value = jnp.sum(value, axis=0, keepdims=True)
                for q in range(per):
                    out_ref[d, pl.ds(f * slot_rows + c * per + q, 1), :] = value[
                        :, q * LANES : (q + 1) * LANES
                    ]
            return carry

        return lax.fori_loop(0, lax.div(count + (chunk - 1), chunk), chunk_body, carry)

    lax.fori_loop(0, owners, owner_body, 0)


def gather(count, cell, field, chunk=512):
    fields, _, cells_i, _ = field.shape
    owners, capacity = cell.shape
    table = (fields * cells_i // 2 * 16, 2 * LANES)
    return pl.pallas_call(
        functools.partial(gather_kernel, chunk=chunk),
        out_shape=jax.ShapeDtypeStruct((owners, fields * capacity // LANES, LANES), F32),
        in_specs=[
            pl.BlockSpec(memory_space=pltpu.SMEM),
            pl.BlockSpec(memory_space=pltpu.VMEM),
            pl.BlockSpec(memory_space=pltpu.VMEM),
        ],
        out_specs=pl.BlockSpec(memory_space=pltpu.VMEM),
        scratch_shapes=[
            pltpu.VMEM(table, BF16),
            pltpu.VMEM(table, BF16),
            pltpu.VMEM((2 * LANES, LANES), BF16),
        ],
        name="gather",
    )(count, cell, field)


def lay_out(entries):
    lane = lax.broadcasted_iota(jnp.int32, (8, LANES), 1)
    tile = jnp.zeros((8, LANES), F32)
    for at, entry in enumerate(entries):
        tile = jnp.where(lane == at, entry, tile)
    return tile


def prepare_i_kernel(i_ref, i_out, *, cells_i):
    lower, upper, edge = i_ref[0], i_ref[1], i_ref[2]

    def edges(matrix, at):
        e0, e1, e2 = col(edge, at), col(edge, at + 1), col(edge, at + 2)
        table = []
        for p in range(cells_i):
            first, second = col(matrix, p * cells_i), col(matrix, p * cells_i + 1)
            table.append((first * e0 + second * e2, first * e1))
        return table

    low_edge = edges(lower, 0)
    up_edge = edges(upper, 3)
    through = []
    for p in range(cells_i):
        total = [jnp.zeros((8, LANES), F32), jnp.zeros((8, LANES), F32)]
        for q in range(p + 1):
            factor = col(upper, p * cells_i + q)
            for a in range(2):
                total[a] = total[a] + factor * low_edge[cells_i - 1 - q][a]
        through.append(total)
    last, prior = cells_i - 1, cells_i - 2
    entries = []
    for table in (through, up_edge):
        for p in range(cells_i):
            entries += [table[p][0], table[p][1]]
    entries += [-low_edge[last][0], -low_edge[last][1], -low_edge[prior][0], -low_edge[prior][1]]
    entries += [-up_edge[last][0], -up_edge[last][1], -up_edge[prior][0], -up_edge[prior][1]]
    entries += [through[last][0], through[last][1], through[prior][0], through[prior][1]]
    i_out[...] = lay_out(entries)


def prepare_i(i_tiles, cells_i):
    return pl.pallas_call(
        functools.partial(prepare_i_kernel, cells_i=cells_i),
        out_shape=jax.ShapeDtypeStruct((8, LANES), F32),
        in_specs=[pl.BlockSpec(memory_space=pltpu.VMEM)],
        out_specs=pl.BlockSpec(memory_space=pltpu.VMEM),
        name="prepare_i",
    )(i_tiles)


def prepare_k_kernel(couple_ref, k_ref, k_tile, k_map, k_rows, k_carry, f_ref):
    fields, length = k_ref.shape[1], k_ref.shape[2]
    lane = lax.broadcasted_iota(jnp.int32, (8, LANES), 1)
    row8 = lax.broadcasted_iota(jnp.int32, (8, LANES), 0)
    row_n = lax.broadcasted_iota(jnp.int32, (length, length), 0)
    lane_n = lax.broadcasted_iota(jnp.int32, (length, length), 1)
    turn = jnp.where(row_n + lane_n == length - 1, 1.0, 0.0).astype(BF16)

    def edge_rows(direction, f):
        e0 = couple_ref[0, direction, f]
        e1 = couple_ref[1, direction, f]
        e2 = couple_ref[2, direction, f]
        first = jnp.where((row8 == 0) & (lane == 0), e0, 0.0)
        first = jnp.where((row8 == 0) & (lane == 1), e2, first)
        return jnp.where((row8 == 1) & (lane == 0), e1, first)

    f_ref[...] = jnp.zeros(f_ref.shape, F32)
    k_carry[...] = jnp.zeros(k_carry.shape, F32)
    for f in range(fields):
        low, up = k_ref[0, f], k_ref[1, f]
        whole = turn_rows(product_nn(up, turn_rows(low, turn)), turn)
        k_map[f] = whole
        low_rows = product_nt(edge_rows(2, f), low)
        across = product_nt(turn_lanes(low_rows, turn), up)
        up_rows = product_nt(edge_rows(3, f), up)
        both = jnp.concatenate([across[0:2], up_rows[0:2], jnp.zeros((4, length), F32)], axis=0)
        both = turn_lanes(both, turn)
        k_rows[f] = jnp.concatenate(
            [
                low[length - 1 : length],
                low[length - 2 : length - 1],
                whole[0:2],
                jnp.zeros((4, length), F32),
            ],
            axis=0,
        )
        for a in range(4):
            k_carry[a, f : f + 1, :] = both[a : a + 1]
        for a in range(2):
            f_ref[a, f : f + 1, :] = low_rows[a : a + 1]
    end = length - 1
    k_tile[...] = lay_out(
        [
            -col(f_ref[0], end),
            -col(f_ref[1], end),
            -col(f_ref[0], end - 1),
            -col(f_ref[1], end - 1),
            -col(k_carry[2], 0),
            -col(k_carry[3], 0),
            -col(k_carry[2], 1),
            -col(k_carry[3], 1),
            col(k_carry[0], 0),
            col(k_carry[1], 0),
            col(k_carry[0], 1),
            col(k_carry[1], 1),
        ]
    )


def prepare_k(couplings, k_factors):
    fields, length = k_factors.shape[1], k_factors.shape[2]
    return pl.pallas_call(
        prepare_k_kernel,
        out_shape=(
            jax.ShapeDtypeStruct((8, LANES), F32),
            jax.ShapeDtypeStruct((fields, length, length), F32),
            jax.ShapeDtypeStruct((fields, 8, length), F32),
            jax.ShapeDtypeStruct((4, 8, length), F32),
        ),
        in_specs=[
            pl.BlockSpec(memory_space=pltpu.SMEM),
            pl.BlockSpec(memory_space=pltpu.VMEM),
        ],
        out_specs=(pl.BlockSpec(memory_space=pltpu.VMEM),) * 4,
        scratch_shapes=[pltpu.VMEM((2, 8, length), F32)],
        name="prepare_k",
    )(couplings, k_factors)


def mat2(a, b):
    return [
        a[0] * b[0] + a[1] * b[2],
        a[0] * b[1] + a[1] * b[3],
        a[2] * b[0] + a[3] * b[2],
        a[2] * b[1] + a[3] * b[3],
    ]


def downstream_map(tiles, base, mine):
    peers = len(tiles)
    total = [jnp.zeros((8, LANES), F32)] * 4
    for m in range(1, peers):
        entry = [col(tiles[m], base + c) for c in range(12)]
        step = mat2(mat2(entry[4:8], total), entry[0:4])
        total = [
            jnp.where(m > mine, new - back, old) for new, back, old in zip(step, entry[8:12], total)
        ]
    return total


def scatter_kernel(*refs, peers, chunk, base):
    mine_ref, solve_ref, got_ref, cell_ref, weight_ref, residual_ref = refs[:6]
    tile_refs = refs[6 : 6 + peers]
    start_ref = refs[6 + peers]
    send_refs = refs[7 + peers : 7 + 2 * peers]
    total_ref, place_ref, fold_ref = refs[7 + 2 * peers :]
    fields, cells_j, cells_i, _ = residual_ref.shape
    sources, capacity = cell_ref.shape
    rows_j = 16
    per = chunk // LANES
    slot_rows = capacity // LANES
    total_ref[...] = jnp.zeros(total_ref.shape, F32)
    place_ref[...] = places(LANES, LANES)

    def source_body(b, carry):
        def chunk_body(c, carry):
            start = pl.multiple_of(c * chunk, chunk)
            cell = cell_ref[pl.ds(b, 1), pl.ds(start, chunk)]
            x = weight_ref[0, pl.ds(b, 1), pl.ds(start, chunk)]
            y = weight_ref[1, pl.ds(b, 1), pl.ds(start, chunk)]
            z = weight_ref[2, pl.ds(b, 1), pl.ds(start, chunk)]
            i, j, k = split_cell(cell, cells_i, cells_j)

            def hat(size, at, t):
                place = lax.broadcasted_iota(jnp.int32, (size, chunk), 0)
                return jnp.where(place == at, 1.0 - t, jnp.where(place == at + 1, t, 0.0))

            along_i = hat(cells_i, i, x)
            along_j = hat(rows_j, j, y)
            first = rows_of(k.astype(F32), 16, BF16)
            second = rows_of((k + 1).astype(F32), 16, BF16)
            far = split(rows_of(z, 16, F32))
            near = split(rows_of(1.0 - z, 16, F32))
            zero = jnp.zeros((16, chunk), BF16)
            place = place_ref[...]
            along_k = []
            for part in range(2):
                for r in range(LANES // 16):
                    here = jnp.concatenate([place[16 * r : 16 * r + 16]] * per, axis=1)
                    weight = jnp.where(here == second, far[part], zero)
                    along_k.append(jnp.where(here == first, near[part], weight))
            along_k = jnp.concatenate(along_k, axis=0)
            blocks = []
            for f in range(fields):
                value = jnp.concatenate(
                    [
                        got_ref[b, pl.ds(f * slot_rows + c * per + q, 1), :]
                        for q in range(per)
                    ],
                    axis=1,
                )
                scaled = along_j * value
                blocks += [along_i * scaled[q : q + 1] for q in range(cells_j)]
            high, low = split(jnp.concatenate(blocks, axis=0))
            total_ref[...] += dot_nt(
                jnp.concatenate([high, low], axis=1), jnp.concatenate([along_k, along_k], axis=1)
            )
            return carry

        return lax.fori_loop(0, capacity // chunk, chunk_body, carry)

    lax.fori_loop(0, sources, source_body, 0)

    fold_ref[...] = total_ref[:, :LANES] + total_ref[:, LANES:]
    mine = mine_ref[0]
    tiles = [ref[...] for ref in tile_refs]
    onward = downstream_map(tiles, base, mine)
    turned = mat2([col(tiles[0], base + 4 + c) for c in range(4)], onward)
    pad = jnp.zeros((rows_j - cells_j, LANES), F32)
    for f in range(fields):
        data = []
        for i in range(cells_i):
            at = pl.ds(f * cells_i * cells_j + i, cells_j, stride=cells_i)
            data.append(jnp.concatenate([fold_ref[at, :] + residual_ref[f, :, i, :], pad], axis=0))

        def solve(direction, columns):
            result = []
            for p in range(cells_i):
                value = solve_ref[direction, f, p * cells_i] * columns[0]
                for q in range(1, p + 1):
                    value = value + solve_ref[direction, f, p * cells_i + q] * columns[q]
                result.append(value)
            return result

        first = solve(0, data)
        second = solve(1, first[::-1])
        e0, e1 = first[-1], first[-2]
        g0, g1 = second[-1], second[-2]
        m = [jnp.broadcast_to(entry[f : f + 1], (rows_j, LANES)) for entry in turned]
        h0 = g0 + m[0] * e0 + m[1] * e1
        h1 = g1 + m[2] * e0 + m[3] * e1
        for i in range(cells_i):
            at = (f * cells_i + i) * rows_j
            start_ref[at : at + rows_j] = second[cells_i - 1 - i]
        for shift in range(peers):
            ahead = mine + shift < peers
            at = f * rows_j
            send_refs[shift][at : at + rows_j] = jnp.where(ahead, e0, h0)
            at = (fields + f) * rows_j
            send_refs[shift][at : at + rows_j] = jnp.where(ahead, e1, h1)


def scatter(mine, solve_tiles, got, cell, weight, residual, tiles, base, chunk=1024):
    fields, cells_j, cells_i, _ = residual.shape
    peers = len(tiles)
    rows = fields * cells_i * 16
    vmem = pl.BlockSpec(memory_space=pltpu.VMEM)
    smem = pl.BlockSpec(memory_space=pltpu.SMEM)
    return pl.pallas_call(
        functools.partial(scatter_kernel, peers=peers, chunk=chunk, base=base),
        out_shape=(jax.ShapeDtypeStruct((rows, LANES), F32),)
        + (jax.ShapeDtypeStruct((2 * fields * 16, LANES), F32),) * peers,
        in_specs=[smem, smem, vmem, vmem, vmem, vmem] + [vmem] * peers,
        out_specs=(vmem,) * (1 + peers),
        scratch_shapes=[
            pltpu.VMEM((fields * cells_i * cells_j, 2 * LANES), F32),
            pltpu.VMEM((LANES, LANES), BF16),
            pltpu.VMEM((fields * cells_i * cells_j, LANES), F32),
        ],
        name="scatter",
    )(mine, solve_tiles, got, cell, weight, residual, *tiles)


def middle_kernel(*refs, peers, base, fields, cells_i):
    mine_ref, own_ref, start_ref, map_ref, rows_ref, k_tile_ref = refs[:6]
    tile_refs = refs[6 : 6 + peers]
    got_refs = refs[6 + peers : 6 + 2 * peers]
    out_ref, send_ref, field_ref, end_ref = refs[6 + 2 * peers :]
    rows_j = 16
    mine = mine_ref[0]
    tiles = [ref[...] for ref in tile_refs]
    onward = downstream_map(tiles, base, mine)
    forward = [[col(tile, base + c) for c in range(4)] for tile in tiles]
    backward = [[col(tile, base + 4 + c) for c in range(4)] for tile in tiles]
    end_ref[...] = jnp.zeros(end_ref.shape, F32)
    rows = cells_i * rows_j
    for f in range(fields):

        def wide(entry):
            return jnp.broadcast_to(entry[f : f + 1], (rows_j, LANES))

        def advance(matrix, state, add):
            m = [wide(entry) for entry in matrix]
            return [
                m[0] * state[0] + m[1] * state[1] + add[0],
                m[2] * state[0] + m[3] * state[1] + add[1],
            ]

        got = []
        for shift in range(peers):
            low = got_refs[shift][f * rows_j : (f + 1) * rows_j]
            high = got_refs[shift][(fields + f) * rows_j : (fields + f + 1) * rows_j]
            got.append((low, high))
        zero = jnp.zeros((rows_j, LANES), F32)
        before = [zero, zero]
        for shift in range(peers - 1, 0, -1):
            new = advance(forward[shift], before, got[shift])
            before = [jnp.where(shift <= mine, n, o) for n, o in zip(new, before)]
        after = [zero, zero]
        for shift in range(1, peers):
            new = advance(backward[shift], after, got[shift])
            after = [jnp.where(shift > mine, n, o) for n, o in zip(new, after)]
        onto = advance(forward[0], before, got[0])
        after = advance(onward, onto, after)
        for p in range(cells_i):
            at = (f * cells_i + cells_i - 1 - p) * rows_j
            value = start_ref[at : at + rows_j]
            value = value - own_ref[f, 2 * p] * before[0] - own_ref[f, 2 * p + 1] * before[1]
            shift = 2 * cells_i
            value = value - own_ref[f, shift + 2 * p] * after[0]
            value = value - own_ref[f, shift + 2 * p + 1] * after[1]
            field_ref[at : at + rows_j] = value
        block = field_ref[f * rows : (f + 1) * rows]
        out_ref[f * rows : (f + 1) * rows] = product_nt(block, map_ref[f])
        ends = product_nt(rows_ref[f], block)
        for a in range(4):
            end_ref[a * fields + f : a * fields + f + 1, :] = ends[a : a + 1]
    end_ref[4 * fields : 4 * fields + 8] = k_tile_ref[...]
    for d in range(send_ref.shape[0]):
        send_ref[d] = end_ref[...]


def middle(mine, own, start, k_map, k_rows, k_tile, tiles, got, base, owners, fields, cells_i):
    peers = len(tiles)
    vmem = pl.BlockSpec(memory_space=pltpu.VMEM)
    smem = pl.BlockSpec(memory_space=pltpu.SMEM)
    return pl.pallas_call(
        functools.partial(middle_kernel, peers=peers, base=base, fields=fields, cells_i=cells_i),
        out_shape=(
            jax.ShapeDtypeStruct(start.shape, F32),
            jax.ShapeDtypeStruct((owners, 4 * fields + 8, LANES), F32),
        ),
        in_specs=[smem, smem] + [vmem] * (4 + 2 * peers),
        out_specs=(vmem, vmem),
        scratch_shapes=[pltpu.VMEM(start.shape, F32), pltpu.VMEM((4 * fields + 8, LANES), F32)],
        name="middle",
    )(mine, own, start, k_map, k_rows, k_tile, *tiles, *got)


def finish_kernel(mine_ref, start_ref, got_ref, carry_ref, out_ref):
    fields, cells_j, cells_i, _ = out_ref.shape
    rows_j = 16
    rows = cells_i * rows_j
    blocks = got_ref.shape[0]
    mine = mine_ref[0]
    zero = jnp.zeros((8, LANES), F32)
    entry = [[col(got_ref[m, 4 * fields : 4 * fields + 8], c) for c in range(12)] for m in range(blocks)]
    part = [[got_ref[m, fields * a : fields * a + 8] for a in range(4)] for m in range(blocks)]
    states = []
    state = [zero, zero]
    for m in range(blocks):
        states.append(state)
        p = entry[m]
        state = [
            p[0] * state[0] + p[1] * state[1] + part[m][0],
            p[2] * state[0] + p[3] * state[1] + part[m][1],
        ]
    before = [zero, zero]
    after = [zero, zero]
    state = [zero, zero]
    for m in range(blocks - 1, -1, -1):
        here = m == mine
        before = [jnp.where(here, n, o) for n, o in zip(states[m], before)]
        after = [jnp.where(here, n, o) for n, o in zip(state, after)]
        q, b = entry[m][4:8], entry[m][8:12]
        old = states[m]
        state = [
            q[0] * state[0] + q[1] * state[1] + part[m][2] - b[0] * old[0] - b[1] * old[1],
            q[2] * state[0] + q[3] * state[1] + part[m][3] - b[2] * old[0] - b[3] * old[1],
        ]
    for f in range(fields):
        carried = jnp.concatenate(
            [x[f : f + 1] for x in (before[0], before[1], after[0], after[1])]
            + [jnp.zeros((4, LANES), F32)],
            axis=0,
        )
        response = jnp.concatenate(
            [carry_ref[a, f : f + 1, :] for a in range(4)] + [jnp.zeros((4, LANES), F32)], axis=0
        )
        change = dot3(dot_tn, carried, response, 0, 0)
        value = start_ref[f * rows : (f + 1) * rows] - change
        for i in range(cells_i):
            out_ref[f, :, i, :] = value[i * rows_j : i * rows_j + cells_j]


def finish(mine, start, got, carry, shape):
    vmem = pl.BlockSpec(memory_space=pltpu.VMEM)
    smem = pl.BlockSpec(memory_space=pltpu.SMEM)
    return pl.pallas_call(
        finish_kernel,
        out_shape=jax.ShapeDtypeStruct(shape, F32),
        in_specs=[smem, vmem, vmem, vmem],
        out_specs=vmem,
        name="finish",
    )(mine, start, got, carry)


def per_device(
    residual,
    adjoint,
    i_factors,
    k_factors,
    couplings,
    receptor_cell,
    send_count,
    donor_cell,
    donor_weight,
):
    fields, cells_i, cells_j, cells_k = adjoint.shape
    owners = receptor_cell.shape[2]
    peers = lax.axis_size("line")
    line = lax.axis_index("line").astype(jnp.int32).reshape(1)
    block = lax.axis_index("block").astype(jnp.int32).reshape(1)
    base = 4 * cells_i

    adjoint, residual = (x.transpose(0, 2, 1, 3) for x in (adjoint, residual))
    outgoing = gather(send_count.reshape(owners), receptor_cell[0, 0], adjoint)
    incoming = lax.all_to_all(outgoing, "block", split_axis=0, concat_axis=0, tiled=True)

    square = i_factors[0].reshape(2, fields, cells_i * cells_i)
    square = jnp.pad(square, ((0, 0), (0, 8 - fields), (0, LANES - cells_i * cells_i)))
    edge = couplings[0, 0, 0:2].reshape(6, fields).T
    edge = jnp.pad(edge, ((0, 8 - fields), (0, LANES - 6)))
    i_tiles = jnp.concatenate([square, edge[None]], axis=0)
    own = prepare_i(i_tiles, cells_i)

    def shifted(value, shift):
        return lax.ppermute(value, "line", [(s, (s + shift) % peers) for s in range(peers)])

    tiles = [own] + [shifted(own, m) for m in range(1, peers)]
    start, *ends = scatter(
        line, i_tiles, incoming, donor_cell[0, 0], donor_weight[0, 0], residual, tiles, base
    )
    got = [ends[0]] + [shifted(ends[m], m) for m in range(1, peers)]
    couple = couplings[0, 0].transpose(1, 0, 2)
    factors, _ = lax.optimization_barrier((k_factors[0], ends[0]))
    k_tile, k_map, k_rows, k_carry = prepare_k(couple, factors)
    start, message = middle(
        line, own, start, k_map, k_rows, k_tile, tiles, got, base, owners, fields, cells_i
    )
    message = lax.all_to_all(message, "block", split_axis=0, concat_axis=0, tiled=True)
    return finish(block, start, message, k_carry, residual.shape).transpose(0, 2, 1, 3)


def solution(mesh):
    return jax.shard_map(
        per_device,
        mesh=mesh,
        in_specs=(
            P(None, "line", None, "block"),
            P(None, "line", None, "block"),
            P("block", None, None, "line", None),
            P("line", None, None, "block", None),
            P("line", "block", None, None, None),
            P("line", "block", None, None),
            P("line", "block", None),
            P("line", "block", None, None),
            P("line", "block", None, None, None),
        ),
        out_specs=P(None, "line", None, "block"),
        check_vma=False,
    )
```

```python
import functools

import jax
import jax.numpy as jnp
from jax import lax
from jax.experimental import pallas as pl
from jax.experimental.pallas import tpu as pltpu
from jax.sharding import PartitionSpec as P

LANES = 128
HIGHEST = lax.Precision.HIGHEST
F32 = jnp.float32
BF16 = jnp.bfloat16


def split(x):
    high = x.astype(BF16)
    return high, (x - high.astype(F32)).astype(BF16)


def dot_nt(a, b, precision=None):
    return lax.dot_general(
        a, b, (((1,), (1,)), ((), ())), precision=precision, preferred_element_type=F32
    )


def dot_nn(a, b, precision=None):
    return lax.dot_general(
        a, b, (((1,), (0,)), ((), ())), precision=precision, preferred_element_type=F32
    )


def dot_tn(a, b, precision=None):
    return lax.dot_general(
        a, b, (((0,), (0,)), ((), ())), precision=precision, preferred_element_type=F32
    )


def dot3(dot, a, b, axis_a, axis_b):
    a_high, a_low = split(a)
    b_high, b_low = split(b)
    left = jnp.concatenate([a_high, a_high, a_low], axis=axis_a)
    right = jnp.concatenate([b_high, b_low, b_high], axis=axis_b)
    return dot(left, right)


def product_nt(a, b):
    return dot3(dot_nt, a, b, 1, 1)


def product_nn(a, b):
    return dot3(dot_nn, a, b, 1, 0)


def turn_lanes(x, turn):
    return dot_nn(jnp.concatenate(split(x), axis=1), jnp.concatenate([turn, turn], axis=0))


def turn_rows(x, turn):
    return dot_nn(jnp.concatenate([turn, turn], axis=1), jnp.concatenate(split(x), axis=0))


def rows_of(value, count, dtype):
    return jnp.broadcast_to(value, (count, value.shape[1])).astype(dtype)


def places(size, width):
    place = lax.broadcasted_iota(jnp.int32, (size, width), 0)
    return place.astype(F32).astype(BF16)


def split_cell(cell, cells_i, cells_j):
    row = lax.shift_right_logical(cell, 7)
    k = lax.bitwise_and(cell, LANES - 1)
    i = jnp.zeros_like(row)
    for m in range(1, cells_i):
        i = i + (row >= m * cells_j).astype(jnp.int32)
    return i, row - i * cells_j, k


def near(x):
    return pltpu.with_memory_space_constraint(x, pltpu.VMEM)


def col(x, c):
    return jnp.broadcast_to(x[:, c : c + 1], x.shape)


def gather_kernel(
    mine_ref, count_ref, cell_ref, field_ref, out_ref, own_ref, high_ref, low_ref, place_ref, *, chunk
):
    fields, cells_j, cells_i, _ = field_ref.shape
    owners, capacity = cell_ref.shape
    rows_j = 16
    half_i = cells_i // 2
    rows = half_i * rows_j
    pad = jnp.zeros((rows_j - cells_j, LANES), F32)
    for f in range(fields):
        for i in range(cells_i):
            high, low = split(jnp.concatenate([field_ref[f, :, i, :], pad], axis=0))
            at = (f * half_i + i // 2) * rows_j
            lane = (i % 2) * LANES
            high_ref[at : at + rows_j, lane : lane + LANES] = high
            low_ref[at : at + rows_j, lane : lane + LANES] = low
    out_ref[...] = jnp.zeros(out_ref.shape, F32)
    place_ref[...] = places(2 * LANES, LANES)
    per = chunk // LANES
    slot_rows = capacity // LANES

    def owner_body(d, carry):
        count = count_ref[d]

        def chunk_body(c, carry):
            start = pl.multiple_of(c * chunk, chunk)
            cell = cell_ref[pl.ds(d, 1), pl.ds(start, chunk)]
            i, j, k = split_cell(cell, cells_i, cells_j)
            slot = start + lax.broadcasted_iota(jnp.int32, cell.shape, 1)
            row = lax.shift_right_logical(i, 1) * rows_j + j
            row = jnp.where(slot < count, row, -1)
            column = (lax.bitwise_and(i, 1) * LANES + k).astype(F32)
            column = rows_of(column, 16, BF16)
            place = place_ref[...]
            hot = []
            for r in range(2 * LANES // 16):
                here = jnp.concatenate([place[16 * r : 16 * r + 16]] * per, axis=1)
                hot.append(jnp.where(here == column, jnp.asarray(1, BF16), jnp.asarray(0, BF16)))
            hot = jnp.concatenate(hot, axis=0)
            found = dot_nn(high_ref[...], hot) + dot_nn(low_ref[...], hot)
            pick = lax.broadcasted_iota(jnp.int32, (rows, chunk), 0) == row
            for f in range(fields):
                value = jnp.where(pick, found[f * rows : (f + 1) * rows], 0.0)
                value = jnp.sum(value, axis=0, keepdims=True)
                for q in range(per):
                    out_ref[d, pl.ds(f * slot_rows + c * per + q, 1), :] = value[
                        :, q * LANES : (q + 1) * LANES
                    ]
            return carry

        return lax.fori_loop(0, lax.div(count + (chunk - 1), chunk), chunk_body, carry)

    lax.fori_loop(0, owners, owner_body, 0)
    own_ref[...] = out_ref[mine_ref[0]]


def gather(mine, count, cell, field, chunk=512):
    fields, _, cells_i, _ = field.shape
    owners, capacity = cell.shape
    table = (fields * cells_i // 2 * 16, 2 * LANES)
    return pl.pallas_call(
        functools.partial(gather_kernel, chunk=chunk),
        out_shape=(
            pltpu.VMEM((owners, fields * capacity // LANES, LANES), F32),
            pltpu.VMEM((fields * capacity // LANES, LANES), F32),
        ),
        in_specs=[
            pl.BlockSpec(memory_space=pltpu.SMEM),
            pl.BlockSpec(memory_space=pltpu.SMEM),
            pl.BlockSpec(memory_space=pltpu.VMEM),
            pl.BlockSpec(memory_space=pltpu.VMEM),
        ],
        out_specs=(pl.BlockSpec(memory_space=pltpu.VMEM),) * 2,
        scratch_shapes=[
            pltpu.VMEM(table, BF16),
            pltpu.VMEM(table, BF16),
            pltpu.VMEM((2 * LANES, LANES), BF16),
        ],
        name="gather",
    )(mine, count, cell, field)


def lay_out(entries):
    lane = lax.broadcasted_iota(jnp.int32, (8, LANES), 1)
    tile = jnp.zeros((8, LANES), F32)
    for at, entry in enumerate(entries):
        tile = jnp.where(lane == at, entry, tile)
    return tile


def prepare_i_kernel(i_ref, i_out, *, cells_i):
    lower, upper, edge = i_ref[0], i_ref[1], i_ref[2]

    def edges(matrix, at):
        e0, e1, e2 = col(edge, at), col(edge, at + 1), col(edge, at + 2)
        table = []
        for p in range(cells_i):
            first, second = col(matrix, p * cells_i), col(matrix, p * cells_i + 1)
            table.append((first * e0 + second * e2, first * e1))
        return table

    low_edge = edges(lower, 0)
    up_edge = edges(upper, 3)
    through = []
    for p in range(cells_i):
        total = [jnp.zeros((8, LANES), F32), jnp.zeros((8, LANES), F32)]
        for q in range(p + 1):
            factor = col(upper, p * cells_i + q)
            for a in range(2):
                total[a] = total[a] + factor * low_edge[cells_i - 1 - q][a]
        through.append(total)
    last, prior = cells_i - 1, cells_i - 2
    entries = []
    for table in (through, up_edge):
        for p in range(cells_i):
            entries += [table[p][0], table[p][1]]
    entries += [-low_edge[last][0], -low_edge[last][1], -low_edge[prior][0], -low_edge[prior][1]]
    entries += [-up_edge[last][0], -up_edge[last][1], -up_edge[prior][0], -up_edge[prior][1]]
    entries += [through[last][0], through[last][1], through[prior][0], through[prior][1]]
    i_out[...] = lay_out(entries)


def prepare_i(i_tiles, cells_i):
    return pl.pallas_call(
        functools.partial(prepare_i_kernel, cells_i=cells_i),
        out_shape=pltpu.VMEM((8, LANES), F32),
        in_specs=[pl.BlockSpec(memory_space=pltpu.VMEM)],
        out_specs=pl.BlockSpec(memory_space=pltpu.VMEM),
        name="prepare_i",
    )(i_tiles)


def prepare_k_kernel(couple_ref, k_ref, k_tile, k_map, k_rows, k_carry, f_ref):
    fields, length = k_ref.shape[1], k_ref.shape[2]
    lane = lax.broadcasted_iota(jnp.int32, (8, LANES), 1)
    row8 = lax.broadcasted_iota(jnp.int32, (8, LANES), 0)
    row_n = lax.broadcasted_iota(jnp.int32, (length, length), 0)
    lane_n = lax.broadcasted_iota(jnp.int32, (length, length), 1)
    turn = jnp.where(row_n + lane_n == length - 1, 1.0, 0.0).astype(BF16)

    def edge_rows(direction, f):
        e0 = couple_ref[0, direction, f]
        e1 = couple_ref[1, direction, f]
        e2 = couple_ref[2, direction, f]
        first = jnp.where((row8 == 0) & (lane == 0), e0, 0.0)
        first = jnp.where((row8 == 0) & (lane == 1), e2, first)
        return jnp.where((row8 == 1) & (lane == 0), e1, first)

    f_ref[...] = jnp.zeros(f_ref.shape, F32)
    k_carry[...] = jnp.zeros(k_carry.shape, F32)
    for f in range(fields):
        low, up = k_ref[0, f], k_ref[1, f]
        whole = turn_rows(product_nn(up, turn_rows(low, turn)), turn)
        k_map[f] = whole
        low_rows = product_nt(edge_rows(2, f), low)
        across = product_nt(turn_lanes(low_rows, turn), up)
        up_rows = product_nt(edge_rows(3, f), up)
        both = jnp.concatenate([across[0:2], up_rows[0:2], jnp.zeros((4, length), F32)], axis=0)
        both = turn_lanes(both, turn)
        k_rows[f] = jnp.concatenate(
            [
                low[length - 1 : length],
                low[length - 2 : length - 1],
                whole[0:2],
                jnp.zeros((4, length), F32),
            ],
            axis=0,
        )
        for a in range(4):
            k_carry[a, f : f + 1, :] = both[a : a + 1]
        for a in range(2):
            f_ref[a, f : f + 1, :] = low_rows[a : a + 1]
    end = length - 1
    k_tile[...] = lay_out(
        [
            -col(f_ref[0], end),
            -col(f_ref[1], end),
            -col(f_ref[0], end - 1),
            -col(f_ref[1], end - 1),
            -col(k_carry[2], 0),
            -col(k_carry[3], 0),
            -col(k_carry[2], 1),
            -col(k_carry[3], 1),
            col(k_carry[0], 0),
            col(k_carry[1], 0),
            col(k_carry[0], 1),
            col(k_carry[1], 1),
        ]
    )


def prepare_k(couplings, k_factors):
    fields, length = k_factors.shape[1], k_factors.shape[2]
    return pl.pallas_call(
        prepare_k_kernel,
        out_shape=(
            pltpu.VMEM((8, LANES), F32),
            pltpu.VMEM((fields, length, length), F32),
            pltpu.VMEM((fields, 8, length), F32),
            pltpu.VMEM((4, 8, length), F32),
        ),
        in_specs=[
            pl.BlockSpec(memory_space=pltpu.SMEM),
            pl.BlockSpec(memory_space=pltpu.VMEM),
        ],
        out_specs=(pl.BlockSpec(memory_space=pltpu.VMEM),) * 4,
        scratch_shapes=[pltpu.VMEM((2, 8, length), F32)],
        name="prepare_k",
    )(couplings, k_factors)


def mat2(a, b):
    return [
        a[0] * b[0] + a[1] * b[2],
        a[0] * b[1] + a[1] * b[3],
        a[2] * b[0] + a[3] * b[2],
        a[2] * b[1] + a[3] * b[3],
    ]


def downstream_map(tiles, base, mine):
    peers = len(tiles)
    total = [jnp.zeros((8, LANES), F32)] * 4
    for m in range(1, peers):
        entry = [col(tiles[m], base + c) for c in range(12)]
        step = mat2(mat2(entry[4:8], total), entry[0:4])
        total = [
            jnp.where(m > mine, new - back, old) for new, back, old in zip(step, entry[8:12], total)
        ]
    return total


def spread_slots(total_ref, place_ref, value_of, cell_ref, weight_ref, b, c, sizes, chunk):
    fields, cells_j, cells_i = sizes
    rows_j = 16
    per = chunk // LANES
    start = pl.multiple_of(c * chunk, chunk)
    cell = cell_ref[pl.ds(b, 1), pl.ds(start, chunk)]
    x = weight_ref[0, pl.ds(b, 1), pl.ds(start, chunk)]
    y = weight_ref[1, pl.ds(b, 1), pl.ds(start, chunk)]
    z = weight_ref[2, pl.ds(b, 1), pl.ds(start, chunk)]
    i, j, k = split_cell(cell, cells_i, cells_j)

    def hat(size, at, t):
        place = lax.broadcasted_iota(jnp.int32, (size, chunk), 0)
        return jnp.where(place == at, 1.0 - t, jnp.where(place == at + 1, t, 0.0))

    along_i = hat(cells_i, i, x)
    along_j = hat(rows_j, j, y)
    first = rows_of(k.astype(F32), 16, BF16)
    second = rows_of((k + 1).astype(F32), 16, BF16)
    far = split(rows_of(z, 16, F32))
    close = split(rows_of(1.0 - z, 16, F32))
    zero = jnp.zeros((16, chunk), BF16)
    place = place_ref[...]
    along_k = []
    for part in range(2):
        for r in range(LANES // 16):
            here = jnp.concatenate([place[16 * r : 16 * r + 16]] * per, axis=1)
            weight = jnp.where(here == second, far[part], zero)
            along_k.append(jnp.where(here == first, close[part], weight))
    along_k = jnp.concatenate(along_k, axis=0)
    blocks = []
    for f in range(fields):
        value = jnp.concatenate([value_of(f, c * per + q) for q in range(per)], axis=1)
        scaled = along_j * value
        blocks += [along_i * scaled[q : q + 1] for q in range(cells_j)]
    high, low = split(jnp.concatenate(blocks, axis=0))
    total_ref[...] += dot_nt(
        jnp.concatenate([high, low], axis=1), jnp.concatenate([along_k, along_k], axis=1)
    )


def scatter_own_kernel(
    mine_ref, got_ref, cell_ref, weight_ref, total_ref, place_ref, *, sizes, chunk
):
    capacity = cell_ref.shape[1]
    slot_rows = capacity // LANES
    total_ref[...] = jnp.zeros(total_ref.shape, F32)
    place_ref[...] = places(LANES, LANES)
    mine = mine_ref[0]

    def chunk_body(c, carry):
        spread_slots(
            total_ref,
            place_ref,
            lambda f, q: got_ref[pl.ds(f * slot_rows + q, 1), :],
            cell_ref,
            weight_ref,
            mine,
            c,
            sizes,
            chunk,
        )
        return carry

    lax.fori_loop(0, capacity // chunk, chunk_body, 0)


def scatter_own(mine, got, cell, weight, sizes, chunk=2048):
    vmem = pl.BlockSpec(memory_space=pltpu.VMEM)
    smem = pl.BlockSpec(memory_space=pltpu.SMEM)
    fields, cells_j, cells_i = sizes
    return pl.pallas_call(
        functools.partial(scatter_own_kernel, sizes=sizes, chunk=chunk),
        out_shape=pltpu.VMEM((fields * cells_i * cells_j, 2 * LANES), F32),
        in_specs=[smem, vmem, vmem, vmem],
        out_specs=vmem,
        scratch_shapes=[pltpu.VMEM((LANES, LANES), BF16)],
        name="scatter_own",
    )(mine, near(got), cell, weight)


def scatter_kernel(*refs, peers, chunk, base):
    mine_ref, block_ref, solve_ref, begun_ref, got_ref, cell_ref, weight_ref, residual_ref = refs[:8]
    refs = refs[8:]
    tile_refs = refs[:peers]
    start_ref = refs[peers]
    send_refs = refs[1 + peers : 1 + 2 * peers]
    total_ref, place_ref, fold_ref = refs[1 + 2 * peers :]
    fields, cells_j, cells_i, _ = residual_ref.shape
    sources, capacity = cell_ref.shape
    rows_j = 16
    slot_rows = capacity // LANES
    total_ref[...] = begun_ref[...]
    place_ref[...] = places(LANES, LANES)
    own = block_ref[0]

    def source_body(at, carry):
        b = at + (at >= own).astype(jnp.int32)

        def chunk_body(c, carry):
            spread_slots(
                total_ref,
                place_ref,
                lambda f, q: got_ref[b, pl.ds(f * slot_rows + q, 1), :],
                cell_ref,
                weight_ref,
                b,
                c,
                (fields, cells_j, cells_i),
                chunk,
            )
            return carry

        return lax.fori_loop(0, capacity // chunk, chunk_body, carry)

    lax.fori_loop(0, sources - 1, source_body, 0)

    fold_ref[...] = total_ref[:, :LANES] + total_ref[:, LANES:]
    mine = mine_ref[0]
    tiles = [ref[...] for ref in tile_refs]
    onward = downstream_map(tiles, base, mine)
    turned = mat2([col(tiles[0], base + 4 + c) for c in range(4)], onward)
    pad = jnp.zeros((rows_j - cells_j, LANES), F32)
    for f in range(fields):
        data = []
        for i in range(cells_i):
            at = pl.ds(f * cells_i * cells_j + i, cells_j, stride=cells_i)
            data.append(jnp.concatenate([fold_ref[at, :] + residual_ref[f, :, i, :], pad], axis=0))

        def solve(direction, columns):
            result = []
            for p in range(cells_i):
                value = solve_ref[direction, f, p * cells_i] * columns[0]
                for q in range(1, p + 1):
                    value = value + solve_ref[direction, f, p * cells_i + q] * columns[q]
                result.append(value)
            return result

        first = solve(0, data)
        second = solve(1, first[::-1])
        e0, e1 = first[-1], first[-2]
        g0, g1 = second[-1], second[-2]
        m = [jnp.broadcast_to(entry[f : f + 1], (rows_j, LANES)) for entry in turned]
        h0 = g0 + m[0] * e0 + m[1] * e1
        h1 = g1 + m[2] * e0 + m[3] * e1
        for i in range(cells_i):
            at = (f * cells_i + i) * rows_j
            start_ref[at : at + rows_j] = second[cells_i - 1 - i]
        for shift in range(peers):
            ahead = mine + shift < peers
            at = f * rows_j
            send_refs[shift][at : at + rows_j] = jnp.where(ahead, e0, h0)
            at = (fields + f) * rows_j
            send_refs[shift][at : at + rows_j] = jnp.where(ahead, e1, h1)


def scatter(mine, block, solve_tiles, begun, got, cell, weight, residual, tiles, base, chunk=2048):
    fields, cells_j, cells_i, _ = residual.shape
    peers = len(tiles)
    rows = fields * cells_i * 16
    vmem = pl.BlockSpec(memory_space=pltpu.VMEM)
    smem = pl.BlockSpec(memory_space=pltpu.SMEM)
    return pl.pallas_call(
        functools.partial(scatter_kernel, peers=peers, chunk=chunk, base=base),
        out_shape=(pltpu.VMEM((rows, LANES), F32),)
        + (pltpu.VMEM((2 * fields * 16, LANES), F32),) * peers,
        in_specs=[smem, smem, smem] + [vmem] * (5 + peers),
        out_specs=(vmem,) * (1 + peers),
        scratch_shapes=[
            pltpu.VMEM((fields * cells_i * cells_j, 2 * LANES), F32),
            pltpu.VMEM((LANES, LANES), BF16),
            pltpu.VMEM((fields * cells_i * cells_j, LANES), F32),
        ],
        name="scatter",
    )(mine, block, solve_tiles, near(begun), near(got), cell, weight, residual, *map(near, tiles))


def middle_kernel(*refs, peers, base, fields, cells_i):
    mine_ref, own_ref, start_ref, rows_ref, k_tile_ref = refs[:5]
    tile_refs = refs[5 : 5 + peers]
    got_refs = refs[5 + peers : 5 + 2 * peers]
    field_ref, send_ref, end_ref = refs[5 + 2 * peers :]
    rows_j = 16
    mine = mine_ref[0]
    tiles = [ref[...] for ref in tile_refs]
    onward = downstream_map(tiles, base, mine)
    forward = [[col(tile, base + c) for c in range(4)] for tile in tiles]
    backward = [[col(tile, base + 4 + c) for c in range(4)] for tile in tiles]
    end_ref[...] = jnp.zeros(end_ref.shape, F32)
    rows = cells_i * rows_j
    for f in range(fields):

        def wide(entry):
            return jnp.broadcast_to(entry[f : f + 1], (rows_j, LANES))

        def advance(matrix, state, add):
            m = [wide(entry) for entry in matrix]
            return [
                m[0] * state[0] + m[1] * state[1] + add[0],
                m[2] * state[0] + m[3] * state[1] + add[1],
            ]

        got = []
        for shift in range(peers):
            low = got_refs[shift][f * rows_j : (f + 1) * rows_j]
            high = got_refs[shift][(fields + f) * rows_j : (fields + f + 1) * rows_j]
            got.append((low, high))
        zero = jnp.zeros((rows_j, LANES), F32)
        before = [zero, zero]
        for shift in range(peers - 1, 0, -1):
            new = advance(forward[shift], before, got[shift])
            before = [jnp.where(shift <= mine, n, o) for n, o in zip(new, before)]
        after = [zero, zero]
        for shift in range(1, peers):
            new = advance(backward[shift], after, got[shift])
            after = [jnp.where(shift > mine, n, o) for n, o in zip(new, after)]
        onto = advance(forward[0], before, got[0])
        after = advance(onward, onto, after)
        for p in range(cells_i):
            at = (f * cells_i + cells_i - 1 - p) * rows_j
            value = start_ref[at : at + rows_j]
            value = value - own_ref[f, 2 * p] * before[0] - own_ref[f, 2 * p + 1] * before[1]
            shift = 2 * cells_i
            value = value - own_ref[f, shift + 2 * p] * after[0]
            value = value - own_ref[f, shift + 2 * p + 1] * after[1]
            field_ref[at : at + rows_j] = value
        block = field_ref[f * rows : (f + 1) * rows]
        ends = product_nt(rows_ref[f], block)
        for a in range(4):
            end_ref[a * fields + f : a * fields + f + 1, :] = ends[a : a + 1]
    end_ref[4 * fields : 4 * fields + 8] = k_tile_ref[...]
    for d in range(send_ref.shape[0]):
        send_ref[d] = end_ref[...]


def middle(mine, own, start, k_rows, k_tile, tiles, got, base, owners, fields, cells_i):
    peers = len(tiles)
    vmem = pl.BlockSpec(memory_space=pltpu.VMEM)
    smem = pl.BlockSpec(memory_space=pltpu.SMEM)
    return pl.pallas_call(
        functools.partial(middle_kernel, peers=peers, base=base, fields=fields, cells_i=cells_i),
        out_shape=(
            pltpu.VMEM(start.shape, F32),
            pltpu.VMEM((owners, 4 * fields + 8, LANES), F32),
        ),
        in_specs=[smem, smem] + [vmem] * (3 + 2 * peers),
        out_specs=(vmem, vmem),
        scratch_shapes=[pltpu.VMEM((4 * fields + 8, LANES), F32)],
        name="middle",
    )(mine, own, *map(near, (start, k_rows, k_tile, *tiles, *got)))


def apply_k_kernel(field_ref, map_ref, out_ref):
    fields = map_ref.shape[0]
    rows = field_ref.shape[0] // fields
    for f in range(fields):
        at = slice(f * rows, (f + 1) * rows)
        out_ref[at] = product_nt(field_ref[at], map_ref[f])


def apply_k(field, k_map):
    vmem = pl.BlockSpec(memory_space=pltpu.VMEM)
    return pl.pallas_call(
        apply_k_kernel,
        out_shape=pltpu.VMEM(field.shape, F32),
        in_specs=[vmem, vmem],
        out_specs=vmem,
        name="apply_k",
    )(near(field), near(k_map))


def finish_kernel(mine_ref, start_ref, got_ref, carry_ref, out_ref):
    fields, cells_j, cells_i, _ = out_ref.shape
    rows_j = 16
    rows = cells_i * rows_j
    blocks = got_ref.shape[0]
    mine = mine_ref[0]
    zero = jnp.zeros((8, LANES), F32)
    entry = [[col(got_ref[m, 4 * fields : 4 * fields + 8], c) for c in range(12)] for m in range(blocks)]
    part = [[got_ref[m, fields * a : fields * a + 8] for a in range(4)] for m in range(blocks)]
    states = []
    state = [zero, zero]
    for m in range(blocks):
        states.append(state)
        p = entry[m]
        state = [
            p[0] * state[0] + p[1] * state[1] + part[m][0],
            p[2] * state[0] + p[3] * state[1] + part[m][1],
        ]
    before = [zero, zero]
    after = [zero, zero]
    state = [zero, zero]
    for m in range(blocks - 1, -1, -1):
        here = m == mine
        before = [jnp.where(here, n, o) for n, o in zip(states[m], before)]
        after = [jnp.where(here, n, o) for n, o in zip(state, after)]
        q, b = entry[m][4:8], entry[m][8:12]
        old = states[m]
        state = [
            q[0] * state[0] + q[1] * state[1] + part[m][2] - b[0] * old[0] - b[1] * old[1],
            q[2] * state[0] + q[3] * state[1] + part[m][3] - b[2] * old[0] - b[3] * old[1],
        ]
    for f in range(fields):
        carried = jnp.concatenate(
            [x[f : f + 1] for x in (before[0], before[1], after[0], after[1])]
            + [jnp.zeros((4, LANES), F32)],
            axis=0,
        )
        response = jnp.concatenate(
            [carry_ref[a, f : f + 1, :] for a in range(4)] + [jnp.zeros((4, LANES), F32)], axis=0
        )
        change = dot3(dot_tn, carried, response, 0, 0)
        value = start_ref[f * rows : (f + 1) * rows] - change
        for i in range(cells_i):
            out_ref[f, :, i, :] = value[i * rows_j : i * rows_j + cells_j]


def finish(mine, start, got, carry, shape):
    vmem = pl.BlockSpec(memory_space=pltpu.VMEM)
    smem = pl.BlockSpec(memory_space=pltpu.SMEM)
    return pl.pallas_call(
        finish_kernel,
        out_shape=jax.ShapeDtypeStruct(shape, F32),
        in_specs=[smem, vmem, vmem, vmem],
        out_specs=vmem,
        name="finish",
    )(mine, near(start), near(got), near(carry))


def per_device(
    residual,
    adjoint,
    i_factors,
    k_factors,
    couplings,
    receptor_cell,
    send_count,
    donor_cell,
    donor_weight,
):
    fields, cells_i, cells_j, cells_k = adjoint.shape
    owners = receptor_cell.shape[2]
    peers = lax.axis_size("line")
    line = lax.axis_index("line").astype(jnp.int32).reshape(1)
    block = lax.axis_index("block").astype(jnp.int32).reshape(1)
    base = 4 * cells_i

    adjoint, residual = (x.transpose(0, 2, 1, 3) for x in (adjoint, residual))
    outgoing, kept = gather(block, send_count.reshape(owners), receptor_cell[0, 0], adjoint)
    incoming = lax.all_to_all(outgoing, "block", split_axis=0, concat_axis=0, tiled=True)

    square = i_factors[0].reshape(2, fields, cells_i * cells_i)
    square = jnp.pad(square, ((0, 0), (0, 8 - fields), (0, LANES - cells_i * cells_i)))
    edge = couplings[0, 0, 0:2].reshape(6, fields).T
    edge = jnp.pad(edge, ((0, 8 - fields), (0, LANES - 6)))
    i_tiles = jnp.concatenate([square, edge[None]], axis=0)
    own = prepare_i(i_tiles, cells_i)

    def shifted(value, shift):
        return lax.ppermute(value, "line", [(s, (s + shift) % peers) for s in range(peers)])

    tiles = [own] + [shifted(own, m) for m in range(1, peers)]
    begun = scatter_own(
        block, kept, donor_cell[0, 0], donor_weight[0, 0], (fields, cells_j, cells_i)
    )
    start, *ends = scatter(
        line,
        block,
        i_tiles,
        begun,
        incoming,
        donor_cell[0, 0],
        donor_weight[0, 0],
        residual,
        tiles,
        base,
    )
    got = [ends[0]] + [shifted(ends[m], m) for m in range(1, peers)]
    couple = couplings[0, 0].transpose(1, 0, 2)
    factors, _ = lax.optimization_barrier((k_factors[0], ends[0]))
    k_tile, k_map, k_rows, k_carry = prepare_k(couple, factors)
    start, message = middle(
        line, own, start, k_rows, k_tile, tiles, got, base, owners, fields, cells_i
    )
    message = lax.all_to_all(message, "block", split_axis=0, concat_axis=0, tiled=True)
    start = apply_k(start, k_map)
    return finish(block, start, message, k_carry, residual.shape).transpose(0, 2, 1, 3)


def solution(mesh):
    return jax.shard_map(
        per_device,
        mesh=mesh,
        in_specs=(
            P(None, "line", None, "block"),
            P(None, "line", None, "block"),
            P("block", None, None, "line", None),
            P("line", None, None, "block", None),
            P("line", "block", None, None, None),
            P("line", "block", None, None),
            P("line", "block", None),
            P("line", "block", None, None),
            P("line", "block", None, None, None),
        ),
        out_specs=P(None, "line", None, "block"),
        check_vma=False,
    )
```

```python
import functools

import jax
import jax.numpy as jnp
from jax import lax
from jax.experimental import pallas as pl
from jax.experimental.pallas import tpu as pltpu
from jax.sharding import PartitionSpec as P

LANES = 128
F32 = jnp.float32
BF16 = jnp.bfloat16
PARAMS = pltpu.CompilerParams(vmem_limit_bytes=32 * 1024 * 1024)


def split(x):
    high = x.astype(BF16)
    return high, (x - high.astype(F32)).astype(BF16)


def dot_nt(a, b, precision=None):
    return lax.dot_general(
        a, b, (((1,), (1,)), ((), ())), precision=precision, preferred_element_type=F32
    )


def dot_nn(a, b, precision=None):
    return lax.dot_general(
        a, b, (((1,), (0,)), ((), ())), precision=precision, preferred_element_type=F32
    )


def dot_tn(a, b, precision=None):
    return lax.dot_general(
        a, b, (((0,), (0,)), ((), ())), precision=precision, preferred_element_type=F32
    )


def dot3(dot, a, b, axis_a, axis_b):
    a_high, a_low = split(a)
    b_high, b_low = split(b)
    left = jnp.concatenate([a_high, a_high, a_low], axis=axis_a)
    right = jnp.concatenate([b_high, b_low, b_high], axis=axis_b)
    return dot(left, right)


def product_nt(a, b):
    return dot3(dot_nt, a, b, 1, 1)


def product_nn(a, b):
    return dot3(dot_nn, a, b, 1, 0)


def turn_lanes(x, turn):
    return dot_nn(jnp.concatenate(split(x), axis=1), jnp.concatenate([turn, turn], axis=0))


def turn_rows(x, turn):
    return dot_nn(jnp.concatenate([turn, turn], axis=1), jnp.concatenate(split(x), axis=0))


def rows_of(value, count, dtype):
    return jnp.broadcast_to(value, (count, value.shape[1])).astype(dtype)


def places(size, width):
    place = lax.broadcasted_iota(jnp.int32, (size, width), 0)
    return place.astype(F32).astype(BF16)


def split_cell(cell, cells_i, cells_j):
    row = lax.shift_right_logical(cell, 7)
    k = lax.bitwise_and(cell, LANES - 1)
    i = jnp.zeros_like(row)
    for m in range(1, cells_i):
        i = i + (row >= m * cells_j).astype(jnp.int32)
    return i, row - i * cells_j, k


def near(x):
    return pltpu.with_memory_space_constraint(x, pltpu.VMEM)


def far(x):
    return pltpu.with_memory_space_constraint(x, pltpu.HBM)


def col(x, c):
    return jnp.broadcast_to(x[:, c : c + 1], x.shape)


def gather_slots(cell_ref, tables, place, d, c, count, sizes, chunk, put):
    high_ref, low_ref = tables
    fields, cells_j, cells_i = sizes
    rows_j = 16
    rows = cells_i // 2 * rows_j
    per = chunk // LANES
    start = pl.multiple_of(c * chunk, chunk)
    cell = cell_ref[pl.ds(d, 1), pl.ds(start, chunk)]
    i, j, k = split_cell(cell, cells_i, cells_j)
    slot = start + lax.broadcasted_iota(jnp.int32, cell.shape, 1)
    row = lax.shift_right_logical(i, 1) * rows_j + j
    row = jnp.where(slot < count, row, -1)
    column = (lax.bitwise_and(i, 1) * LANES + k).astype(F32)
    column = rows_of(column, 16, BF16)
    hot = []
    for r in range(2 * LANES // 16):
        here = jnp.concatenate([place[16 * r : 16 * r + 16]] * per, axis=1)
        hot.append(jnp.where(here == column, jnp.asarray(1, BF16), jnp.asarray(0, BF16)))
    hot = jnp.concatenate(hot, axis=0)
    found = dot_nn(high_ref[...], hot) + dot_nn(low_ref[...], hot)
    pick = lax.broadcasted_iota(jnp.int32, (rows, chunk), 0) == row
    for f in range(fields):
        value = jnp.where(pick, found[f * rows : (f + 1) * rows], 0.0)
        value = jnp.sum(value, axis=0, keepdims=True)
        for q in range(per):
            put(f, c * per + q, value[:, q * LANES : (q + 1) * LANES])


def gather_kernel(
    mine_ref,
    count_ref,
    cell_hbm,
    field_hbm,
    out_hbm,
    high_ref,
    low_ref,
    cell_ref,
    field_ref,
    out_ref,
    place_ref,
    cell_sem,
    field_sem,
    out_sem,
    *,
    chunk,
):
    fields, cells_j, cells_i, _ = field_ref.shape
    owners, capacity = cell_ref.shape
    rows_j = 16
    half_i = cells_i // 2
    slot_rows = capacity // LANES
    loads = [
        pltpu.make_async_copy(field_hbm.at[f], field_ref.at[f], field_sem.at[f])
        for f in range(fields)
    ]
    cell_load = pltpu.make_async_copy(cell_hbm, cell_ref, cell_sem)
    for load in loads:
        load.start()
    cell_load.start()
    out_ref[...] = jnp.zeros(out_ref.shape, F32)
    place_ref[...] = places(2 * LANES, LANES)
    pad = jnp.zeros((rows_j - cells_j, LANES), F32)
    for f in range(fields):
        loads[f].wait()
        for i in range(cells_i):
            high, low = split(jnp.concatenate([field_ref[f, :, i, :], pad], axis=0))
            at = (f * half_i + i // 2) * rows_j
            lane = (i % 2) * LANES
            high_ref[at : at + rows_j, lane : lane + LANES] = high
            low_ref[at : at + rows_j, lane : lane + LANES] = low
    cell_load.wait()
    mine = mine_ref[0]

    def send(d):
        return pltpu.make_async_copy(out_ref.at[d], out_hbm.at[d], out_sem.at[d])

    def owner_body(d, carry):
        count = jnp.where(d == mine, 0, count_ref[d])

        def put(f, row, value):
            out_ref[d, pl.ds(f * slot_rows + row, 1), :] = value

        def chunk_body(c, carry):
            gather_slots(
                cell_ref,
                (high_ref, low_ref),
                place_ref[...],
                d,
                c,
                count,
                (fields, cells_j, cells_i),
                chunk,
                put,
            )
            return carry

        lax.fori_loop(0, lax.div(count + (chunk - 1), chunk), chunk_body, 0)
        send(d).start()
        return carry

    lax.fori_loop(0, owners, owner_body, 0)

    def wait_body(d, carry):
        send(d).wait()
        return carry

    lax.fori_loop(0, owners, wait_body, 0)


def gather(mine, count, cell, field, chunk=512):
    fields, _, cells_i, _ = field.shape
    owners, capacity = cell.shape
    table = (fields * cells_i // 2 * 16, 2 * LANES)
    out = (owners, fields * capacity // LANES, LANES)
    smem = pl.BlockSpec(memory_space=pltpu.SMEM)
    vmem = pl.BlockSpec(memory_space=pltpu.VMEM)
    hbm = pl.BlockSpec(memory_space=pltpu.HBM)
    return pl.pallas_call(
        functools.partial(gather_kernel, chunk=chunk),
        out_shape=(
            jax.ShapeDtypeStruct(out, F32),
            pltpu.VMEM(table, BF16),
            pltpu.VMEM(table, BF16),
        ),
        in_specs=[smem, smem, hbm, hbm],
        out_specs=(hbm, vmem, vmem),
        scratch_shapes=[
            pltpu.VMEM(cell.shape, jnp.int32),
            pltpu.VMEM(field.shape, F32),
            pltpu.VMEM(out, F32),
            pltpu.VMEM((2 * LANES, LANES), BF16),
            pltpu.SemaphoreType.DMA(()),
            pltpu.SemaphoreType.DMA((fields,)),
            pltpu.SemaphoreType.DMA((owners,)),
        ],
        compiler_params=PARAMS,
        name="gather",
    )(mine, far(count), far(cell), far(field))


def lay_out(entries):
    lane = lax.broadcasted_iota(jnp.int32, (8, LANES), 1)
    tile = jnp.zeros((8, LANES), F32)
    for at, entry in enumerate(entries):
        tile = jnp.where(lane == at, entry, tile)
    return tile


def prepare_i_kernel(i_ref, i_out, *, cells_i):
    lower, upper, edge = i_ref[0], i_ref[1], i_ref[2]

    def edges(matrix, at):
        e0, e1, e2 = col(edge, at), col(edge, at + 1), col(edge, at + 2)
        table = []
        for p in range(cells_i):
            first, second = col(matrix, p * cells_i), col(matrix, p * cells_i + 1)
            table.append((first * e0 + second * e2, first * e1))
        return table

    low_edge = edges(lower, 0)
    up_edge = edges(upper, 3)
    through = []
    for p in range(cells_i):
        total = [jnp.zeros((8, LANES), F32), jnp.zeros((8, LANES), F32)]
        for q in range(p + 1):
            factor = col(upper, p * cells_i + q)
            for a in range(2):
                total[a] = total[a] + factor * low_edge[cells_i - 1 - q][a]
        through.append(total)
    last, prior = cells_i - 1, cells_i - 2
    entries = []
    for table in (through, up_edge):
        for p in range(cells_i):
            entries += [table[p][0], table[p][1]]
    entries += [-low_edge[last][0], -low_edge[last][1], -low_edge[prior][0], -low_edge[prior][1]]
    entries += [-up_edge[last][0], -up_edge[last][1], -up_edge[prior][0], -up_edge[prior][1]]
    entries += [through[last][0], through[last][1], through[prior][0], through[prior][1]]
    i_out[...] = lay_out(entries)


def prepare_i(i_tiles, cells_i):
    return pl.pallas_call(
        functools.partial(prepare_i_kernel, cells_i=cells_i),
        out_shape=pltpu.VMEM((8, LANES), F32),
        in_specs=[pl.BlockSpec(memory_space=pltpu.VMEM)],
        out_specs=pl.BlockSpec(memory_space=pltpu.VMEM),
        compiler_params=PARAMS,
        name="prepare_i",
    )(near(i_tiles))


def prepare_k_kernel(couple_ref, k_ref, k_tile, k_map, k_rows, k_carry, f_ref):
    fields, length = k_ref.shape[1], k_ref.shape[2]
    lane = lax.broadcasted_iota(jnp.int32, (8, LANES), 1)
    row8 = lax.broadcasted_iota(jnp.int32, (8, LANES), 0)
    row_n = lax.broadcasted_iota(jnp.int32, (length, length), 0)
    lane_n = lax.broadcasted_iota(jnp.int32, (length, length), 1)
    turn = jnp.where(row_n + lane_n == length - 1, 1.0, 0.0).astype(BF16)

    def edge_rows(direction, f):
        e0 = couple_ref[0, direction, f]
        e1 = couple_ref[1, direction, f]
        e2 = couple_ref[2, direction, f]
        first = jnp.where((row8 == 0) & (lane == 0), e0, 0.0)
        first = jnp.where((row8 == 0) & (lane == 1), e2, first)
        return jnp.where((row8 == 1) & (lane == 0), e1, first)

    f_ref[...] = jnp.zeros(f_ref.shape, F32)
    k_carry[...] = jnp.zeros(k_carry.shape, F32)
    for f in range(fields):
        low, up = k_ref[0, f], k_ref[1, f]
        whole = turn_rows(product_nn(up, turn_rows(low, turn)), turn)
        k_map[f] = whole
        low_rows = product_nt(edge_rows(2, f), low)
        across = product_nt(turn_lanes(low_rows, turn), up)
        up_rows = product_nt(edge_rows(3, f), up)
        both = jnp.concatenate([across[0:2], up_rows[0:2], jnp.zeros((4, length), F32)], axis=0)
        both = turn_lanes(both, turn)
        k_rows[f] = jnp.concatenate(
            [
                low[length - 1 : length],
                low[length - 2 : length - 1],
                whole[0:2],
                jnp.zeros((4, length), F32),
            ],
            axis=0,
        )
        for a in range(4):
            k_carry[a, f : f + 1, :] = both[a : a + 1]
        for a in range(2):
            f_ref[a, f : f + 1, :] = low_rows[a : a + 1]
    end = length - 1
    k_tile[...] = lay_out(
        [
            -col(f_ref[0], end),
            -col(f_ref[1], end),
            -col(f_ref[0], end - 1),
            -col(f_ref[1], end - 1),
            -col(k_carry[2], 0),
            -col(k_carry[3], 0),
            -col(k_carry[2], 1),
            -col(k_carry[3], 1),
            col(k_carry[0], 0),
            col(k_carry[1], 0),
            col(k_carry[0], 1),
            col(k_carry[1], 1),
        ]
    )


def prepare_k(couplings, k_factors):
    fields, length = k_factors.shape[1], k_factors.shape[2]
    return pl.pallas_call(
        prepare_k_kernel,
        out_shape=(
            pltpu.VMEM((8, LANES), F32),
            pltpu.VMEM((fields, length, length), F32),
            pltpu.VMEM((fields, 8, length), F32),
            pltpu.VMEM((4, 8, length), F32),
        ),
        in_specs=[
            pl.BlockSpec(memory_space=pltpu.SMEM),
            pl.BlockSpec(memory_space=pltpu.VMEM),
        ],
        out_specs=(pl.BlockSpec(memory_space=pltpu.VMEM),) * 4,
        scratch_shapes=[pltpu.VMEM((2, 8, length), F32)],
        compiler_params=PARAMS,
        name="prepare_k",
    )(couplings, near(k_factors))


def mat2(a, b):
    return [
        a[0] * b[0] + a[1] * b[2],
        a[0] * b[1] + a[1] * b[3],
        a[2] * b[0] + a[3] * b[2],
        a[2] * b[1] + a[3] * b[3],
    ]


def downstream_map(tiles, base, mine):
    peers = len(tiles)
    total = [jnp.zeros((8, LANES), F32)] * 4
    for m in range(1, peers):
        entry = [col(tiles[m], base + c) for c in range(12)]
        step = mat2(mat2(entry[4:8], total), entry[0:4])
        total = [
            jnp.where(m > mine, new - back, old) for new, back, old in zip(step, entry[8:12], total)
        ]
    return total


def spread_slots(total_ref, place_ref, value_of, cell_ref, weight_ref, b, c, sizes, chunk):
    fields, cells_j, cells_i = sizes
    rows_j = 16
    per = chunk // LANES
    start = pl.multiple_of(c * chunk, chunk)
    cell = cell_ref[pl.ds(b, 1), pl.ds(start, chunk)]
    x = weight_ref[0, pl.ds(b, 1), pl.ds(start, chunk)]
    y = weight_ref[1, pl.ds(b, 1), pl.ds(start, chunk)]
    z = weight_ref[2, pl.ds(b, 1), pl.ds(start, chunk)]
    i, j, k = split_cell(cell, cells_i, cells_j)

    def hat(size, at, t):
        place = lax.broadcasted_iota(jnp.int32, (size, chunk), 0)
        return jnp.where(place == at, 1.0 - t, jnp.where(place == at + 1, t, 0.0))

    along_i = hat(cells_i, i, x)
    along_j = hat(rows_j, j, y)
    first = rows_of(k.astype(F32), 16, BF16)
    second = rows_of((k + 1).astype(F32), 16, BF16)
    remote = split(rows_of(z, 16, F32))
    close = split(rows_of(1.0 - z, 16, F32))
    zero = jnp.zeros((16, chunk), BF16)
    place = place_ref[:LANES]
    along_k = []
    for part in range(2):
        for r in range(LANES // 16):
            here = jnp.concatenate([place[16 * r : 16 * r + 16]] * per, axis=1)
            weight = jnp.where(here == second, remote[part], zero)
            along_k.append(jnp.where(here == first, close[part], weight))
    along_k = jnp.concatenate(along_k, axis=0)
    blocks = []
    for f in range(fields):
        value = jnp.concatenate([value_of(f, c * per + q) for q in range(per)], axis=1)
        scaled = along_j * value
        blocks += [along_i * scaled[q : q + 1] for q in range(cells_j)]
    high, low = split(jnp.concatenate(blocks, axis=0))
    total_ref[...] += dot_nt(
        jnp.concatenate([high, low], axis=1), jnp.concatenate([along_k, along_k], axis=1)
    )


def scatter_own_kernel(
    mine_ref,
    count_ref,
    high_ref,
    low_ref,
    from_ref,
    cell_ref,
    weight_ref,
    total_ref,
    got_ref,
    place_ref,
    *,
    sizes,
    chunk,
    gather_chunk,
):
    capacity = cell_ref.shape[1]
    slot_rows = capacity // LANES
    total_ref[...] = jnp.zeros(total_ref.shape, F32)
    got_ref[...] = jnp.zeros(got_ref.shape, F32)
    place_ref[...] = places(2 * LANES, LANES)
    mine = mine_ref[0]
    count = count_ref[mine]

    def put(f, row, value):
        got_ref[pl.ds(f * slot_rows + row, 1), :] = value

    def find_body(c, carry):
        gather_slots(
            from_ref,
            (high_ref, low_ref),
            place_ref[...],
            mine,
            c,
            count,
            sizes,
            gather_chunk,
            put,
        )
        return carry

    lax.fori_loop(0, lax.div(count + (gather_chunk - 1), gather_chunk), find_body, 0)

    def chunk_body(c, carry):
        spread_slots(
            total_ref,
            place_ref,
            lambda f, q: got_ref[pl.ds(f * slot_rows + q, 1), :],
            cell_ref,
            weight_ref,
            mine,
            c,
            sizes,
            chunk,
        )
        return carry

    lax.fori_loop(0, capacity // chunk, chunk_body, 0)


def scatter_own(mine, count, tables, receptor, cell, weight, sizes, chunk=2048, gather_chunk=512):
    vmem = pl.BlockSpec(memory_space=pltpu.VMEM)
    smem = pl.BlockSpec(memory_space=pltpu.SMEM)
    fields, cells_j, cells_i = sizes
    return pl.pallas_call(
        functools.partial(
            scatter_own_kernel, sizes=sizes, chunk=chunk, gather_chunk=gather_chunk
        ),
        out_shape=pltpu.VMEM((fields * cells_i * cells_j, 2 * LANES), F32),
        in_specs=[smem, smem] + [vmem] * 5,
        out_specs=vmem,
        scratch_shapes=[
            pltpu.VMEM((fields * cell.shape[1] // LANES, LANES), F32),
            pltpu.VMEM((2 * LANES, LANES), BF16),
        ],
        compiler_params=PARAMS,
        name="scatter_own",
    )(mine, far(count), *map(near, (*tables, receptor, cell, weight)))


def scatter_kernel(*refs, peers, chunk, base):
    mine_ref, block_ref, solve_ref, begun_ref, got_ref, cell_ref, weight_ref, residual_ref = refs[:8]
    refs = refs[8:]
    tile_refs = refs[:peers]
    start_ref = refs[peers]
    send_refs = refs[1 + peers : 1 + 2 * peers]
    total_ref, place_ref, fold_ref = refs[1 + 2 * peers :]
    fields, cells_j, cells_i, _ = residual_ref.shape
    sources, capacity = cell_ref.shape
    rows_j = 16
    slot_rows = capacity // LANES
    total_ref[...] = begun_ref[...]
    place_ref[...] = places(LANES, LANES)
    own = block_ref[0]

    def source_body(at, carry):
        b = at + (at >= own).astype(jnp.int32)

        def chunk_body(c, carry):
            spread_slots(
                total_ref,
                place_ref,
                lambda f, q: got_ref[b, pl.ds(f * slot_rows + q, 1), :],
                cell_ref,
                weight_ref,
                b,
                c,
                (fields, cells_j, cells_i),
                chunk,
            )
            return carry

        return lax.fori_loop(0, capacity // chunk, chunk_body, carry)

    lax.fori_loop(0, sources - 1, source_body, 0)

    fold_ref[...] = total_ref[:, :LANES] + total_ref[:, LANES:]
    mine = mine_ref[0]
    tiles = [ref[...] for ref in tile_refs]
    onward = downstream_map(tiles, base, mine)
    turned = mat2([col(tiles[0], base + 4 + c) for c in range(4)], onward)
    pad = jnp.zeros((rows_j - cells_j, LANES), F32)
    for f in range(fields):
        data = []
        for i in range(cells_i):
            at = pl.ds(f * cells_i * cells_j + i, cells_j, stride=cells_i)
            data.append(jnp.concatenate([fold_ref[at, :] + residual_ref[f, :, i, :], pad], axis=0))

        def solve(direction, columns):
            result = []
            for p in range(cells_i):
                value = solve_ref[direction, f, p * cells_i] * columns[0]
                for q in range(1, p + 1):
                    value = value + solve_ref[direction, f, p * cells_i + q] * columns[q]
                result.append(value)
            return result

        first = solve(0, data)
        second = solve(1, first[::-1])
        e0, e1 = first[-1], first[-2]
        g0, g1 = second[-1], second[-2]
        m = [jnp.broadcast_to(entry[f : f + 1], (rows_j, LANES)) for entry in turned]
        h0 = g0 + m[0] * e0 + m[1] * e1
        h1 = g1 + m[2] * e0 + m[3] * e1
        for i in range(cells_i):
            at = (f * cells_i + i) * rows_j
            start_ref[at : at + rows_j] = second[cells_i - 1 - i]
        for shift in range(peers):
            ahead = mine + shift < peers
            at = f * rows_j
            send_refs[shift][at : at + rows_j] = jnp.where(ahead, e0, h0)
            at = (fields + f) * rows_j
            send_refs[shift][at : at + rows_j] = jnp.where(ahead, e1, h1)


def scatter(mine, block, solve_tiles, begun, got, cell, weight, residual, tiles, base, chunk=2048):
    fields, cells_j, cells_i, _ = residual.shape
    peers = len(tiles)
    rows = fields * cells_i * 16
    vmem = pl.BlockSpec(memory_space=pltpu.VMEM)
    smem = pl.BlockSpec(memory_space=pltpu.SMEM)
    return pl.pallas_call(
        functools.partial(scatter_kernel, peers=peers, chunk=chunk, base=base),
        out_shape=(pltpu.VMEM((rows, LANES), F32),)
        + (pltpu.VMEM((2 * fields * 16, LANES), F32),) * peers,
        in_specs=[smem, smem, smem] + [vmem] * (5 + peers),
        out_specs=(vmem,) * (1 + peers),
        scratch_shapes=[
            pltpu.VMEM((fields * cells_i * cells_j, 2 * LANES), F32),
            pltpu.VMEM((LANES, LANES), BF16),
            pltpu.VMEM((fields * cells_i * cells_j, LANES), F32),
        ],
        compiler_params=PARAMS,
        name="scatter",
    )(mine, block, solve_tiles, *map(near, (begun, got, cell, weight, residual, *tiles)))


def middle_kernel(*refs, peers, base, fields, cells_i):
    mine_ref, own_ref, start_ref, rows_ref, k_tile_ref = refs[:5]
    tile_refs = refs[5 : 5 + peers]
    got_refs = refs[5 + peers : 5 + 2 * peers]
    field_ref, send_ref, end_ref = refs[5 + 2 * peers :]
    rows_j = 16
    mine = mine_ref[0]
    tiles = [ref[...] for ref in tile_refs]
    onward = downstream_map(tiles, base, mine)
    forward = [[col(tile, base + c) for c in range(4)] for tile in tiles]
    backward = [[col(tile, base + 4 + c) for c in range(4)] for tile in tiles]
    end_ref[...] = jnp.zeros(end_ref.shape, F32)
    rows = cells_i * rows_j
    for f in range(fields):

        def wide(entry):
            return jnp.broadcast_to(entry[f : f + 1], (rows_j, LANES))

        def advance(matrix, state, add):
            m = [wide(entry) for entry in matrix]
            return [
                m[0] * state[0] + m[1] * state[1] + add[0],
                m[2] * state[0] + m[3] * state[1] + add[1],
            ]

        got = []
        for shift in range(peers):
            low = got_refs[shift][f * rows_j : (f + 1) * rows_j]
            high = got_refs[shift][(fields + f) * rows_j : (fields + f + 1) * rows_j]
            got.append((low, high))
        zero = jnp.zeros((rows_j, LANES), F32)
        before = [zero, zero]
        for shift in range(peers - 1, 0, -1):
            new = advance(forward[shift], before, got[shift])
            before = [jnp.where(shift <= mine, n, o) for n, o in zip(new, before)]
        after = [zero, zero]
        for shift in range(1, peers):
            new = advance(backward[shift], after, got[shift])
            after = [jnp.where(shift > mine, n, o) for n, o in zip(new, after)]
        onto = advance(forward[0], before, got[0])
        after = advance(onward, onto, after)
        for p in range(cells_i):
            at = (f * cells_i + cells_i - 1 - p) * rows_j
            value = start_ref[at : at + rows_j]
            value = value - own_ref[f, 2 * p] * before[0] - own_ref[f, 2 * p + 1] * before[1]
            shift = 2 * cells_i
            value = value - own_ref[f, shift + 2 * p] * after[0]
            value = value - own_ref[f, shift + 2 * p + 1] * after[1]
            field_ref[at : at + rows_j] = value
        block = field_ref[f * rows : (f + 1) * rows]
        ends = product_nt(rows_ref[f], block)
        for a in range(4):
            end_ref[a * fields + f : a * fields + f + 1, :] = ends[a : a + 1]
    end_ref[4 * fields : 4 * fields + 8] = k_tile_ref[...]
    for d in range(send_ref.shape[0]):
        send_ref[d] = end_ref[...]


def middle(mine, own, start, k_rows, k_tile, tiles, got, base, owners, fields, cells_i):
    peers = len(tiles)
    vmem = pl.BlockSpec(memory_space=pltpu.VMEM)
    smem = pl.BlockSpec(memory_space=pltpu.SMEM)
    return pl.pallas_call(
        functools.partial(middle_kernel, peers=peers, base=base, fields=fields, cells_i=cells_i),
        out_shape=(
            pltpu.VMEM(start.shape, F32),
            pltpu.VMEM((owners, 4 * fields + 8, LANES), F32),
        ),
        in_specs=[smem, smem] + [vmem] * (3 + 2 * peers),
        out_specs=(vmem, vmem),
        scratch_shapes=[pltpu.VMEM((4 * fields + 8, LANES), F32)],
        compiler_params=PARAMS,
        name="middle",
    )(mine, own, *map(near, (start, k_rows, k_tile, *tiles, *got)))


def apply_k_kernel(field_ref, map_ref, out_ref):
    fields = map_ref.shape[0]
    rows = field_ref.shape[0] // fields
    for f in range(fields):
        at = slice(f * rows, (f + 1) * rows)
        out_ref[at] = product_nt(field_ref[at], map_ref[f])


def apply_k(field, k_map):
    vmem = pl.BlockSpec(memory_space=pltpu.VMEM)
    return pl.pallas_call(
        apply_k_kernel,
        out_shape=pltpu.VMEM(field.shape, F32),
        in_specs=[vmem, vmem],
        out_specs=vmem,
        compiler_params=PARAMS,
        name="apply_k",
    )(near(field), near(k_map))


def finish_kernel(mine_ref, start_ref, got_ref, carry_ref, out_hbm, out_ref, out_sem):
    fields, cells_j, cells_i, _ = out_ref.shape
    rows_j = 16
    rows = cells_i * rows_j
    blocks = got_ref.shape[0]
    mine = mine_ref[0]
    zero = jnp.zeros((8, LANES), F32)
    entry = [[col(got_ref[m, 4 * fields : 4 * fields + 8], c) for c in range(12)] for m in range(blocks)]
    part = [[got_ref[m, fields * a : fields * a + 8] for a in range(4)] for m in range(blocks)]
    states = []
    state = [zero, zero]
    for m in range(blocks):
        states.append(state)
        p = entry[m]
        state = [
            p[0] * state[0] + p[1] * state[1] + part[m][0],
            p[2] * state[0] + p[3] * state[1] + part[m][1],
        ]
    before = [zero, zero]
    after = [zero, zero]
    state = [zero, zero]
    for m in range(blocks - 1, -1, -1):
        here = m == mine
        before = [jnp.where(here, n, o) for n, o in zip(states[m], before)]
        after = [jnp.where(here, n, o) for n, o in zip(state, after)]
        q, b = entry[m][4:8], entry[m][8:12]
        old = states[m]
        state = [
            q[0] * state[0] + q[1] * state[1] + part[m][2] - b[0] * old[0] - b[1] * old[1],
            q[2] * state[0] + q[3] * state[1] + part[m][3] - b[2] * old[0] - b[3] * old[1],
        ]
    for f in range(fields):
        carried = jnp.concatenate(
            [x[f : f + 1] for x in (before[0], before[1], after[0], after[1])]
            + [jnp.zeros((4, LANES), F32)],
            axis=0,
        )
        response = jnp.concatenate(
            [carry_ref[a, f : f + 1, :] for a in range(4)] + [jnp.zeros((4, LANES), F32)], axis=0
        )
        change = dot3(dot_tn, carried, response, 0, 0)
        value = start_ref[f * rows : (f + 1) * rows] - change
        for i in range(cells_i):
            out_ref[f, :, i, :] = value[i * rows_j : i * rows_j + cells_j]
        pltpu.make_async_copy(out_ref.at[f], out_hbm.at[f], out_sem.at[f]).start()
    for f in range(fields):
        pltpu.make_async_copy(out_ref.at[f], out_hbm.at[f], out_sem.at[f]).wait()


def finish(mine, start, got, carry, shape):
    vmem = pl.BlockSpec(memory_space=pltpu.VMEM)
    smem = pl.BlockSpec(memory_space=pltpu.SMEM)
    return pl.pallas_call(
        finish_kernel,
        out_shape=jax.ShapeDtypeStruct(shape, F32),
        in_specs=[smem, vmem, vmem, vmem],
        out_specs=pl.BlockSpec(memory_space=pltpu.HBM),
        scratch_shapes=[pltpu.VMEM(shape, F32), pltpu.SemaphoreType.DMA((shape[0],))],
        compiler_params=PARAMS,
        name="finish",
    )(mine, near(start), near(got), near(carry))


def per_device(
    residual,
    adjoint,
    i_factors,
    k_factors,
    couplings,
    receptor_cell,
    send_count,
    donor_cell,
    donor_weight,
):
    fields, cells_i, cells_j, cells_k = adjoint.shape
    owners = receptor_cell.shape[2]
    peers = lax.axis_size("line")
    line = lax.axis_index("line").astype(jnp.int32).reshape(1)
    block = lax.axis_index("block").astype(jnp.int32).reshape(1)
    base = 4 * cells_i

    adjoint, residual = (x.transpose(0, 2, 1, 3) for x in (adjoint, residual))
    counts = send_count.reshape(owners)
    outgoing, *tables = gather(block, counts, receptor_cell[0, 0], adjoint)
    incoming = lax.all_to_all(outgoing, "block", split_axis=0, concat_axis=0, tiled=True)

    square = i_factors[0].reshape(2, fields, cells_i * cells_i)
    square = jnp.pad(square, ((0, 0), (0, 8 - fields), (0, LANES - cells_i * cells_i)))
    edge = couplings[0, 0, 0:2].reshape(6, fields).T
    edge = jnp.pad(edge, ((0, 8 - fields), (0, LANES - 6)))
    i_tiles = jnp.concatenate([square, edge[None]], axis=0)
    own = prepare_i(i_tiles, cells_i)

    def shifted(value, shift):
        return lax.ppermute(value, "line", [(s, (s + shift) % peers) for s in range(peers)])

    tiles = [own] + [shifted(own, m) for m in range(1, peers)]
    begun = scatter_own(
        block,
        counts,
        tables,
        receptor_cell[0, 0],
        donor_cell[0, 0],
        donor_weight[0, 0],
        (fields, cells_j, cells_i),
    )
    start, *ends = scatter(
        line,
        block,
        i_tiles,
        begun,
        incoming,
        donor_cell[0, 0],
        donor_weight[0, 0],
        residual,
        tiles,
        base,
    )
    got = [ends[0]] + [shifted(ends[m], m) for m in range(1, peers)]
    couple = couplings[0, 0].transpose(1, 0, 2)
    couple, _ = lax.optimization_barrier((couple, ends[0]))
    k_tile, k_map, k_rows, k_carry = prepare_k(couple, k_factors[0])
    start, message = middle(
        line, own, start, k_rows, k_tile, tiles, got, base, owners, fields, cells_i
    )
    message = lax.all_to_all(message, "block", split_axis=0, concat_axis=0, tiled=True)
    start = apply_k(start, k_map)
    return finish(block, start, message, k_carry, residual.shape).transpose(0, 2, 1, 3)


def solution(mesh):
    return jax.shard_map(
        per_device,
        mesh=mesh,
        in_specs=(
            P(None, "line", None, "block"),
            P(None, "line", None, "block"),
            P("block", None, None, "line", None),
            P("line", None, None, "block", None),
            P("line", "block", None, None, None),
            P("line", "block", None, None),
            P("line", "block", None),
            P("line", "block", None, None),
            P("line", "block", None, None, None),
        ),
        out_specs=P(None, "line", None, "block"),
        check_vma=False,
    )
```

```python
import functools

import jax
import jax.numpy as jnp
from jax import lax
from jax.experimental import pallas as pl
from jax.experimental.pallas import tpu as pltpu
from jax.sharding import PartitionSpec as P

LANES = 128
F32 = jnp.float32
BF16 = jnp.bfloat16
PARAMS = pltpu.CompilerParams(vmem_limit_bytes=32 * 1024 * 1024)


def split(x):
    high = x.astype(BF16)
    return high, (x - high.astype(F32)).astype(BF16)


def dot_nt(a, b, precision=None):
    return lax.dot_general(
        a, b, (((1,), (1,)), ((), ())), precision=precision, preferred_element_type=F32
    )


def dot_nn(a, b, precision=None):
    return lax.dot_general(
        a, b, (((1,), (0,)), ((), ())), precision=precision, preferred_element_type=F32
    )


def dot_tn(a, b, precision=None):
    return lax.dot_general(
        a, b, (((0,), (0,)), ((), ())), precision=precision, preferred_element_type=F32
    )


def dot3(dot, a, b, axis_a, axis_b):
    a_high, a_low = split(a)
    b_high, b_low = split(b)
    left = jnp.concatenate([a_high, a_high, a_low], axis=axis_a)
    right = jnp.concatenate([b_high, b_low, b_high], axis=axis_b)
    return dot(left, right)


def product_nt(a, b):
    return dot3(dot_nt, a, b, 1, 1)


def product_nn(a, b):
    return dot3(dot_nn, a, b, 1, 0)


def turn_lanes(x, turn):
    return dot_nn(jnp.concatenate(split(x), axis=1), jnp.concatenate([turn, turn], axis=0))


def turn_rows(x, turn):
    return dot_nn(jnp.concatenate([turn, turn], axis=1), jnp.concatenate(split(x), axis=0))


def rows_of(value, count, dtype):
    return jnp.broadcast_to(value, (count, value.shape[1])).astype(dtype)


def places(size, width):
    place = lax.broadcasted_iota(jnp.int32, (size, width), 0)
    return place.astype(F32).astype(BF16)


def split_cell(cell, cells_i, cells_j):
    row = lax.shift_right_logical(cell, 7)
    k = lax.bitwise_and(cell, LANES - 1)
    i = jnp.zeros_like(row)
    for m in range(1, cells_i):
        i = i + (row >= m * cells_j).astype(jnp.int32)
    return i, row - i * cells_j, k


def near(x):
    return pltpu.with_memory_space_constraint(x, pltpu.VMEM)


def far(x):
    return pltpu.with_memory_space_constraint(x, pltpu.HBM)


def col(x, c):
    return jnp.broadcast_to(x[:, c : c + 1], x.shape)


def build_hot(hot_ref, lane, cell_ref, place, d, c, chunk, sizes):
    _, cells_j, cells_i = sizes
    start = pl.multiple_of(c * chunk, chunk)
    cell = cell_ref[pl.ds(d, 1), pl.ds(start, chunk)]
    i, _, k = split_cell(cell, cells_i, cells_j)
    column = (lax.bitwise_and(i, 1) * LANES + k).astype(F32)
    column = rows_of(column, 16, BF16)
    for r in range(2 * LANES // 16):
        here = jnp.concatenate([place[16 * r : 16 * r + 16]] * (chunk // LANES), axis=1)
        hot_ref[16 * r : 16 * r + 16, lane : lane + chunk] = jnp.where(
            here == column, jnp.asarray(1, BF16), jnp.asarray(0, BF16)
        )


def pick_rows(found_ref, lane, cell_ref, d, c, count, chunk, sizes, put):
    fields, cells_j, cells_i = sizes
    rows_j = 16
    rows = cells_i // 2 * rows_j
    per = chunk // LANES
    start = pl.multiple_of(c * chunk, chunk)
    cell = cell_ref[pl.ds(d, 1), pl.ds(start, chunk)]
    i, j, _ = split_cell(cell, cells_i, cells_j)
    slot = start + lax.broadcasted_iota(jnp.int32, cell.shape, 1)
    row = lax.shift_right_logical(i, 1) * rows_j + j
    row = jnp.where(slot < count, row, -1)
    pick = lax.broadcasted_iota(jnp.int32, (rows, chunk), 0) == row
    for f in range(fields):
        value = found_ref[f * rows : (f + 1) * rows, lane : lane + chunk]
        value = jnp.where(pick, value, 0.0)
        value = jnp.sum(value, axis=0, keepdims=True)
        for q in range(per):
            put(f, c * per + q, value[:, q * LANES : (q + 1) * LANES])


def gather_kernel(
    mine_ref,
    count_ref,
    cell_hbm,
    field_hbm,
    out_hbm,
    high_ref,
    low_ref,
    cell_ref,
    field_ref,
    out_ref,
    place_ref,
    hot_ref,
    found_ref,
    list_ref,
    cell_sem,
    field_sem,
    out_sem,
    *,
    chunk,
    group,
):
    fields, cells_j, cells_i, _ = field_ref.shape
    owners, capacity = cell_ref.shape
    sizes = (fields, cells_j, cells_i)
    rows_j = 16
    half_i = cells_i // 2
    slot_rows = capacity // LANES
    steps = capacity // chunk
    loads = [
        pltpu.make_async_copy(field_hbm.at[f], field_ref.at[f], field_sem.at[f])
        for f in range(fields)
    ]
    cell_load = pltpu.make_async_copy(cell_hbm, cell_ref, cell_sem)
    cell_load.start()
    for load in loads:
        load.start()
    mine = mine_ref[0]

    def send(d):
        return pltpu.make_async_copy(out_ref.at[d], out_hbm.at[d], out_sem.at[d])

    out_ref[...] = jnp.zeros(out_ref.shape, F32)
    send(mine).start()
    place_ref[...] = places(2 * LANES, LANES)

    def list_owner(d, total):
        live = jnp.maximum(lax.div(count_ref[d] + (chunk - 1), chunk), 1)
        live = jnp.where(d == mine, 0, live)

        def list_chunk(c, at):
            list_ref[at] = d * steps + c
            return at + 1

        return lax.fori_loop(0, live, list_chunk, total)

    total = lax.fori_loop(0, owners, list_owner, 0)
    groups = lax.div(total + (group - 1), group)

    def place_of(n):
        entry = list_ref[jnp.minimum(n, total - 1)]
        return lax.div(entry, steps), lax.rem(entry, steps)

    def build(n):
        for g in range(group):
            d, c = place_of(n * group + g)
            build_hot(hot_ref, g * chunk, cell_ref, place_ref[...], d, c, chunk, sizes)

    cell_load.wait()
    build(0)
    pad = jnp.zeros((rows_j - cells_j, LANES), F32)
    for f in range(fields):
        loads[f].wait()
        for i in range(cells_i):
            high, low = split(jnp.concatenate([field_ref[f, :, i, :], pad], axis=0))
            at = (f * half_i + i // 2) * rows_j
            lane = (i % 2) * LANES
            high_ref[at : at + rows_j, lane : lane + LANES] = high
            low_ref[at : at + rows_j, lane : lane + LANES] = low

    def pick(n):
        for g in range(group):
            d, c = place_of(n * group + g)

            def put(f, row, value, d=d):
                out_ref[d, pl.ds(f * slot_rows + row, 1), :] = value

            pick_rows(
                found_ref, g * chunk, cell_ref, d, c, count_ref[d], chunk, sizes, put
            )

    def body(n, carry):
        done = jnp.maximum(n - 1, 0)
        pick(done)
        hot = hot_ref[...]
        found_ref[...] = dot_nn(high_ref[...], hot) + dot_nn(low_ref[...], hot)
        build(n + 1)
        for g in range(group):
            here, _ = place_of(done * group + g)
            following, _ = place_of(done * group + g + 1)

            @pl.when((n > 0) & (here != following))
            def _(here=here):
                send(here).start()

        return carry

    lax.fori_loop(0, groups, body, 0)
    pick(groups - 1)
    for g in range(group):
        here, _ = place_of((groups - 1) * group + g)
        following, _ = place_of((groups - 1) * group + g + 1)

        @pl.when(here != following)
        def _(here=here):
            send(here).start()

    last, _ = place_of(total - 1)
    send(last).start()

    def wait_body(d, carry):
        send(d).wait()
        return carry

    lax.fori_loop(0, owners, wait_body, 0)


def gather(mine, count, cell, field, chunk=256, group=4):
    fields, _, cells_i, _ = field.shape
    owners, capacity = cell.shape
    table = (fields * cells_i // 2 * 16, 2 * LANES)
    out = (owners, fields * capacity // LANES, LANES)
    smem = pl.BlockSpec(memory_space=pltpu.SMEM)
    vmem = pl.BlockSpec(memory_space=pltpu.VMEM)
    hbm = pl.BlockSpec(memory_space=pltpu.HBM)
    return pl.pallas_call(
        functools.partial(gather_kernel, chunk=chunk, group=group),
        out_shape=(
            jax.ShapeDtypeStruct(out, F32),
            pltpu.VMEM(table, BF16),
            pltpu.VMEM(table, BF16),
        ),
        in_specs=[smem, smem, hbm, hbm],
        out_specs=(hbm, vmem, vmem),
        scratch_shapes=[
            pltpu.VMEM(cell.shape, jnp.int32),
            pltpu.VMEM(field.shape, F32),
            pltpu.VMEM(out, F32),
            pltpu.VMEM((2 * LANES, LANES), BF16),
            pltpu.VMEM((2 * LANES, group * chunk), BF16),
            pltpu.VMEM((table[0], group * chunk), F32),
            pltpu.SMEM((owners * capacity // chunk,), jnp.int32),
            pltpu.SemaphoreType.DMA(()),
            pltpu.SemaphoreType.DMA((fields,)),
            pltpu.SemaphoreType.DMA((owners,)),
        ],
        compiler_params=PARAMS,
        name="gather",
    )(mine, far(count), far(cell), far(field))


def lay_out(entries):
    lane = lax.broadcasted_iota(jnp.int32, (8, LANES), 1)
    tile = jnp.zeros((8, LANES), F32)
    for at, entry in enumerate(entries):
        tile = jnp.where(lane == at, entry, tile)
    return tile


def prepare_i_kernel(i_ref, i_out, *, cells_i):
    lower, upper, edge = i_ref[0], i_ref[1], i_ref[2]

    def edges(matrix, at):
        e0, e1, e2 = col(edge, at), col(edge, at + 1), col(edge, at + 2)
        table = []
        for p in range(cells_i):
            first, second = col(matrix, p * cells_i), col(matrix, p * cells_i + 1)
            table.append((first * e0 + second * e2, first * e1))
        return table

    low_edge = edges(lower, 0)
    up_edge = edges(upper, 3)
    through = []
    for p in range(cells_i):
        total = [jnp.zeros((8, LANES), F32), jnp.zeros((8, LANES), F32)]
        for q in range(p + 1):
            factor = col(upper, p * cells_i + q)
            for a in range(2):
                total[a] = total[a] + factor * low_edge[cells_i - 1 - q][a]
        through.append(total)
    last, prior = cells_i - 1, cells_i - 2
    entries = []
    for table in (through, up_edge):
        for p in range(cells_i):
            entries += [table[p][0], table[p][1]]
    entries += [-low_edge[last][0], -low_edge[last][1], -low_edge[prior][0], -low_edge[prior][1]]
    entries += [-up_edge[last][0], -up_edge[last][1], -up_edge[prior][0], -up_edge[prior][1]]
    entries += [through[last][0], through[last][1], through[prior][0], through[prior][1]]
    i_out[...] = lay_out(entries)


def prepare_i(i_tiles, cells_i):
    return pl.pallas_call(
        functools.partial(prepare_i_kernel, cells_i=cells_i),
        out_shape=pltpu.VMEM((8, LANES), F32),
        in_specs=[pl.BlockSpec(memory_space=pltpu.VMEM)],
        out_specs=pl.BlockSpec(memory_space=pltpu.VMEM),
        compiler_params=PARAMS,
        name="prepare_i",
    )(near(i_tiles))


def prepare_k_kernel(couple_ref, k_ref, k_tile, k_map, k_rows, k_carry, f_ref):
    fields, length = k_ref.shape[1], k_ref.shape[2]
    lane = lax.broadcasted_iota(jnp.int32, (8, LANES), 1)
    row8 = lax.broadcasted_iota(jnp.int32, (8, LANES), 0)
    row_n = lax.broadcasted_iota(jnp.int32, (length, length), 0)
    lane_n = lax.broadcasted_iota(jnp.int32, (length, length), 1)
    turn = jnp.where(row_n + lane_n == length - 1, 1.0, 0.0).astype(BF16)

    def edge_rows(direction, f):
        e0 = couple_ref[0, direction, f]
        e1 = couple_ref[1, direction, f]
        e2 = couple_ref[2, direction, f]
        first = jnp.where((row8 == 0) & (lane == 0), e0, 0.0)
        first = jnp.where((row8 == 0) & (lane == 1), e2, first)
        return jnp.where((row8 == 1) & (lane == 0), e1, first)

    f_ref[...] = jnp.zeros(f_ref.shape, F32)
    k_carry[...] = jnp.zeros(k_carry.shape, F32)
    for f in range(fields):
        low, up = k_ref[0, f], k_ref[1, f]
        whole = turn_rows(product_nn(up, turn_rows(low, turn)), turn)
        k_map[f] = whole
        low_rows = product_nt(edge_rows(2, f), low)
        across = product_nt(turn_lanes(low_rows, turn), up)
        up_rows = product_nt(edge_rows(3, f), up)
        both = jnp.concatenate([across[0:2], up_rows[0:2], jnp.zeros((4, length), F32)], axis=0)
        both = turn_lanes(both, turn)
        k_rows[f] = jnp.concatenate(
            [
                low[length - 1 : length],
                low[length - 2 : length - 1],
                whole[0:2],
                jnp.zeros((4, length), F32),
            ],
            axis=0,
        )
        for a in range(4):
            k_carry[a, f : f + 1, :] = both[a : a + 1]
        for a in range(2):
            f_ref[a, f : f + 1, :] = low_rows[a : a + 1]
    end = length - 1
    k_tile[...] = lay_out(
        [
            -col(f_ref[0], end),
            -col(f_ref[1], end),
            -col(f_ref[0], end - 1),
            -col(f_ref[1], end - 1),
            -col(k_carry[2], 0),
            -col(k_carry[3], 0),
            -col(k_carry[2], 1),
            -col(k_carry[3], 1),
            col(k_carry[0], 0),
            col(k_carry[1], 0),
            col(k_carry[0], 1),
            col(k_carry[1], 1),
        ]
    )


def prepare_k(couplings, k_factors):
    fields, length = k_factors.shape[1], k_factors.shape[2]
    return pl.pallas_call(
        prepare_k_kernel,
        out_shape=(
            pltpu.VMEM((8, LANES), F32),
            pltpu.VMEM((fields, length, length), F32),
            pltpu.VMEM((fields, 8, length), F32),
            pltpu.VMEM((4, 8, length), F32),
        ),
        in_specs=[
            pl.BlockSpec(memory_space=pltpu.SMEM),
            pl.BlockSpec(memory_space=pltpu.VMEM),
        ],
        out_specs=(pl.BlockSpec(memory_space=pltpu.VMEM),) * 4,
        scratch_shapes=[pltpu.VMEM((2, 8, length), F32)],
        compiler_params=PARAMS,
        name="prepare_k",
    )(couplings, near(k_factors))


def mat2(a, b):
    return [
        a[0] * b[0] + a[1] * b[2],
        a[0] * b[1] + a[1] * b[3],
        a[2] * b[0] + a[3] * b[2],
        a[2] * b[1] + a[3] * b[3],
    ]


def downstream_map(tiles, base, mine):
    peers = len(tiles)
    total = [jnp.zeros((8, LANES), F32)] * 4
    for m in range(1, peers):
        entry = [col(tiles[m], base + c) for c in range(12)]
        step = mat2(mat2(entry[4:8], total), entry[0:4])
        total = [
            jnp.where(m > mine, new - back, old) for new, back, old in zip(step, entry[8:12], total)
        ]
    return total


def spread_slots(total_ref, place_ref, value_of, cell_ref, weight_ref, b, c, sizes, chunk):
    fields, cells_j, cells_i = sizes
    rows_j = 16
    per = chunk // LANES
    start = pl.multiple_of(c * chunk, chunk)
    cell = cell_ref[pl.ds(b, 1), pl.ds(start, chunk)]
    x = weight_ref[0, pl.ds(b, 1), pl.ds(start, chunk)]
    y = weight_ref[1, pl.ds(b, 1), pl.ds(start, chunk)]
    z = weight_ref[2, pl.ds(b, 1), pl.ds(start, chunk)]
    i, j, k = split_cell(cell, cells_i, cells_j)

    def hat(size, at, t):
        place = lax.broadcasted_iota(jnp.int32, (size, chunk), 0)
        return jnp.where(place == at, 1.0 - t, jnp.where(place == at + 1, t, 0.0))

    along_i = hat(cells_i, i, x)
    along_j = hat(rows_j, j, y)
    first = rows_of(k.astype(F32), 16, BF16)
    second = rows_of((k + 1).astype(F32), 16, BF16)
    remote = split(rows_of(z, 16, F32))
    close = split(rows_of(1.0 - z, 16, F32))
    zero = jnp.zeros((16, chunk), BF16)
    place = place_ref[:LANES]
    along_k = []
    for part in range(2):
        for r in range(LANES // 16):
            here = jnp.concatenate([place[16 * r : 16 * r + 16]] * per, axis=1)
            weight = jnp.where(here == second, remote[part], zero)
            along_k.append(jnp.where(here == first, close[part], weight))
    along_k = jnp.concatenate(along_k, axis=0)
    blocks = []
    for f in range(fields):
        value = jnp.concatenate([value_of(f, c * per + q) for q in range(per)], axis=1)
        scaled = along_j * value
        blocks += [along_i * scaled[q : q + 1] for q in range(cells_j)]
    high, low = split(jnp.concatenate(blocks, axis=0))
    total_ref[...] += dot_nt(
        jnp.concatenate([high, low], axis=1), jnp.concatenate([along_k, along_k], axis=1)
    )


def scatter_own_kernel(
    mine_ref,
    count_ref,
    high_ref,
    low_ref,
    from_ref,
    cell_ref,
    weight_ref,
    total_ref,
    got_ref,
    place_ref,
    hot_ref,
    found_ref,
    *,
    sizes,
    chunk,
    gather_chunk,
):
    capacity = cell_ref.shape[1]
    slot_rows = capacity // LANES
    total_ref[...] = jnp.zeros(total_ref.shape, F32)
    got_ref[...] = jnp.zeros(got_ref.shape, F32)
    place_ref[...] = places(2 * LANES, LANES)
    mine = mine_ref[0]
    count = count_ref[mine]

    def put(f, row, value):
        got_ref[pl.ds(f * slot_rows + row, 1), :] = value

    def find_body(c, carry):
        build_hot(hot_ref, 0, from_ref, place_ref[...], mine, c, gather_chunk, sizes)
        hot = hot_ref[...]
        found_ref[...] = dot_nn(high_ref[...], hot) + dot_nn(low_ref[...], hot)
        pick_rows(found_ref, 0, from_ref, mine, c, count, gather_chunk, sizes, put)
        return carry

    lax.fori_loop(0, lax.div(count + (gather_chunk - 1), gather_chunk), find_body, 0)

    def chunk_body(c, carry):
        spread_slots(
            total_ref,
            place_ref,
            lambda f, q: got_ref[pl.ds(f * slot_rows + q, 1), :],
            cell_ref,
            weight_ref,
            mine,
            c,
            sizes,
            chunk,
        )
        return carry

    lax.fori_loop(0, capacity // chunk, chunk_body, 0)


def scatter_own(mine, count, tables, receptor, cell, weight, sizes, chunk=2048, gather_chunk=512):
    vmem = pl.BlockSpec(memory_space=pltpu.VMEM)
    smem = pl.BlockSpec(memory_space=pltpu.SMEM)
    fields, cells_j, cells_i = sizes
    return pl.pallas_call(
        functools.partial(
            scatter_own_kernel, sizes=sizes, chunk=chunk, gather_chunk=gather_chunk
        ),
        out_shape=pltpu.VMEM((fields * cells_i * cells_j, 2 * LANES), F32),
        in_specs=[smem, smem] + [vmem] * 5,
        out_specs=vmem,
        scratch_shapes=[
            pltpu.VMEM((fields * cell.shape[1] // LANES, LANES), F32),
            pltpu.VMEM((2 * LANES, LANES), BF16),
            pltpu.VMEM((2 * LANES, gather_chunk), BF16),
            pltpu.VMEM((tables[0].shape[0], gather_chunk), F32),
        ],
        compiler_params=PARAMS,
        name="scatter_own",
    )(mine, far(count), *map(near, (*tables, receptor, cell, weight)))


def scatter_kernel(*refs, peers, chunk, base):
    mine_ref, block_ref, solve_ref, begun_ref, got_ref, cell_ref, weight_ref, residual_ref = refs[:8]
    refs = refs[8:]
    tile_refs = refs[:peers]
    start_ref = refs[peers]
    send_refs = refs[1 + peers : 1 + 2 * peers]
    total_ref, place_ref, fold_ref = refs[1 + 2 * peers :]
    fields, cells_j, cells_i, _ = residual_ref.shape
    sources, capacity = cell_ref.shape
    rows_j = 16
    slot_rows = capacity // LANES
    total_ref[...] = begun_ref[...]
    place_ref[...] = places(LANES, LANES)
    own = block_ref[0]

    def source_body(at, carry):
        b = at + (at >= own).astype(jnp.int32)

        def chunk_body(c, carry):
            spread_slots(
                total_ref,
                place_ref,
                lambda f, q: got_ref[b, pl.ds(f * slot_rows + q, 1), :],
                cell_ref,
                weight_ref,
                b,
                c,
                (fields, cells_j, cells_i),
                chunk,
            )
            return carry

        return lax.fori_loop(0, capacity // chunk, chunk_body, carry)

    lax.fori_loop(0, sources - 1, source_body, 0)

    fold_ref[...] = total_ref[:, :LANES] + total_ref[:, LANES:]
    mine = mine_ref[0]
    tiles = [ref[...] for ref in tile_refs]
    onward = downstream_map(tiles, base, mine)
    turned = mat2([col(tiles[0], base + 4 + c) for c in range(4)], onward)
    pad = jnp.zeros((rows_j - cells_j, LANES), F32)
    for f in range(fields):
        data = []
        for i in range(cells_i):
            at = pl.ds(f * cells_i * cells_j + i, cells_j, stride=cells_i)
            data.append(jnp.concatenate([fold_ref[at, :] + residual_ref[f, :, i, :], pad], axis=0))

        def solve(direction, columns):
            result = []
            for p in range(cells_i):
                value = solve_ref[direction, f, p * cells_i] * columns[0]
                for q in range(1, p + 1):
                    value = value + solve_ref[direction, f, p * cells_i + q] * columns[q]
                result.append(value)
            return result

        first = solve(0, data)
        second = solve(1, first[::-1])
        e0, e1 = first[-1], first[-2]
        g0, g1 = second[-1], second[-2]
        m = [jnp.broadcast_to(entry[f : f + 1], (rows_j, LANES)) for entry in turned]
        h0 = g0 + m[0] * e0 + m[1] * e1
        h1 = g1 + m[2] * e0 + m[3] * e1
        for i in range(cells_i):
            at = (f * cells_i + i) * rows_j
            start_ref[at : at + rows_j] = second[cells_i - 1 - i]
        for shift in range(peers):
            ahead = mine + shift < peers
            at = f * rows_j
            send_refs[shift][at : at + rows_j] = jnp.where(ahead, e0, h0)
            at = (fields + f) * rows_j
            send_refs[shift][at : at + rows_j] = jnp.where(ahead, e1, h1)


def scatter(mine, block, solve_tiles, begun, got, cell, weight, residual, tiles, base, chunk=2048):
    fields, cells_j, cells_i, _ = residual.shape
    peers = len(tiles)
    rows = fields * cells_i * 16
    vmem = pl.BlockSpec(memory_space=pltpu.VMEM)
    smem = pl.BlockSpec(memory_space=pltpu.SMEM)
    return pl.pallas_call(
        functools.partial(scatter_kernel, peers=peers, chunk=chunk, base=base),
        out_shape=(pltpu.VMEM((rows, LANES), F32),)
        + (pltpu.VMEM((2 * fields * 16, LANES), F32),) * peers,
        in_specs=[smem, smem, smem] + [vmem] * (5 + peers),
        out_specs=(vmem,) * (1 + peers),
        scratch_shapes=[
            pltpu.VMEM((fields * cells_i * cells_j, 2 * LANES), F32),
            pltpu.VMEM((LANES, LANES), BF16),
            pltpu.VMEM((fields * cells_i * cells_j, LANES), F32),
        ],
        compiler_params=PARAMS,
        name="scatter",
    )(mine, block, solve_tiles, *map(near, (begun, got, cell, weight, residual, *tiles)))


def middle_kernel(*refs, peers, base, fields, cells_i):
    mine_ref, own_ref, start_ref, rows_ref, k_tile_ref = refs[:5]
    tile_refs = refs[5 : 5 + peers]
    got_refs = refs[5 + peers : 5 + 2 * peers]
    field_ref, send_ref, end_ref = refs[5 + 2 * peers :]
    rows_j = 16
    mine = mine_ref[0]
    tiles = [ref[...] for ref in tile_refs]
    onward = downstream_map(tiles, base, mine)
    forward = [[col(tile, base + c) for c in range(4)] for tile in tiles]
    backward = [[col(tile, base + 4 + c) for c in range(4)] for tile in tiles]
    end_ref[...] = jnp.zeros(end_ref.shape, F32)
    rows = cells_i * rows_j
    for f in range(fields):

        def wide(entry):
            return jnp.broadcast_to(entry[f : f + 1], (rows_j, LANES))

        def advance(matrix, state, add):
            m = [wide(entry) for entry in matrix]
            return [
                m[0] * state[0] + m[1] * state[1] + add[0],
                m[2] * state[0] + m[3] * state[1] + add[1],
            ]

        got = []
        for shift in range(peers):
            low = got_refs[shift][f * rows_j : (f + 1) * rows_j]
            high = got_refs[shift][(fields + f) * rows_j : (fields + f + 1) * rows_j]
            got.append((low, high))
        zero = jnp.zeros((rows_j, LANES), F32)
        before = [zero, zero]
        for shift in range(peers - 1, 0, -1):
            new = advance(forward[shift], before, got[shift])
            before = [jnp.where(shift <= mine, n, o) for n, o in zip(new, before)]
        after = [zero, zero]
        for shift in range(1, peers):
            new = advance(backward[shift], after, got[shift])
            after = [jnp.where(shift > mine, n, o) for n, o in zip(new, after)]
        onto = advance(forward[0], before, got[0])
        after = advance(onward, onto, after)
        for p in range(cells_i):
            at = (f * cells_i + cells_i - 1 - p) * rows_j
            value = start_ref[at : at + rows_j]
            value = value - own_ref[f, 2 * p] * before[0] - own_ref[f, 2 * p + 1] * before[1]
            shift = 2 * cells_i
            value = value - own_ref[f, shift + 2 * p] * after[0]
            value = value - own_ref[f, shift + 2 * p + 1] * after[1]
            field_ref[at : at + rows_j] = value
        block = field_ref[f * rows : (f + 1) * rows]
        ends = product_nt(rows_ref[f], block)
        for a in range(4):
            end_ref[a * fields + f : a * fields + f + 1, :] = ends[a : a + 1]
    end_ref[4 * fields : 4 * fields + 8] = k_tile_ref[...]
    for d in range(send_ref.shape[0]):
        send_ref[d] = end_ref[...]


def middle(mine, own, start, k_rows, k_tile, tiles, got, base, owners, fields, cells_i):
    peers = len(tiles)
    vmem = pl.BlockSpec(memory_space=pltpu.VMEM)
    smem = pl.BlockSpec(memory_space=pltpu.SMEM)
    return pl.pallas_call(
        functools.partial(middle_kernel, peers=peers, base=base, fields=fields, cells_i=cells_i),
        out_shape=(
            pltpu.VMEM(start.shape, F32),
            pltpu.VMEM((owners, 4 * fields + 8, LANES), F32),
        ),
        in_specs=[smem, smem] + [vmem] * (3 + 2 * peers),
        out_specs=(vmem, vmem),
        scratch_shapes=[pltpu.VMEM((4 * fields + 8, LANES), F32)],
        compiler_params=PARAMS,
        name="middle",
    )(mine, own, *map(near, (start, k_rows, k_tile, *tiles, *got)))


def apply_k_kernel(field_ref, map_ref, out_ref):
    fields = map_ref.shape[0]
    rows = field_ref.shape[0] // fields
    for f in range(fields):
        at = slice(f * rows, (f + 1) * rows)
        out_ref[at] = product_nt(field_ref[at], map_ref[f])


def apply_k(field, k_map):
    vmem = pl.BlockSpec(memory_space=pltpu.VMEM)
    return pl.pallas_call(
        apply_k_kernel,
        out_shape=pltpu.VMEM(field.shape, F32),
        in_specs=[vmem, vmem],
        out_specs=vmem,
        compiler_params=PARAMS,
        name="apply_k",
    )(near(field), near(k_map))


def finish_kernel(mine_ref, start_ref, got_ref, carry_ref, out_hbm, out_ref, out_sem):
    fields, cells_j, cells_i, _ = out_ref.shape
    rows_j = 16
    rows = cells_i * rows_j
    blocks = got_ref.shape[0]
    mine = mine_ref[0]
    zero = jnp.zeros((8, LANES), F32)
    entry = [[col(got_ref[m, 4 * fields : 4 * fields + 8], c) for c in range(12)] for m in range(blocks)]
    part = [[got_ref[m, fields * a : fields * a + 8] for a in range(4)] for m in range(blocks)]
    states = []
    state = [zero, zero]
    for m in range(blocks):
        states.append(state)
        p = entry[m]
        state = [
            p[0] * state[0] + p[1] * state[1] + part[m][0],
            p[2] * state[0] + p[3] * state[1] + part[m][1],
        ]
    before = [zero, zero]
    after = [zero, zero]
    state = [zero, zero]
    for m in range(blocks - 1, -1, -1):
        here = m == mine
        before = [jnp.where(here, n, o) for n, o in zip(states[m], before)]
        after = [jnp.where(here, n, o) for n, o in zip(state, after)]
        q, b = entry[m][4:8], entry[m][8:12]
        old = states[m]
        state = [
            q[0] * state[0] + q[1] * state[1] + part[m][2] - b[0] * old[0] - b[1] * old[1],
            q[2] * state[0] + q[3] * state[1] + part[m][3] - b[2] * old[0] - b[3] * old[1],
        ]
    for f in range(fields):
        carried = jnp.concatenate(
            [x[f : f + 1] for x in (before[0], before[1], after[0], after[1])]
            + [jnp.zeros((4, LANES), F32)],
            axis=0,
        )
        response = jnp.concatenate(
            [carry_ref[a, f : f + 1, :] for a in range(4)] + [jnp.zeros((4, LANES), F32)], axis=0
        )
        change = dot3(dot_tn, carried, response, 0, 0)
        value = start_ref[f * rows : (f + 1) * rows] - change
        for i in range(cells_i):
            out_ref[f, :, i, :] = value[i * rows_j : i * rows_j + cells_j]
        pltpu.make_async_copy(out_ref.at[f], out_hbm.at[f], out_sem.at[f]).start()
    for f in range(fields):
        pltpu.make_async_copy(out_ref.at[f], out_hbm.at[f], out_sem.at[f]).wait()


def finish(mine, start, got, carry, shape):
    vmem = pl.BlockSpec(memory_space=pltpu.VMEM)
    smem = pl.BlockSpec(memory_space=pltpu.SMEM)
    return pl.pallas_call(
        finish_kernel,
        out_shape=jax.ShapeDtypeStruct(shape, F32),
        in_specs=[smem, vmem, vmem, vmem],
        out_specs=pl.BlockSpec(memory_space=pltpu.HBM),
        scratch_shapes=[pltpu.VMEM(shape, F32), pltpu.SemaphoreType.DMA((shape[0],))],
        compiler_params=PARAMS,
        name="finish",
    )(mine, near(start), near(got), near(carry))


def per_device(
    residual,
    adjoint,
    i_factors,
    k_factors,
    couplings,
    receptor_cell,
    send_count,
    donor_cell,
    donor_weight,
):
    fields, cells_i, cells_j, cells_k = adjoint.shape
    owners = receptor_cell.shape[2]
    peers = lax.axis_size("line")
    line = lax.axis_index("line").astype(jnp.int32).reshape(1)
    block = lax.axis_index("block").astype(jnp.int32).reshape(1)
    base = 4 * cells_i

    adjoint, residual = (x.transpose(0, 2, 1, 3) for x in (adjoint, residual))
    counts = send_count.reshape(owners)
    outgoing, *tables = gather(block, counts, receptor_cell[0, 0], adjoint)
    incoming = lax.all_to_all(outgoing, "block", split_axis=0, concat_axis=0, tiled=True)

    square = i_factors[0].reshape(2, fields, cells_i * cells_i)
    square = jnp.pad(square, ((0, 0), (0, 8 - fields), (0, LANES - cells_i * cells_i)))
    edge = couplings[0, 0, 0:2].reshape(6, fields).T
    edge = jnp.pad(edge, ((0, 8 - fields), (0, LANES - 6)))
    i_tiles = jnp.concatenate([square, edge[None]], axis=0)
    own = prepare_i(i_tiles, cells_i)

    def shifted(value, shift):
        return lax.ppermute(value, "line", [(s, (s + shift) % peers) for s in range(peers)])

    tiles = [own] + [shifted(own, m) for m in range(1, peers)]
    begun = scatter_own(
        block,
        counts,
        tables,
        receptor_cell[0, 0],
        donor_cell[0, 0],
        donor_weight[0, 0],
        (fields, cells_j, cells_i),
    )
    start, *ends = scatter(
        line,
        block,
        i_tiles,
        begun,
        incoming,
        donor_cell[0, 0],
        donor_weight[0, 0],
        residual,
        tiles,
        base,
    )
    got = [ends[0]] + [shifted(ends[m], m) for m in range(1, peers)]
    couple = couplings[0, 0].transpose(1, 0, 2)
    couple, _ = lax.optimization_barrier((couple, ends[0]))
    k_tile, k_map, k_rows, k_carry = prepare_k(couple, k_factors[0])
    start, message = middle(
        line, own, start, k_rows, k_tile, tiles, got, base, owners, fields, cells_i
    )
    message = lax.all_to_all(message, "block", split_axis=0, concat_axis=0, tiled=True)
    start = apply_k(start, k_map)
    return finish(block, start, message, k_carry, residual.shape).transpose(0, 2, 1, 3)


def solution(mesh):
    return jax.shard_map(
        per_device,
        mesh=mesh,
        in_specs=(
            P(None, "line", None, "block"),
            P(None, "line", None, "block"),
            P("block", None, None, "line", None),
            P("line", None, None, "block", None),
            P("line", "block", None, None, None),
            P("line", "block", None, None),
            P("line", "block", None),
            P("line", "block", None, None),
            P("line", "block", None, None, None),
        ),
        out_specs=P(None, "line", None, "block"),
        check_vma=False,
    )
```

```python
import functools

import jax
import jax.numpy as jnp
from jax import lax
from jax.experimental import pallas as pl
from jax.experimental.pallas import tpu as pltpu
from jax.sharding import PartitionSpec as P

LANES = 128
F32 = jnp.float32
BF16 = jnp.bfloat16
PARAMS = pltpu.CompilerParams(vmem_limit_bytes=32 * 1024 * 1024)


def split(x):
    high = x.astype(BF16)
    return high, (x - high.astype(F32)).astype(BF16)


def dot_nt(a, b, precision=None):
    return lax.dot_general(
        a, b, (((1,), (1,)), ((), ())), precision=precision, preferred_element_type=F32
    )


def dot_nn(a, b, precision=None):
    return lax.dot_general(
        a, b, (((1,), (0,)), ((), ())), precision=precision, preferred_element_type=F32
    )


def dot_tn(a, b, precision=None):
    return lax.dot_general(
        a, b, (((0,), (0,)), ((), ())), precision=precision, preferred_element_type=F32
    )


def dot3(dot, a, b, axis_a, axis_b):
    a_high, a_low = split(a)
    b_high, b_low = split(b)
    left = jnp.concatenate([a_high, a_high, a_low], axis=axis_a)
    right = jnp.concatenate([b_high, b_low, b_high], axis=axis_b)
    return dot(left, right)


def product_nt(a, b):
    return dot3(dot_nt, a, b, 1, 1)


def product_nn(a, b):
    return dot3(dot_nn, a, b, 1, 0)


def turn_lanes(x, turn):
    return dot_nn(jnp.concatenate(split(x), axis=1), jnp.concatenate([turn, turn], axis=0))


def turn_rows(x, turn):
    return dot_nn(jnp.concatenate([turn, turn], axis=1), jnp.concatenate(split(x), axis=0))


def rows_of(value, count, dtype):
    return jnp.broadcast_to(value, (count, value.shape[1])).astype(dtype)


def places(size, width):
    place = lax.broadcasted_iota(jnp.int32, (size, width), 0)
    return place.astype(F32).astype(BF16)


def split_cell(cell, cells_i, cells_j):
    row = lax.shift_right_logical(cell, 7)
    k = lax.bitwise_and(cell, LANES - 1)
    i = jnp.zeros_like(row)
    for m in range(1, cells_i):
        i = i + (row >= m * cells_j).astype(jnp.int32)
    return i, row - i * cells_j, k


def near(x):
    return pltpu.with_memory_space_constraint(x, pltpu.VMEM)


def far(x):
    return pltpu.with_memory_space_constraint(x, pltpu.HBM)


def col(x, c):
    return jnp.broadcast_to(x[:, c : c + 1], x.shape)


def build_hot(hot_ref, lane, cell_ref, place, d, c, chunk, sizes):
    _, cells_j, cells_i = sizes
    start = pl.multiple_of(c * chunk, chunk)
    cell = cell_ref[pl.ds(d, 1), pl.ds(start, chunk)]
    i, _, k = split_cell(cell, cells_i, cells_j)
    column = (lax.bitwise_and(i, 1) * LANES + k).astype(F32)
    column = rows_of(column, 16, BF16)
    for r in range(2 * LANES // 16):
        here = jnp.concatenate([place[16 * r : 16 * r + 16]] * (chunk // LANES), axis=1)
        hot_ref[16 * r : 16 * r + 16, lane : lane + chunk] = jnp.where(
            here == column, jnp.asarray(1, BF16), jnp.asarray(0, BF16)
        )


def pick_rows(found_ref, lane, cell_ref, d, c, count, chunk, sizes, put):
    fields, cells_j, cells_i = sizes
    rows_j = 16
    rows = cells_i // 2 * rows_j
    per = chunk // LANES
    start = pl.multiple_of(c * chunk, chunk)
    cell = cell_ref[pl.ds(d, 1), pl.ds(start, chunk)]
    i, j, _ = split_cell(cell, cells_i, cells_j)
    slot = start + lax.broadcasted_iota(jnp.int32, cell.shape, 1)
    row = lax.shift_right_logical(i, 1) * rows_j + j
    row = jnp.where(slot < count, row, -1)
    pick = lax.broadcasted_iota(jnp.int32, (rows, chunk), 0) == row
    for f in range(fields):
        value = found_ref[f * rows : (f + 1) * rows, lane : lane + chunk]
        value = jnp.where(pick, value, 0.0)
        value = jnp.sum(value, axis=0, keepdims=True)
        for q in range(per):
            put(f, c * per + q, value[:, q * LANES : (q + 1) * LANES])


def gather_kernel(
    mine_ref,
    count_ref,
    cell_hbm,
    field_hbm,
    out_hbm,
    high_ref,
    low_ref,
    cell_ref,
    field_ref,
    out_ref,
    place_ref,
    hot_ref,
    found_ref,
    list_ref,
    cell_sem,
    field_sem,
    out_sem,
    *,
    chunk,
    group,
):
    fields, cells_j, cells_i, _ = field_ref.shape
    owners, capacity = cell_ref.shape
    sizes = (fields, cells_j, cells_i)
    rows_j = 16
    half_i = cells_i // 2
    slot_rows = capacity // LANES
    steps = capacity // chunk
    loads = [
        pltpu.make_async_copy(field_hbm.at[f], field_ref.at[f], field_sem.at[f])
        for f in range(fields)
    ]
    cell_load = pltpu.make_async_copy(cell_hbm, cell_ref, cell_sem)
    cell_load.start()
    for load in loads:
        load.start()
    mine = mine_ref[0]

    def send(d):
        return pltpu.make_async_copy(out_ref.at[d], out_hbm.at[d], out_sem.at[d])

    out_ref[...] = jnp.zeros(out_ref.shape, F32)
    send(mine).start()
    place_ref[...] = places(2 * LANES, LANES)

    def list_owner(d, total):
        live = jnp.maximum(lax.div(count_ref[d] + (chunk - 1), chunk), 1)
        live = jnp.where(d == mine, 0, live)

        def list_chunk(c, at):
            list_ref[at] = d * steps + c
            return at + 1

        return lax.fori_loop(0, live, list_chunk, total)

    total = lax.fori_loop(0, owners, list_owner, 0)
    groups = lax.div(total + (group - 1), group)

    def place_of(n):
        entry = list_ref[jnp.minimum(n, total - 1)]
        return lax.div(entry, steps), lax.rem(entry, steps)

    def build(n):
        for g in range(group):
            d, c = place_of(n * group + g)
            build_hot(hot_ref, g * chunk, cell_ref, place_ref[...], d, c, chunk, sizes)

    cell_load.wait()
    build(0)
    pad = jnp.zeros((rows_j - cells_j, LANES), F32)
    for f in range(fields):
        loads[f].wait()
        for i in range(cells_i):
            high, low = split(jnp.concatenate([field_ref[f, :, i, :], pad], axis=0))
            at = (f * half_i + i // 2) * rows_j
            lane = (i % 2) * LANES
            high_ref[at : at + rows_j, lane : lane + LANES] = high
            low_ref[at : at + rows_j, lane : lane + LANES] = low

    def pick(n):
        for g in range(group):
            d, c = place_of(n * group + g)

            def put(f, row, value, d=d):
                out_ref[d, pl.ds(f * slot_rows + row, 1), :] = value

            pick_rows(
                found_ref, g * chunk, cell_ref, d, c, count_ref[d], chunk, sizes, put
            )

    def body(n, carry):
        done = jnp.maximum(n - 1, 0)
        pick(done)
        hot = hot_ref[...]
        found_ref[...] = dot_nn(high_ref[...], hot) + dot_nn(low_ref[...], hot)
        build(n + 1)
        for g in range(group):
            here, _ = place_of(done * group + g)
            following, _ = place_of(done * group + g + 1)

            @pl.when((n > 0) & (here != following))
            def _(here=here):
                send(here).start()

        return carry

    lax.fori_loop(0, groups, body, 0)
    pick(groups - 1)
    for g in range(group):
        here, _ = place_of((groups - 1) * group + g)
        following, _ = place_of((groups - 1) * group + g + 1)

        @pl.when(here != following)
        def _(here=here):
            send(here).start()

    last, _ = place_of(total - 1)
    send(last).start()

    def wait_body(d, carry):
        send(d).wait()
        return carry

    lax.fori_loop(0, owners, wait_body, 0)


def gather(mine, count, cell, field, chunk=256, group=4):
    fields, _, cells_i, _ = field.shape
    owners, capacity = cell.shape
    table = (fields * cells_i // 2 * 16, 2 * LANES)
    out = (owners, fields * capacity // LANES, LANES)
    smem = pl.BlockSpec(memory_space=pltpu.SMEM)
    vmem = pl.BlockSpec(memory_space=pltpu.VMEM)
    hbm = pl.BlockSpec(memory_space=pltpu.HBM)
    return pl.pallas_call(
        functools.partial(gather_kernel, chunk=chunk, group=group),
        out_shape=(
            jax.ShapeDtypeStruct(out, F32),
            pltpu.VMEM(table, BF16),
            pltpu.VMEM(table, BF16),
        ),
        in_specs=[smem, smem, hbm, hbm],
        out_specs=(hbm, vmem, vmem),
        scratch_shapes=[
            pltpu.VMEM(cell.shape, jnp.int32),
            pltpu.VMEM(field.shape, F32),
            pltpu.VMEM(out, F32),
            pltpu.VMEM((2 * LANES, LANES), BF16),
            pltpu.VMEM((2 * LANES, group * chunk), BF16),
            pltpu.VMEM((table[0], group * chunk), F32),
            pltpu.SMEM((owners * capacity // chunk,), jnp.int32),
            pltpu.SemaphoreType.DMA(()),
            pltpu.SemaphoreType.DMA((fields,)),
            pltpu.SemaphoreType.DMA((owners,)),
        ],
        compiler_params=PARAMS,
        name="gather",
    )(mine, far(count), far(cell), far(field))


def lay_out(entries):
    lane = lax.broadcasted_iota(jnp.int32, (8, LANES), 1)
    tile = jnp.zeros((8, LANES), F32)
    for at, entry in enumerate(entries):
        tile = jnp.where(lane == at, entry, tile)
    return tile


def prepare_i_kernel(i_ref, i_out, *, cells_i):
    lower, upper, edge = i_ref[0], i_ref[1], i_ref[2]

    def edges(matrix, at):
        e0, e1, e2 = col(edge, at), col(edge, at + 1), col(edge, at + 2)
        table = []
        for p in range(cells_i):
            first, second = col(matrix, p * cells_i), col(matrix, p * cells_i + 1)
            table.append((first * e0 + second * e2, first * e1))
        return table

    low_edge = edges(lower, 0)
    up_edge = edges(upper, 3)
    through = []
    for p in range(cells_i):
        total = [jnp.zeros((8, LANES), F32), jnp.zeros((8, LANES), F32)]
        for q in range(p + 1):
            factor = col(upper, p * cells_i + q)
            for a in range(2):
                total[a] = total[a] + factor * low_edge[cells_i - 1 - q][a]
        through.append(total)
    last, prior = cells_i - 1, cells_i - 2
    entries = []
    for table in (through, up_edge):
        for p in range(cells_i):
            entries += [table[p][0], table[p][1]]
    entries += [-low_edge[last][0], -low_edge[last][1], -low_edge[prior][0], -low_edge[prior][1]]
    entries += [-up_edge[last][0], -up_edge[last][1], -up_edge[prior][0], -up_edge[prior][1]]
    entries += [through[last][0], through[last][1], through[prior][0], through[prior][1]]
    i_out[...] = lay_out(entries)


def prepare_i(i_tiles, cells_i):
    return pl.pallas_call(
        functools.partial(prepare_i_kernel, cells_i=cells_i),
        out_shape=pltpu.VMEM((8, LANES), F32),
        in_specs=[pl.BlockSpec(memory_space=pltpu.VMEM)],
        out_specs=pl.BlockSpec(memory_space=pltpu.VMEM),
        compiler_params=PARAMS,
        name="prepare_i",
    )(near(i_tiles))


def prepare_k_kernel(couple_ref, k_ref, k_tile, k_map, k_rows, k_carry):
    fields, length = k_ref.shape[1], k_ref.shape[2]
    row8 = lax.broadcasted_iota(jnp.int32, (8, LANES), 0)
    row_n = lax.broadcasted_iota(jnp.int32, (length, length), 0)
    lane_n = lax.broadcasted_iota(jnp.int32, (length, length), 1)
    turn = jnp.where(row_n + lane_n == length - 1, 1.0, 0.0).astype(BF16)
    columns = jnp.zeros((length, length), F32)
    for f in range(fields):
        low, up = k_ref[0, f], k_ref[1, f]
        whole = product_nn(up, turn_rows(low, turn))
        k_map[f] = whole
        k_rows[f] = jnp.concatenate(
            [x[length - q : length - q + 1] for x in (low, whole) for q in (1, 2)]
            + [jnp.zeros((4, length), F32)],
            axis=0,
        )
        for m, matrix in enumerate((low, up, whole)):
            for q in range(2):
                value = jnp.broadcast_to(matrix[:, q : q + 1], (length, length))
                columns = jnp.where(lane_n == 16 * m + 8 * q + f, value, columns)
    columns = columns.T
    low0, low1, up0, up1, all0, all1 = (columns[8 * q : 8 * q + 8] for q in range(6))

    def edges(direction):
        table = []
        for c in range(3):
            value = jnp.zeros((8, LANES), F32)
            for f in range(fields):
                value = jnp.where(row8 == f, couple_ref[c, direction, f], value)
            table.append(value)
        return table

    e0, e1, e2 = edges(2)
    d0, d1, d2 = edges(3)
    first = (low0 * e0 + low1 * e2, low0 * e1)
    through = (all0 * e0 + all1 * e2, all0 * e1)
    second = (up0 * d0 + up1 * d2, up0 * d1)
    turned = turn_lanes(jnp.concatenate(through + second, axis=0), turn)
    for a in range(4):
        k_carry[a] = turned[8 * a : 8 * a + 8]
    ends = [(pair, p) for p in (length - 1, length - 2) for pair in (0, 1)]
    k_tile[...] = lay_out(
        [-col(first[pair], p) for pair, p in ends]
        + [-col(second[pair], p) for pair, p in ends]
        + [col(through[pair], p) for pair, p in ends]
    )


def prepare_k(couplings, k_factors):
    fields, length = k_factors.shape[1], k_factors.shape[2]
    return pl.pallas_call(
        prepare_k_kernel,
        out_shape=(
            pltpu.VMEM((8, LANES), F32),
            pltpu.VMEM((fields, length, length), F32),
            pltpu.VMEM((fields, 8, length), F32),
            pltpu.VMEM((4, 8, length), F32),
        ),
        in_specs=[
            pl.BlockSpec(memory_space=pltpu.SMEM),
            pl.BlockSpec(memory_space=pltpu.VMEM),
        ],
        out_specs=(pl.BlockSpec(memory_space=pltpu.VMEM),) * 4,
        compiler_params=PARAMS,
        name="prepare_k",
    )(couplings, near(k_factors))


def mat2(a, b):
    return [
        a[0] * b[0] + a[1] * b[2],
        a[0] * b[1] + a[1] * b[3],
        a[2] * b[0] + a[3] * b[2],
        a[2] * b[1] + a[3] * b[3],
    ]


def downstream_map(tiles, base, mine):
    peers = len(tiles)
    total = [jnp.zeros((8, LANES), F32)] * 4
    for m in range(1, peers):
        entry = [col(tiles[m], base + c) for c in range(12)]
        step = mat2(mat2(entry[4:8], total), entry[0:4])
        total = [
            jnp.where(m > mine, new - back, old) for new, back, old in zip(step, entry[8:12], total)
        ]
    return total


def spread_slots(total_ref, place_ref, value_of, cell_ref, weight_ref, b, c, sizes, chunk):
    fields, cells_j, cells_i = sizes
    rows_j = 16
    per = chunk // LANES
    start = pl.multiple_of(c * chunk, chunk)
    cell = cell_ref[pl.ds(b, 1), pl.ds(start, chunk)]
    x = weight_ref[0, pl.ds(b, 1), pl.ds(start, chunk)]
    y = weight_ref[1, pl.ds(b, 1), pl.ds(start, chunk)]
    z = weight_ref[2, pl.ds(b, 1), pl.ds(start, chunk)]
    i, j, k = split_cell(cell, cells_i, cells_j)

    def hat(size, at, t):
        place = lax.broadcasted_iota(jnp.int32, (size, chunk), 0)
        return jnp.where(place == at, 1.0 - t, jnp.where(place == at + 1, t, 0.0))

    along_i = hat(cells_i, i, x)
    along_j = hat(rows_j, j, y)
    first = rows_of(k.astype(F32), 16, BF16)
    second = rows_of((k + 1).astype(F32), 16, BF16)
    remote = split(rows_of(z, 16, F32))
    close = split(rows_of(1.0 - z, 16, F32))
    zero = jnp.zeros((16, chunk), BF16)
    place = place_ref[:LANES]
    along_k = []
    for part in range(2):
        for r in range(LANES // 16):
            here = jnp.concatenate([place[16 * r : 16 * r + 16]] * per, axis=1)
            weight = jnp.where(here == second, remote[part], zero)
            along_k.append(jnp.where(here == first, close[part], weight))
    along_k = jnp.concatenate(along_k, axis=0)
    blocks = []
    for f in range(fields):
        value = jnp.concatenate([value_of(f, c * per + q) for q in range(per)], axis=1)
        scaled = along_j * value
        blocks += [along_i * scaled[q : q + 1] for q in range(cells_j)]
    high, low = split(jnp.concatenate(blocks, axis=0))
    total_ref[...] += dot_nt(
        jnp.concatenate([high, low], axis=1), jnp.concatenate([along_k, along_k], axis=1)
    )


def scatter_own_kernel(
    mine_ref,
    count_ref,
    high_ref,
    low_ref,
    from_ref,
    cell_ref,
    weight_ref,
    total_ref,
    got_ref,
    place_ref,
    hot_ref,
    found_ref,
    *,
    sizes,
    chunk,
    gather_chunk,
):
    capacity = cell_ref.shape[1]
    slot_rows = capacity // LANES
    total_ref[...] = jnp.zeros(total_ref.shape, F32)
    got_ref[...] = jnp.zeros(got_ref.shape, F32)
    place_ref[...] = places(2 * LANES, LANES)
    mine = mine_ref[0]
    count = count_ref[mine]

    def put(f, row, value):
        got_ref[pl.ds(f * slot_rows + row, 1), :] = value

    def find_body(c, carry):
        build_hot(hot_ref, 0, from_ref, place_ref[...], mine, c, gather_chunk, sizes)
        hot = hot_ref[...]
        found_ref[...] = dot_nn(high_ref[...], hot) + dot_nn(low_ref[...], hot)
        pick_rows(found_ref, 0, from_ref, mine, c, count, gather_chunk, sizes, put)
        return carry

    lax.fori_loop(0, lax.div(count + (gather_chunk - 1), gather_chunk), find_body, 0)

    def chunk_body(c, carry):
        spread_slots(
            total_ref,
            place_ref,
            lambda f, q: got_ref[pl.ds(f * slot_rows + q, 1), :],
            cell_ref,
            weight_ref,
            mine,
            c,
            sizes,
            chunk,
        )
        return carry

    lax.fori_loop(0, capacity // chunk, chunk_body, 0)


def scatter_own(mine, count, tables, receptor, cell, weight, sizes, chunk=2048, gather_chunk=512):
    vmem = pl.BlockSpec(memory_space=pltpu.VMEM)
    smem = pl.BlockSpec(memory_space=pltpu.SMEM)
    fields, cells_j, cells_i = sizes
    return pl.pallas_call(
        functools.partial(
            scatter_own_kernel, sizes=sizes, chunk=chunk, gather_chunk=gather_chunk
        ),
        out_shape=pltpu.VMEM((fields * cells_i * cells_j, 2 * LANES), F32),
        in_specs=[smem, smem] + [vmem] * 5,
        out_specs=vmem,
        scratch_shapes=[
            pltpu.VMEM((fields * cell.shape[1] // LANES, LANES), F32),
            pltpu.VMEM((2 * LANES, LANES), BF16),
            pltpu.VMEM((2 * LANES, gather_chunk), BF16),
            pltpu.VMEM((tables[0].shape[0], gather_chunk), F32),
        ],
        compiler_params=PARAMS,
        name="scatter_own",
    )(mine, far(count), *map(near, (*tables, receptor, cell, weight)))


def scatter_kernel(*refs, peers, chunk, base):
    mine_ref, block_ref, solve_ref, begun_ref, got_ref, cell_ref, weight_ref, residual_ref = refs[:8]
    refs = refs[8:]
    tile_refs = refs[:peers]
    start_ref = refs[peers]
    send_refs = refs[1 + peers : 1 + 2 * peers]
    total_ref, place_ref, fold_ref = refs[1 + 2 * peers :]
    fields, cells_j, cells_i, _ = residual_ref.shape
    sources, capacity = cell_ref.shape
    rows_j = 16
    slot_rows = capacity // LANES
    total_ref[...] = begun_ref[...]
    place_ref[...] = places(LANES, LANES)
    own = block_ref[0]

    def source_body(at, carry):
        b = at + (at >= own).astype(jnp.int32)

        def chunk_body(c, carry):
            spread_slots(
                total_ref,
                place_ref,
                lambda f, q: got_ref[b, pl.ds(f * slot_rows + q, 1), :],
                cell_ref,
                weight_ref,
                b,
                c,
                (fields, cells_j, cells_i),
                chunk,
            )
            return carry

        return lax.fori_loop(0, capacity // chunk, chunk_body, carry)

    lax.fori_loop(0, sources - 1, source_body, 0)

    fold_ref[...] = total_ref[:, :LANES] + total_ref[:, LANES:]
    mine = mine_ref[0]
    tiles = [ref[...] for ref in tile_refs]
    onward = downstream_map(tiles, base, mine)
    turned = mat2([col(tiles[0], base + 4 + c) for c in range(4)], onward)
    pad = jnp.zeros((rows_j - cells_j, LANES), F32)
    for f in range(fields):
        data = []
        for i in range(cells_i):
            at = pl.ds(f * cells_i * cells_j + i, cells_j, stride=cells_i)
            data.append(jnp.concatenate([fold_ref[at, :] + residual_ref[f, :, i, :], pad], axis=0))

        def solve(direction, columns):
            result = []
            for p in range(cells_i):
                value = solve_ref[direction, f, p * cells_i] * columns[0]
                for q in range(1, p + 1):
                    value = value + solve_ref[direction, f, p * cells_i + q] * columns[q]
                result.append(value)
            return result

        first = solve(0, data)
        second = solve(1, first[::-1])
        e0, e1 = first[-1], first[-2]
        g0, g1 = second[-1], second[-2]
        m = [jnp.broadcast_to(entry[f : f + 1], (rows_j, LANES)) for entry in turned]
        h0 = g0 + m[0] * e0 + m[1] * e1
        h1 = g1 + m[2] * e0 + m[3] * e1
        for i in range(cells_i):
            at = (f * cells_i + i) * rows_j
            start_ref[at : at + rows_j] = second[cells_i - 1 - i]
        for shift in range(peers):
            ahead = mine + shift < peers
            at = f * rows_j
            send_refs[shift][at : at + rows_j] = jnp.where(ahead, e0, h0)
            at = (fields + f) * rows_j
            send_refs[shift][at : at + rows_j] = jnp.where(ahead, e1, h1)


def scatter(mine, block, solve_tiles, begun, got, cell, weight, residual, tiles, base, chunk=2048):
    fields, cells_j, cells_i, _ = residual.shape
    peers = len(tiles)
    rows = fields * cells_i * 16
    vmem = pl.BlockSpec(memory_space=pltpu.VMEM)
    smem = pl.BlockSpec(memory_space=pltpu.SMEM)
    return pl.pallas_call(
        functools.partial(scatter_kernel, peers=peers, chunk=chunk, base=base),
        out_shape=(pltpu.VMEM((rows, LANES), F32),)
        + (pltpu.VMEM((2 * fields * 16, LANES), F32),) * peers,
        in_specs=[smem, smem, smem] + [vmem] * (5 + peers),
        out_specs=(vmem,) * (1 + peers),
        scratch_shapes=[
            pltpu.VMEM((fields * cells_i * cells_j, 2 * LANES), F32),
            pltpu.VMEM((LANES, LANES), BF16),
            pltpu.VMEM((fields * cells_i * cells_j, LANES), F32),
        ],
        compiler_params=PARAMS,
        name="scatter",
    )(mine, block, solve_tiles, *map(near, (begun, got, cell, weight, residual, *tiles)))


def middle_kernel(*refs, peers, base, fields, cells_i):
    mine_ref, own_ref, start_ref, rows_ref, k_tile_ref = refs[:5]
    tile_refs = refs[5 : 5 + peers]
    got_refs = refs[5 + peers : 5 + 2 * peers]
    field_ref, send_ref, end_ref = refs[5 + 2 * peers :]
    rows_j = 16
    mine = mine_ref[0]
    tiles = [ref[...] for ref in tile_refs]
    onward = downstream_map(tiles, base, mine)
    forward = [[col(tile, base + c) for c in range(4)] for tile in tiles]
    backward = [[col(tile, base + 4 + c) for c in range(4)] for tile in tiles]
    end_ref[...] = jnp.zeros(end_ref.shape, F32)
    rows = cells_i * rows_j
    for f in range(fields):

        def wide(entry):
            return jnp.broadcast_to(entry[f : f + 1], (rows_j, LANES))

        def advance(matrix, state, add):
            m = [wide(entry) for entry in matrix]
            return [
                m[0] * state[0] + m[1] * state[1] + add[0],
                m[2] * state[0] + m[3] * state[1] + add[1],
            ]

        got = []
        for shift in range(peers):
            low = got_refs[shift][f * rows_j : (f + 1) * rows_j]
            high = got_refs[shift][(fields + f) * rows_j : (fields + f + 1) * rows_j]
            got.append((low, high))
        zero = jnp.zeros((rows_j, LANES), F32)
        before = [zero, zero]
        for shift in range(peers - 1, 0, -1):
            new = advance(forward[shift], before, got[shift])
            before = [jnp.where(shift <= mine, n, o) for n, o in zip(new, before)]
        after = [zero, zero]
        for shift in range(1, peers):
            new = advance(backward[shift], after, got[shift])
            after = [jnp.where(shift > mine, n, o) for n, o in zip(new, after)]
        onto = advance(forward[0], before, got[0])
        after = advance(onward, onto, after)
        for p in range(cells_i):
            at = (f * cells_i + cells_i - 1 - p) * rows_j
            value = start_ref[at : at + rows_j]
            value = value - own_ref[f, 2 * p] * before[0] - own_ref[f, 2 * p + 1] * before[1]
            shift = 2 * cells_i
            value = value - own_ref[f, shift + 2 * p] * after[0]
            value = value - own_ref[f, shift + 2 * p + 1] * after[1]
            field_ref[at : at + rows_j] = value
        block = field_ref[f * rows : (f + 1) * rows]
        ends = product_nt(rows_ref[f], block)
        for a in range(4):
            end_ref[a * fields + f : a * fields + f + 1, :] = ends[a : a + 1]
    lane = lax.broadcasted_iota(jnp.int32, (fields, LANES), 1)
    for a in range(4):
        part = end_ref[a * fields : (a + 1) * fields]
        for q in range(3):
            entry = col(k_tile_ref[0:fields], 3 * a + q)
            part = jnp.where(lane == rows_j * q + rows_j - 1, entry, part)
        end_ref[a * fields : (a + 1) * fields] = part
    for d in range(send_ref.shape[0]):
        send_ref[d] = end_ref[...]


def middle(mine, own, start, k_rows, k_tile, tiles, got, base, owners, fields, cells_i):
    peers = len(tiles)
    vmem = pl.BlockSpec(memory_space=pltpu.VMEM)
    smem = pl.BlockSpec(memory_space=pltpu.SMEM)
    return pl.pallas_call(
        functools.partial(middle_kernel, peers=peers, base=base, fields=fields, cells_i=cells_i),
        out_shape=(
            pltpu.VMEM(start.shape, F32),
            pltpu.VMEM((owners, 4 * fields, LANES), F32),
        ),
        in_specs=[smem, smem] + [vmem] * (3 + 2 * peers),
        out_specs=(vmem, vmem),
        scratch_shapes=[pltpu.VMEM((4 * fields, LANES), F32)],
        compiler_params=PARAMS,
        name="middle",
    )(mine, own, *map(near, (start, k_rows, k_tile, *tiles, *got)))


def apply_k_kernel(field_ref, map_ref, out_ref):
    fields = map_ref.shape[0]
    rows = field_ref.shape[0] // fields
    length = map_ref.shape[1]
    row_n = lax.broadcasted_iota(jnp.int32, (length, length), 0)
    lane_n = lax.broadcasted_iota(jnp.int32, (length, length), 1)
    turn = jnp.where(row_n + lane_n == length - 1, 1.0, 0.0).astype(BF16)
    for f in range(fields):
        at = slice(f * rows, (f + 1) * rows)
        out_ref[at] = turn_lanes(product_nt(field_ref[at], map_ref[f]), turn)


def apply_k(field, k_map):
    vmem = pl.BlockSpec(memory_space=pltpu.VMEM)
    return pl.pallas_call(
        apply_k_kernel,
        out_shape=pltpu.VMEM(field.shape, F32),
        in_specs=[vmem, vmem],
        out_specs=vmem,
        compiler_params=PARAMS,
        name="apply_k",
    )(near(field), near(k_map))


def finish_kernel(mine_ref, start_ref, got_ref, carry_ref, out_hbm, out_ref, out_sem):
    fields, cells_j, cells_i, _ = out_ref.shape
    rows_j = 16
    rows = cells_i * rows_j
    blocks = got_ref.shape[0]
    mine = mine_ref[0]
    zero = jnp.zeros((fields, LANES), F32)
    part = [
        [got_ref[m, fields * a : fields * (a + 1)] for a in range(4)] for m in range(blocks)
    ]
    entry = [
        [col(part[m][c // 3], rows_j * (c % 3) + rows_j - 1) for c in range(12)]
        for m in range(blocks)
    ]
    states = []
    state = [zero, zero]
    for m in range(blocks):
        states.append(state)
        p = entry[m]
        state = [
            p[0] * state[0] + p[1] * state[1] + part[m][0],
            p[2] * state[0] + p[3] * state[1] + part[m][1],
        ]
    before = [zero, zero]
    after = [zero, zero]
    state = [zero, zero]
    for m in range(blocks - 1, -1, -1):
        here = m == mine
        before = [jnp.where(here, n, o) for n, o in zip(states[m], before)]
        after = [jnp.where(here, n, o) for n, o in zip(state, after)]
        q, b = entry[m][4:8], entry[m][8:12]
        old = states[m]
        state = [
            q[0] * state[0] + q[1] * state[1] + part[m][2] - b[0] * old[0] - b[1] * old[1],
            q[2] * state[0] + q[3] * state[1] + part[m][3] - b[2] * old[0] - b[3] * old[1],
        ]
    for f in range(fields):
        carried = jnp.concatenate(
            [x[f : f + 1] for x in (before[0], before[1], after[0], after[1])]
            + [jnp.zeros((4, LANES), F32)],
            axis=0,
        )
        response = jnp.concatenate(
            [carry_ref[a, f : f + 1, :] for a in range(4)] + [jnp.zeros((4, LANES), F32)], axis=0
        )
        change = dot3(dot_tn, carried, response, 0, 0)
        value = start_ref[f * rows : (f + 1) * rows] - change
        for i in range(cells_i):
            out_ref[f, :, i, :] = value[i * rows_j : i * rows_j + cells_j]
        pltpu.make_async_copy(out_ref.at[f], out_hbm.at[f], out_sem.at[f]).start()
    for f in range(fields):
        pltpu.make_async_copy(out_ref.at[f], out_hbm.at[f], out_sem.at[f]).wait()


def finish(mine, start, got, carry, shape):
    vmem = pl.BlockSpec(memory_space=pltpu.VMEM)
    smem = pl.BlockSpec(memory_space=pltpu.SMEM)
    return pl.pallas_call(
        finish_kernel,
        out_shape=jax.ShapeDtypeStruct(shape, F32),
        in_specs=[smem, vmem, vmem, vmem],
        out_specs=pl.BlockSpec(memory_space=pltpu.HBM),
        scratch_shapes=[pltpu.VMEM(shape, F32), pltpu.SemaphoreType.DMA((shape[0],))],
        compiler_params=PARAMS,
        name="finish",
    )(mine, near(start), near(got), near(carry))


def per_device(
    residual,
    adjoint,
    i_factors,
    k_factors,
    couplings,
    receptor_cell,
    send_count,
    donor_cell,
    donor_weight,
):
    fields, cells_i, cells_j, cells_k = adjoint.shape
    owners = receptor_cell.shape[2]
    peers = lax.axis_size("line")
    line = lax.axis_index("line").astype(jnp.int32).reshape(1)
    block = lax.axis_index("block").astype(jnp.int32).reshape(1)
    base = 4 * cells_i

    adjoint, residual = (x.transpose(0, 2, 1, 3) for x in (adjoint, residual))
    counts = send_count.reshape(owners)
    outgoing, *tables = gather(block, counts, receptor_cell[0, 0], adjoint)
    incoming = lax.all_to_all(outgoing, "block", split_axis=0, concat_axis=0, tiled=True)

    square = i_factors[0].reshape(2, fields, cells_i * cells_i)
    square = jnp.pad(square, ((0, 0), (0, 8 - fields), (0, LANES - cells_i * cells_i)))
    edge = couplings[0, 0, 0:2].reshape(6, fields).T
    edge = jnp.pad(edge, ((0, 8 - fields), (0, LANES - 6)))
    i_tiles = jnp.concatenate([square, edge[None]], axis=0)
    own = prepare_i(i_tiles, cells_i)

    def shifted(value, shift):
        return lax.ppermute(value, "line", [(s, (s + shift) % peers) for s in range(peers)])

    tiles = [own] + [shifted(own, m) for m in range(1, peers)]
    couple = couplings[0, 0].transpose(1, 0, 2)
    couple, _ = lax.optimization_barrier((couple, outgoing))
    k_tile, k_map, k_rows, k_carry = prepare_k(couple, k_factors[0])
    counts, _ = lax.optimization_barrier((counts, k_tile))
    begun = scatter_own(
        block,
        counts,
        tables,
        receptor_cell[0, 0],
        donor_cell[0, 0],
        donor_weight[0, 0],
        (fields, cells_j, cells_i),
    )
    start, *ends = scatter(
        line,
        block,
        i_tiles,
        begun,
        incoming,
        donor_cell[0, 0],
        donor_weight[0, 0],
        residual,
        tiles,
        base,
    )
    got = [ends[0]] + [shifted(ends[m], m) for m in range(1, peers)]
    start, message = middle(
        line, own, start, k_rows, k_tile, tiles, got, base, owners, fields, cells_i
    )
    message = lax.all_to_all(message, "block", split_axis=0, concat_axis=0, tiled=True)
    start = apply_k(start, k_map)
    return finish(block, start, message, k_carry, residual.shape).transpose(0, 2, 1, 3)


def solution(mesh):
    return jax.shard_map(
        per_device,
        mesh=mesh,
        in_specs=(
            P(None, "line", None, "block"),
            P(None, "line", None, "block"),
            P("block", None, None, "line", None),
            P("line", None, None, "block", None),
            P("line", "block", None, None, None),
            P("line", "block", None, None),
            P("line", "block", None),
            P("line", "block", None, None),
            P("line", "block", None, None, None),
        ),
        out_specs=P(None, "line", None, "block"),
        check_vma=False,
    )
```

```python
import functools

import jax
import jax.numpy as jnp
from jax import lax
from jax.experimental import pallas as pl
from jax.experimental.pallas import tpu as pltpu
from jax.sharding import PartitionSpec as P

LANES = 128
F32 = jnp.float32
BF16 = jnp.bfloat16
PARAMS = pltpu.CompilerParams(vmem_limit_bytes=32 * 1024 * 1024)


def split(x):
    high = x.astype(BF16)
    return high, (x - high.astype(F32)).astype(BF16)


def dot_nt(a, b, precision=None):
    return lax.dot_general(
        a, b, (((1,), (1,)), ((), ())), precision=precision, preferred_element_type=F32
    )


def dot_nn(a, b, precision=None):
    return lax.dot_general(
        a, b, (((1,), (0,)), ((), ())), precision=precision, preferred_element_type=F32
    )


def dot_tn(a, b, precision=None):
    return lax.dot_general(
        a, b, (((0,), (0,)), ((), ())), precision=precision, preferred_element_type=F32
    )


def dot3(dot, a, b, axis_a, axis_b):
    a_high, a_low = split(a)
    b_high, b_low = split(b)
    left = jnp.concatenate([a_high, a_high, a_low], axis=axis_a)
    right = jnp.concatenate([b_high, b_low, b_high], axis=axis_b)
    return dot(left, right)


def product_nt(a, b):
    return dot3(dot_nt, a, b, 1, 1)


def product_nn(a, b):
    return dot3(dot_nn, a, b, 1, 0)


def turn_lanes(x, turn):
    return dot_nn(jnp.concatenate(split(x), axis=1), jnp.concatenate([turn, turn], axis=0))


def turn_rows(x, turn):
    return dot_nn(jnp.concatenate([turn, turn], axis=1), jnp.concatenate(split(x), axis=0))


def rows_of(value, count, dtype):
    return jnp.broadcast_to(value, (count, value.shape[1])).astype(dtype)


def places(size, width):
    place = lax.broadcasted_iota(jnp.int32, (size, width), 0)
    return place.astype(F32).astype(BF16)


def split_cell(cell, cells_i, cells_j):
    row = lax.shift_right_logical(cell, 7)
    k = lax.bitwise_and(cell, LANES - 1)
    i = jnp.zeros_like(row)
    for m in range(1, cells_i):
        i = i + (row >= m * cells_j).astype(jnp.int32)
    return i, row - i * cells_j, k


def near(x):
    return pltpu.with_memory_space_constraint(x, pltpu.VMEM)


def far(x):
    return pltpu.with_memory_space_constraint(x, pltpu.HBM)


def col(x, c):
    return jnp.broadcast_to(x[:, c : c + 1], x.shape)


def build_hot(hot_ref, lane, cell_ref, place, d, c, chunk, sizes):
    _, cells_j, cells_i = sizes
    start = pl.multiple_of(c * chunk, chunk)
    cell = cell_ref[pl.ds(d, 1), pl.ds(start, chunk)]
    i, _, k = split_cell(cell, cells_i, cells_j)
    column = (lax.bitwise_and(i, 1) * LANES + k).astype(F32)
    column = rows_of(column, 16, BF16)
    for r in range(2 * LANES // 16):
        here = jnp.concatenate([place[16 * r : 16 * r + 16]] * (chunk // LANES), axis=1)
        hot_ref[16 * r : 16 * r + 16, lane : lane + chunk] = jnp.where(
            here == column, jnp.asarray(1, BF16), jnp.asarray(0, BF16)
        )


def pick_rows(found_ref, lane, cell_ref, d, c, count, chunk, sizes, put):
    fields, cells_j, cells_i = sizes
    rows_j = 16
    rows = cells_i // 2 * rows_j
    per = chunk // LANES
    start = pl.multiple_of(c * chunk, chunk)
    cell = cell_ref[pl.ds(d, 1), pl.ds(start, chunk)]
    i, j, _ = split_cell(cell, cells_i, cells_j)
    slot = start + lax.broadcasted_iota(jnp.int32, cell.shape, 1)
    row = lax.shift_right_logical(i, 1) * rows_j + j
    row = jnp.where(slot < count, row, -1)
    pick = lax.broadcasted_iota(jnp.int32, (rows, chunk), 0) == row
    for f in range(fields):
        value = found_ref[f * rows : (f + 1) * rows, lane : lane + chunk]
        value = jnp.where(pick, value, 0.0)
        value = jnp.sum(value, axis=0, keepdims=True)
        for q in range(per):
            put(f, c * per + q, value[:, q * LANES : (q + 1) * LANES])


def gather_kernel(
    count_hbm,
    cell_hbm,
    field_hbm,
    out_hbm,
    high_ref,
    low_ref,
    cell_ref,
    field_ref,
    out_ref,
    place_ref,
    hot_ref,
    found_ref,
    list_ref,
    count_ref,
    count_sem,
    cell_sem,
    field_sem,
    out_sem,
    *,
    chunk,
    group,
):
    fields, cells_j, cells_i, _ = field_ref.shape
    owners, capacity = cell_ref.shape
    sizes = (fields, cells_j, cells_i)
    rows_j = 16
    half_i = cells_i // 2
    slot_rows = capacity // LANES
    steps = capacity // chunk
    loads = [
        pltpu.make_async_copy(field_hbm.at[f], field_ref.at[f], field_sem.at[f])
        for f in range(fields)
    ]
    cell_load = pltpu.make_async_copy(cell_hbm, cell_ref, cell_sem)
    count_load = pltpu.make_async_copy(count_hbm, count_ref, count_sem)
    count_load.start()
    cell_load.start()
    for load in loads:
        load.start()
    mine = lax.axis_index("block")

    def send(d):
        return pltpu.make_async_copy(out_ref.at[d], out_hbm.at[d], out_sem.at[d])

    out_ref[...] = jnp.zeros(out_ref.shape, F32)
    send(mine).start()
    place_ref[...] = places(2 * LANES, LANES)

    count_load.wait()

    def list_owner(d, total):
        live = jnp.maximum(lax.div(count_ref[d] + (chunk - 1), chunk), 1)
        live = jnp.where(d == mine, 0, live)

        def list_chunk(c, at):
            list_ref[at] = d * steps + c
            return at + 1

        return lax.fori_loop(0, live, list_chunk, total)

    total = lax.fori_loop(0, owners, list_owner, 0)
    groups = lax.div(total + (group - 1), group)

    def place_of(n):
        entry = list_ref[jnp.minimum(n, total - 1)]
        return lax.div(entry, steps), lax.rem(entry, steps)

    def build(n):
        for g in range(group):
            d, c = place_of(n * group + g)
            build_hot(hot_ref, g * chunk, cell_ref, place_ref[...], d, c, chunk, sizes)

    cell_load.wait()
    build(0)
    pad = jnp.zeros((rows_j - cells_j, LANES), F32)
    for f in range(fields):
        loads[f].wait()
        for i in range(cells_i):
            high, low = split(jnp.concatenate([field_ref[f, :, i, :], pad], axis=0))
            at = (f * half_i + i // 2) * rows_j
            lane = (i % 2) * LANES
            high_ref[at : at + rows_j, lane : lane + LANES] = high
            low_ref[at : at + rows_j, lane : lane + LANES] = low

    def pick(n):
        for g in range(group):
            d, c = place_of(n * group + g)

            def put(f, row, value, d=d):
                out_ref[d, pl.ds(f * slot_rows + row, 1), :] = value

            pick_rows(
                found_ref, g * chunk, cell_ref, d, c, count_ref[d], chunk, sizes, put
            )

    def body(n, carry):
        done = jnp.maximum(n - 1, 0)
        pick(done)
        hot = hot_ref[...]
        found_ref[...] = dot_nn(high_ref[...], hot) + dot_nn(low_ref[...], hot)
        build(n + 1)
        for g in range(group):
            here, _ = place_of(done * group + g)
            following, _ = place_of(done * group + g + 1)

            @pl.when((n > 0) & (here != following))
            def _(here=here):
                send(here).start()

        return carry

    lax.fori_loop(0, groups, body, 0)
    pick(groups - 1)
    for g in range(group):
        here, _ = place_of((groups - 1) * group + g)
        following, _ = place_of((groups - 1) * group + g + 1)

        @pl.when(here != following)
        def _(here=here):
            send(here).start()

    last, _ = place_of(total - 1)
    send(last).start()

    def wait_body(d, carry):
        send(d).wait()
        return carry

    lax.fori_loop(0, owners, wait_body, 0)


def gather(count, cell, field, chunk=256, group=4):
    fields, _, cells_i, _ = field.shape
    owners, capacity = cell.shape
    table = (fields * cells_i // 2 * 16, 2 * LANES)
    out = (owners, fields * capacity // LANES, LANES)
    vmem = pl.BlockSpec(memory_space=pltpu.VMEM)
    hbm = pl.BlockSpec(memory_space=pltpu.HBM)
    return pl.pallas_call(
        functools.partial(gather_kernel, chunk=chunk, group=group),
        out_shape=(
            jax.ShapeDtypeStruct(out, F32),
            pltpu.VMEM(table, BF16),
            pltpu.VMEM(table, BF16),
        ),
        in_specs=[hbm, hbm, hbm],
        out_specs=(hbm, vmem, vmem),
        scratch_shapes=[
            pltpu.VMEM(cell.shape, jnp.int32),
            pltpu.VMEM(field.shape, F32),
            pltpu.VMEM(out, F32),
            pltpu.VMEM((2 * LANES, LANES), BF16),
            pltpu.VMEM((2 * LANES, group * chunk), BF16),
            pltpu.VMEM((table[0], group * chunk), F32),
            pltpu.SMEM((owners * capacity // chunk,), jnp.int32),
            pltpu.SMEM((owners,), jnp.int32),
            pltpu.SemaphoreType.DMA(()),
            pltpu.SemaphoreType.DMA(()),
            pltpu.SemaphoreType.DMA((fields,)),
            pltpu.SemaphoreType.DMA((owners,)),
        ],
        compiler_params=PARAMS,
        name="gather",
    )(far(count), far(cell), far(field))


def lay_out(entries):
    lane = lax.broadcasted_iota(jnp.int32, (8, LANES), 1)
    tile = jnp.zeros((8, LANES), F32)
    for at, entry in enumerate(entries):
        tile = jnp.where(lane == at, entry, tile)
    return tile


def edge_entries(couple_ref, direction):
    row = lax.broadcasted_iota(jnp.int32, (8, LANES), 0)
    table = []
    for c in range(3):
        value = jnp.zeros((8, LANES), F32)
        for f in range(couple_ref.shape[2]):
            value = jnp.where(row == f, couple_ref[c, direction, f], value)
        table.append(value)
    return table


def prepare_i_kernel(couple_ref, i_ref, i_out, *, cells_i):
    lower, upper = i_ref[0], i_ref[1]

    def edges(matrix, direction):
        e0, e1, e2 = edge_entries(couple_ref, direction)
        table = []
        for p in range(cells_i):
            first, second = col(matrix, p * cells_i), col(matrix, p * cells_i + 1)
            table.append((first * e0 + second * e2, first * e1))
        return table

    low_edge = edges(lower, 0)
    up_edge = edges(upper, 1)
    through = []
    for p in range(cells_i):
        total = [jnp.zeros((8, LANES), F32), jnp.zeros((8, LANES), F32)]
        for q in range(p + 1):
            factor = col(upper, p * cells_i + q)
            for a in range(2):
                total[a] = total[a] + factor * low_edge[cells_i - 1 - q][a]
        through.append(total)
    last, prior = cells_i - 1, cells_i - 2
    entries = []
    for table in (through, up_edge):
        for p in range(cells_i):
            entries += [table[p][0], table[p][1]]
    entries += [-low_edge[last][0], -low_edge[last][1], -low_edge[prior][0], -low_edge[prior][1]]
    entries += [-up_edge[last][0], -up_edge[last][1], -up_edge[prior][0], -up_edge[prior][1]]
    entries += [through[last][0], through[last][1], through[prior][0], through[prior][1]]
    i_out[...] = lay_out(entries)


def prepare_i(couplings, i_tiles, cells_i):
    return pl.pallas_call(
        functools.partial(prepare_i_kernel, cells_i=cells_i),
        out_shape=pltpu.VMEM((8, LANES), F32),
        in_specs=[
            pl.BlockSpec(memory_space=pltpu.SMEM),
            pl.BlockSpec(memory_space=pltpu.VMEM),
        ],
        out_specs=pl.BlockSpec(memory_space=pltpu.VMEM),
        compiler_params=PARAMS,
        name="prepare_i",
    )(couplings, near(i_tiles))


def prepare_k_kernel(couple_ref, k_ref, k_tile, k_map, k_rows, k_carry):
    fields, length = k_ref.shape[1], k_ref.shape[2]
    row_n = lax.broadcasted_iota(jnp.int32, (length, length), 0)
    lane_n = lax.broadcasted_iota(jnp.int32, (length, length), 1)
    turn = jnp.where(row_n + lane_n == length - 1, 1.0, 0.0).astype(BF16)
    columns = jnp.zeros((length, length), F32)
    for f in range(fields):
        low, up = k_ref[0, f], k_ref[1, f]
        whole = product_nn(up, turn_rows(low, turn))
        k_map[f] = whole
        k_rows[f] = jnp.concatenate(
            [x[length - q : length - q + 1] for x in (low, whole) for q in (1, 2)]
            + [jnp.zeros((4, length), F32)],
            axis=0,
        )
        for m, matrix in enumerate((low, up, whole)):
            for q in range(2):
                value = jnp.broadcast_to(matrix[:, q : q + 1], (length, length))
                columns = jnp.where(lane_n == 16 * m + 8 * q + f, value, columns)
    columns = columns.T
    low0, low1, up0, up1, all0, all1 = (columns[8 * q : 8 * q + 8] for q in range(6))

    e0, e1, e2 = edge_entries(couple_ref, 2)
    d0, d1, d2 = edge_entries(couple_ref, 3)
    first = (low0 * e0 + low1 * e2, low0 * e1)
    through = (all0 * e0 + all1 * e2, all0 * e1)
    second = (up0 * d0 + up1 * d2, up0 * d1)
    turned = turn_lanes(jnp.concatenate(through + second, axis=0), turn)
    for a in range(4):
        k_carry[a] = turned[8 * a : 8 * a + 8]
    ends = [(pair, p) for p in (length - 1, length - 2) for pair in (0, 1)]
    k_tile[...] = lay_out(
        [-col(first[pair], p) for pair, p in ends]
        + [-col(second[pair], p) for pair, p in ends]
        + [col(through[pair], p) for pair, p in ends]
    )


def prepare_k(couplings, k_factors):
    fields, length = k_factors.shape[1], k_factors.shape[2]
    return pl.pallas_call(
        prepare_k_kernel,
        out_shape=(
            pltpu.VMEM((8, LANES), F32),
            pltpu.VMEM((fields, length, length), F32),
            pltpu.VMEM((fields, 8, length), F32),
            pltpu.VMEM((4, 8, length), F32),
        ),
        in_specs=[
            pl.BlockSpec(memory_space=pltpu.SMEM),
            pl.BlockSpec(memory_space=pltpu.VMEM),
        ],
        out_specs=(pl.BlockSpec(memory_space=pltpu.VMEM),) * 4,
        compiler_params=PARAMS,
        name="prepare_k",
    )(couplings, near(k_factors))


def mat2(a, b):
    return [
        a[0] * b[0] + a[1] * b[2],
        a[0] * b[1] + a[1] * b[3],
        a[2] * b[0] + a[3] * b[2],
        a[2] * b[1] + a[3] * b[3],
    ]


def downstream_map(tiles, base, mine):
    peers = len(tiles)
    total = [jnp.zeros((8, LANES), F32)] * 4
    for m in range(1, peers):
        entry = [col(tiles[m], base + c) for c in range(12)]
        step = mat2(mat2(entry[4:8], total), entry[0:4])
        total = [
            jnp.where(m > mine, new - back, old) for new, back, old in zip(step, entry[8:12], total)
        ]
    return total


def spread_slots(total_ref, place_ref, value_of, cell_ref, weight_ref, b, c, sizes, chunk):
    fields, cells_j, cells_i = sizes
    rows_j = 16
    per = chunk // LANES
    start = pl.multiple_of(c * chunk, chunk)
    cell = cell_ref[pl.ds(b, 1), pl.ds(start, chunk)]
    x = weight_ref[0, pl.ds(b, 1), pl.ds(start, chunk)]
    y = weight_ref[1, pl.ds(b, 1), pl.ds(start, chunk)]
    z = weight_ref[2, pl.ds(b, 1), pl.ds(start, chunk)]
    i, j, k = split_cell(cell, cells_i, cells_j)

    def hat(size, at, t):
        place = lax.broadcasted_iota(jnp.int32, (size, chunk), 0)
        return jnp.where(place == at, 1.0 - t, jnp.where(place == at + 1, t, 0.0))

    along_i = hat(cells_i, i, x)
    along_j = hat(rows_j, j, y)
    first = rows_of(k.astype(F32), 16, BF16)
    second = rows_of((k + 1).astype(F32), 16, BF16)
    remote = split(rows_of(z, 16, F32))
    close = split(rows_of(1.0 - z, 16, F32))
    zero = jnp.zeros((16, chunk), BF16)
    place = place_ref[:LANES]
    along_k = []
    for part in range(2):
        for r in range(LANES // 16):
            here = jnp.concatenate([place[16 * r : 16 * r + 16]] * per, axis=1)
            weight = jnp.where(here == second, remote[part], zero)
            along_k.append(jnp.where(here == first, close[part], weight))
    along_k = jnp.concatenate(along_k, axis=0)
    blocks = []
    for f in range(fields):
        value = jnp.concatenate([value_of(f, c * per + q) for q in range(per)], axis=1)
        scaled = along_j * value
        blocks += [along_i * scaled[q : q + 1] for q in range(cells_j)]
    high, low = split(jnp.concatenate(blocks, axis=0))
    total_ref[...] += dot_nt(
        jnp.concatenate([high, low], axis=1), jnp.concatenate([along_k, along_k], axis=1)
    )


def scatter_own_kernel(
    count_ref,
    high_ref,
    low_ref,
    from_ref,
    cell_ref,
    weight_ref,
    total_ref,
    got_ref,
    place_ref,
    hot_ref,
    found_ref,
    *,
    sizes,
    chunk,
    gather_chunk,
):
    capacity = cell_ref.shape[1]
    slot_rows = capacity // LANES
    total_ref[...] = jnp.zeros(total_ref.shape, F32)
    got_ref[...] = jnp.zeros(got_ref.shape, F32)
    place_ref[...] = places(2 * LANES, LANES)
    mine = lax.axis_index("block")
    count = count_ref[mine]

    def put(f, row, value):
        got_ref[pl.ds(f * slot_rows + row, 1), :] = value

    def find_body(c, carry):
        build_hot(hot_ref, 0, from_ref, place_ref[...], mine, c, gather_chunk, sizes)
        hot = hot_ref[...]
        found_ref[...] = dot_nn(high_ref[...], hot) + dot_nn(low_ref[...], hot)
        pick_rows(found_ref, 0, from_ref, mine, c, count, gather_chunk, sizes, put)
        return carry

    lax.fori_loop(0, lax.div(count + (gather_chunk - 1), gather_chunk), find_body, 0)

    def chunk_body(c, carry):
        spread_slots(
            total_ref,
            place_ref,
            lambda f, q: got_ref[pl.ds(f * slot_rows + q, 1), :],
            cell_ref,
            weight_ref,
            mine,
            c,
            sizes,
            chunk,
        )
        return carry

    lax.fori_loop(0, capacity // chunk, chunk_body, 0)


def scatter_own(count, tables, receptor, cell, weight, sizes, chunk=2048, gather_chunk=512):
    vmem = pl.BlockSpec(memory_space=pltpu.VMEM)
    smem = pl.BlockSpec(memory_space=pltpu.SMEM)
    fields, cells_j, cells_i = sizes
    return pl.pallas_call(
        functools.partial(
            scatter_own_kernel, sizes=sizes, chunk=chunk, gather_chunk=gather_chunk
        ),
        out_shape=pltpu.VMEM((fields * cells_i * cells_j, 2 * LANES), F32),
        in_specs=[smem] + [vmem] * 5,
        out_specs=vmem,
        scratch_shapes=[
            pltpu.VMEM((fields * cell.shape[1] // LANES, LANES), F32),
            pltpu.VMEM((2 * LANES, LANES), BF16),
            pltpu.VMEM((2 * LANES, gather_chunk), BF16),
            pltpu.VMEM((tables[0].shape[0], gather_chunk), F32),
        ],
        compiler_params=PARAMS,
        name="scatter_own",
    )(far(count), *map(near, (*tables, receptor, cell, weight)))


def scatter_kernel(*refs, peers, chunk, base):
    factor_ref, begun_ref, got_ref, cell_ref, weight_ref, residual_ref = refs[:6]
    refs = refs[6:]
    tile_refs = refs[:peers]
    start_ref = refs[peers]
    send_refs = refs[1 + peers : 1 + 2 * peers]
    total_ref, place_ref, fold_ref, solve_ref, solve_sem = refs[1 + 2 * peers :]
    fields, cells_j, cells_i, _ = residual_ref.shape
    sources, capacity = cell_ref.shape
    rows_j = 16
    slot_rows = capacity // LANES
    solve_load = pltpu.make_async_copy(factor_ref, solve_ref, solve_sem)
    solve_load.start()
    total_ref[...] = begun_ref[...]
    place_ref[...] = places(LANES, LANES)
    own = lax.axis_index("block")

    def source_body(at, carry):
        b = at + (at >= own).astype(jnp.int32)

        def chunk_body(c, carry):
            spread_slots(
                total_ref,
                place_ref,
                lambda f, q: got_ref[b, pl.ds(f * slot_rows + q, 1), :],
                cell_ref,
                weight_ref,
                b,
                c,
                (fields, cells_j, cells_i),
                chunk,
            )
            return carry

        return lax.fori_loop(0, capacity // chunk, chunk_body, carry)

    lax.fori_loop(0, sources - 1, source_body, 0)

    fold_ref[...] = total_ref[:, :LANES] + total_ref[:, LANES:]
    solve_load.wait()
    mine = lax.axis_index("line")
    tiles = [ref[...] for ref in tile_refs]
    onward = downstream_map(tiles, base, mine)
    turned = mat2([col(tiles[0], base + 4 + c) for c in range(4)], onward)
    pad = jnp.zeros((rows_j - cells_j, LANES), F32)
    for f in range(fields):
        data = []
        for i in range(cells_i):
            at = pl.ds(f * cells_i * cells_j + i, cells_j, stride=cells_i)
            data.append(jnp.concatenate([fold_ref[at, :] + residual_ref[f, :, i, :], pad], axis=0))

        def solve(direction, columns):
            result = []
            for p in range(cells_i):
                value = solve_ref[direction, f, p * cells_i] * columns[0]
                for q in range(1, p + 1):
                    value = value + solve_ref[direction, f, p * cells_i + q] * columns[q]
                result.append(value)
            return result

        first = solve(0, data)
        second = solve(1, first[::-1])
        e0, e1 = first[-1], first[-2]
        g0, g1 = second[-1], second[-2]
        m = [jnp.broadcast_to(entry[f : f + 1], (rows_j, LANES)) for entry in turned]
        h0 = g0 + m[0] * e0 + m[1] * e1
        h1 = g1 + m[2] * e0 + m[3] * e1
        for i in range(cells_i):
            at = (f * cells_i + i) * rows_j
            start_ref[at : at + rows_j] = second[cells_i - 1 - i]
        for shift in range(peers):
            ahead = mine + shift < peers
            at = f * rows_j
            send_refs[shift][at : at + rows_j] = jnp.where(ahead, e0, h0)
            at = (fields + f) * rows_j
            send_refs[shift][at : at + rows_j] = jnp.where(ahead, e1, h1)


def scatter(solve_tiles, begun, got, cell, weight, residual, tiles, base, chunk=2048):
    fields, cells_j, cells_i, _ = residual.shape
    peers = len(tiles)
    rows = fields * cells_i * 16
    vmem = pl.BlockSpec(memory_space=pltpu.VMEM)
    smem = pl.BlockSpec(memory_space=pltpu.SMEM)
    return pl.pallas_call(
        functools.partial(scatter_kernel, peers=peers, chunk=chunk, base=base),
        out_shape=(pltpu.VMEM((rows, LANES), F32),)
        + (pltpu.VMEM((2 * fields * 16, LANES), F32),) * peers,
        in_specs=[vmem] * (6 + peers),
        out_specs=(vmem,) * (1 + peers),
        scratch_shapes=[
            pltpu.VMEM((fields * cells_i * cells_j, 2 * LANES), F32),
            pltpu.VMEM((LANES, LANES), BF16),
            pltpu.VMEM((fields * cells_i * cells_j, LANES), F32),
            pltpu.SMEM(solve_tiles.shape, F32),
            pltpu.SemaphoreType.DMA(()),
        ],
        compiler_params=PARAMS,
        name="scatter",
    )(*map(near, (solve_tiles, begun, got, cell, weight, residual, *tiles)))


def middle_kernel(*refs, peers, base, fields, cells_i):
    start_ref, rows_ref, k_tile_ref = refs[:3]
    tile_refs = refs[3 : 3 + peers]
    got_refs = refs[3 + peers : 3 + 2 * peers]
    field_ref, send_hbm, end_ref, own_ref, own_sem, send_sem = refs[3 + 2 * peers :]
    own_load = pltpu.make_async_copy(tile_refs[0], own_ref, own_sem)
    own_load.start()
    rows_j = 16
    mine = lax.axis_index("line")
    tiles = [ref[...] for ref in tile_refs]
    onward = downstream_map(tiles, base, mine)
    forward = [[col(tile, base + c) for c in range(4)] for tile in tiles]
    backward = [[col(tile, base + 4 + c) for c in range(4)] for tile in tiles]
    end_ref[...] = jnp.zeros(end_ref.shape, F32)
    rows = cells_i * rows_j
    own_load.wait()
    for f in range(fields):

        def wide(entry):
            return jnp.broadcast_to(entry[f : f + 1], (rows_j, LANES))

        def advance(matrix, state, add):
            m = [wide(entry) for entry in matrix]
            return [
                m[0] * state[0] + m[1] * state[1] + add[0],
                m[2] * state[0] + m[3] * state[1] + add[1],
            ]

        got = []
        for shift in range(peers):
            low = got_refs[shift][f * rows_j : (f + 1) * rows_j]
            high = got_refs[shift][(fields + f) * rows_j : (fields + f + 1) * rows_j]
            got.append((low, high))
        zero = jnp.zeros((rows_j, LANES), F32)
        before = [zero, zero]
        for shift in range(peers - 1, 0, -1):
            new = advance(forward[shift], before, got[shift])
            before = [jnp.where(shift <= mine, n, o) for n, o in zip(new, before)]
        after = [zero, zero]
        for shift in range(1, peers):
            new = advance(backward[shift], after, got[shift])
            after = [jnp.where(shift > mine, n, o) for n, o in zip(new, after)]
        onto = advance(forward[0], before, got[0])
        after = advance(onward, onto, after)
        for p in range(cells_i):
            at = (f * cells_i + cells_i - 1 - p) * rows_j
            value = start_ref[at : at + rows_j]
            value = value - own_ref[f, 2 * p] * before[0] - own_ref[f, 2 * p + 1] * before[1]
            shift = 2 * cells_i
            value = value - own_ref[f, shift + 2 * p] * after[0]
            value = value - own_ref[f, shift + 2 * p + 1] * after[1]
            field_ref[at : at + rows_j] = value
        block = field_ref[f * rows : (f + 1) * rows]
        ends = product_nt(rows_ref[f], block)
        for a in range(4):
            end_ref[a * fields + f : a * fields + f + 1, :] = ends[a : a + 1]
    lane = lax.broadcasted_iota(jnp.int32, (fields, LANES), 1)
    for a in range(4):
        part = end_ref[a * fields : (a + 1) * fields]
        for q in range(3):
            entry = col(k_tile_ref[0:fields], 3 * a + q)
            part = jnp.where(lane == rows_j * q + rows_j - 1, entry, part)
        end_ref[a * fields : (a + 1) * fields] = part
    sends = [
        pltpu.make_async_copy(end_ref, send_hbm.at[d], send_sem.at[d])
        for d in range(send_hbm.shape[0])
    ]
    for copy in sends:
        copy.start()
    for copy in sends:
        copy.wait()


def middle(start, k_rows, k_tile, tiles, got, base, owners, fields, cells_i):
    peers = len(tiles)
    vmem = pl.BlockSpec(memory_space=pltpu.VMEM)
    smem = pl.BlockSpec(memory_space=pltpu.SMEM)
    return pl.pallas_call(
        functools.partial(middle_kernel, peers=peers, base=base, fields=fields, cells_i=cells_i),
        out_shape=(
            pltpu.VMEM(start.shape, F32),
            jax.ShapeDtypeStruct((owners, 4 * fields, LANES), F32),
        ),
        in_specs=[vmem] * (3 + 2 * peers),
        out_specs=(vmem, pl.BlockSpec(memory_space=pltpu.HBM)),
        scratch_shapes=[
            pltpu.VMEM((4 * fields, LANES), F32),
            pltpu.SMEM((8, LANES), F32),
            pltpu.SemaphoreType.DMA(()),
            pltpu.SemaphoreType.DMA((owners,)),
        ],
        compiler_params=PARAMS,
        name="middle",
    )(*map(near, (start, k_rows, k_tile, *tiles, *got)))


def apply_k_kernel(field_ref, map_ref, out_ref):
    fields = map_ref.shape[0]
    rows = field_ref.shape[0] // fields
    length = map_ref.shape[1]
    row_n = lax.broadcasted_iota(jnp.int32, (length, length), 0)
    lane_n = lax.broadcasted_iota(jnp.int32, (length, length), 1)
    turn = jnp.where(row_n + lane_n == length - 1, 1.0, 0.0).astype(BF16)
    for f in range(fields):
        at = slice(f * rows, (f + 1) * rows)
        out_ref[at] = turn_lanes(product_nt(field_ref[at], map_ref[f]), turn)


def apply_k(field, k_map):
    vmem = pl.BlockSpec(memory_space=pltpu.VMEM)
    return pl.pallas_call(
        apply_k_kernel,
        out_shape=pltpu.VMEM(field.shape, F32),
        in_specs=[vmem, vmem],
        out_specs=vmem,
        compiler_params=PARAMS,
        name="apply_k",
    )(near(field), near(k_map))


def finish_kernel(start_ref, got_ref, carry_ref, out_hbm, out_ref, out_sem):
    fields, cells_j, cells_i, _ = out_ref.shape
    rows_j = 16
    rows = cells_i * rows_j
    blocks = got_ref.shape[0]
    mine = lax.axis_index("block")
    zero = jnp.zeros((fields, LANES), F32)
    part = [
        [got_ref[m, fields * a : fields * (a + 1)] for a in range(4)] for m in range(blocks)
    ]
    entry = [
        [col(part[m][c // 3], rows_j * (c % 3) + rows_j - 1) for c in range(12)]
        for m in range(blocks)
    ]
    states = []
    state = [zero, zero]
    for m in range(blocks):
        states.append(state)
        p = entry[m]
        state = [
            p[0] * state[0] + p[1] * state[1] + part[m][0],
            p[2] * state[0] + p[3] * state[1] + part[m][1],
        ]
    before = [zero, zero]
    after = [zero, zero]
    state = [zero, zero]
    for m in range(blocks - 1, -1, -1):
        here = m == mine
        before = [jnp.where(here, n, o) for n, o in zip(states[m], before)]
        after = [jnp.where(here, n, o) for n, o in zip(state, after)]
        q, b = entry[m][4:8], entry[m][8:12]
        old = states[m]
        state = [
            q[0] * state[0] + q[1] * state[1] + part[m][2] - b[0] * old[0] - b[1] * old[1],
            q[2] * state[0] + q[3] * state[1] + part[m][3] - b[2] * old[0] - b[3] * old[1],
        ]
    for f in range(fields):
        carried = jnp.concatenate(
            [x[f : f + 1] for x in (before[0], before[1], after[0], after[1])]
            + [jnp.zeros((4, LANES), F32)],
            axis=0,
        )
        response = jnp.concatenate(
            [carry_ref[a, f : f + 1, :] for a in range(4)] + [jnp.zeros((4, LANES), F32)], axis=0
        )
        change = dot3(dot_tn, carried, response, 0, 0)
        value = start_ref[f * rows : (f + 1) * rows] - change
        for i in range(cells_i):
            out_ref[f, :, i, :] = value[i * rows_j : i * rows_j + cells_j]
        pltpu.make_async_copy(out_ref.at[f], out_hbm.at[f], out_sem.at[f]).start()
    for f in range(fields):
        pltpu.make_async_copy(out_ref.at[f], out_hbm.at[f], out_sem.at[f]).wait()


def finish(start, got, carry, shape):
    vmem = pl.BlockSpec(memory_space=pltpu.VMEM)
    smem = pl.BlockSpec(memory_space=pltpu.SMEM)
    return pl.pallas_call(
        finish_kernel,
        out_shape=jax.ShapeDtypeStruct(shape, F32),
        in_specs=[vmem, vmem, vmem],
        out_specs=pl.BlockSpec(memory_space=pltpu.HBM),
        scratch_shapes=[pltpu.VMEM(shape, F32), pltpu.SemaphoreType.DMA((shape[0],))],
        compiler_params=PARAMS,
        name="finish",
    )(near(start), near(got), near(carry))


def per_device(
    residual,
    adjoint,
    i_factors,
    k_factors,
    couplings,
    receptor_cell,
    send_count,
    donor_cell,
    donor_weight,
):
    fields, cells_i, cells_j, cells_k = adjoint.shape
    owners = receptor_cell.shape[2]
    peers = lax.axis_size("line")
    base = 4 * cells_i

    adjoint, residual = (x.transpose(0, 2, 1, 3) for x in (adjoint, residual))
    counts = send_count.reshape(owners)
    outgoing, *tables = gather(counts, receptor_cell[0, 0], adjoint)
    incoming = lax.all_to_all(outgoing, "block", split_axis=0, concat_axis=0, tiled=True)

    square = i_factors[0].reshape(2, fields, cells_i * cells_i)
    i_tiles = jnp.pad(square, ((0, 0), (0, 8 - fields), (0, LANES - cells_i * cells_i)))
    couple = couplings[0, 0].transpose(1, 0, 2)
    own = prepare_i(couple, i_tiles, cells_i)

    def shifted(value, shift):
        return lax.ppermute(value, "line", [(s, (s + shift) % peers) for s in range(peers)])

    tiles = [own] + [shifted(own, m) for m in range(1, peers)]
    begun = scatter_own(
        counts,
        tables,
        receptor_cell[0, 0],
        donor_cell[0, 0],
        donor_weight[0, 0],
        (fields, cells_j, cells_i),
    )
    start, *ends = scatter(
        i_tiles,
        begun,
        incoming,
        donor_cell[0, 0],
        donor_weight[0, 0],
        residual,
        tiles,
        base,
    )
    got = [ends[0]] + [shifted(ends[m], m) for m in range(1, peers)]
    couple, _ = lax.optimization_barrier((couple, ends[0]))
    k_tile, k_map, k_rows, k_carry = prepare_k(couple, k_factors[0])
    start, message = middle(
        start, k_rows, k_tile, tiles, got, base, owners, fields, cells_i
    )
    message = lax.all_to_all(message, "block", split_axis=0, concat_axis=0, tiled=True)
    start = apply_k(start, k_map)
    return finish(start, message, k_carry, residual.shape).transpose(0, 2, 1, 3)


def solution(mesh):
    return jax.shard_map(
        per_device,
        mesh=mesh,
        in_specs=(
            P(None, "line", None, "block"),
            P(None, "line", None, "block"),
            P("block", None, None, "line", None),
            P("line", None, None, "block", None),
            P("line", "block", None, None, None),
            P("line", "block", None, None),
            P("line", "block", None),
            P("line", "block", None, None),
            P("line", "block", None, None, None),
        ),
        out_specs=P(None, "line", None, "block"),
        check_vma=False,
    )
```

```python
import functools

import jax
import jax.numpy as jnp
from jax import lax
from jax.experimental import pallas as pl
from jax.experimental.pallas import tpu as pltpu
from jax.sharding import PartitionSpec as P

LANES = 128
F32 = jnp.float32
BF16 = jnp.bfloat16
PARAMS = pltpu.CompilerParams(vmem_limit_bytes=32 * 1024 * 1024)


def split(x):
    high = x.astype(BF16)
    return high, (x - high.astype(F32)).astype(BF16)


def dot_nt(a, b, precision=None):
    return lax.dot_general(
        a, b, (((1,), (1,)), ((), ())), precision=precision, preferred_element_type=F32
    )


def dot_nn(a, b, precision=None):
    return lax.dot_general(
        a, b, (((1,), (0,)), ((), ())), precision=precision, preferred_element_type=F32
    )


def dot_tn(a, b, precision=None):
    return lax.dot_general(
        a, b, (((0,), (0,)), ((), ())), precision=precision, preferred_element_type=F32
    )


def dot3(dot, a, b, axis_a, axis_b):
    a_high, a_low = split(a)
    b_high, b_low = split(b)
    left = jnp.concatenate([a_high, a_high, a_low], axis=axis_a)
    right = jnp.concatenate([b_high, b_low, b_high], axis=axis_b)
    return dot(left, right)


def product_nt(a, b):
    return dot3(dot_nt, a, b, 1, 1)


def product_nn(a, b):
    return dot3(dot_nn, a, b, 1, 0)


def turn_lanes(x, turn):
    return dot_nn(jnp.concatenate(split(x), axis=1), jnp.concatenate([turn, turn], axis=0))


def turn_rows(x, turn):
    return dot_nn(jnp.concatenate([turn, turn], axis=1), jnp.concatenate(split(x), axis=0))


def rows_of(value, count, dtype):
    return jnp.broadcast_to(value, (count, value.shape[1])).astype(dtype)


def places(size, width):
    place = lax.broadcasted_iota(jnp.int32, (size, width), 0)
    return place.astype(F32).astype(BF16)


def split_cell(cell, cells_i, cells_j):
    row = lax.shift_right_logical(cell, 7)
    k = lax.bitwise_and(cell, LANES - 1)
    i = jnp.zeros_like(row)
    for m in range(1, cells_i):
        i = i + (row >= m * cells_j).astype(jnp.int32)
    return i, row - i * cells_j, k


def near(x):
    return pltpu.with_memory_space_constraint(x, pltpu.VMEM)


def far(x):
    return pltpu.with_memory_space_constraint(x, pltpu.HBM)


def col(x, c):
    return jnp.broadcast_to(x[:, c : c + 1], x.shape)


def build_hot(hot_ref, lane, cell_ref, place, d, c, chunk, sizes):
    _, cells_j, cells_i = sizes
    start = pl.multiple_of(c * chunk, chunk)
    cell = cell_ref[pl.ds(d, 1), pl.ds(start, chunk)]
    i, _, k = split_cell(cell, cells_i, cells_j)
    column = (lax.bitwise_and(i, 1) * LANES + k).astype(F32)
    column = rows_of(column, 16, BF16)
    for r in range(2 * LANES // 16):
        here = jnp.concatenate([place[16 * r : 16 * r + 16]] * (chunk // LANES), axis=1)
        hot_ref[16 * r : 16 * r + 16, lane : lane + chunk] = jnp.where(
            here == column, jnp.asarray(1, BF16), jnp.asarray(0, BF16)
        )


def pick_rows(found_ref, lane, cell_ref, d, c, count, chunk, sizes, put):
    fields, cells_j, cells_i = sizes
    rows_j = 16
    rows = cells_i // 2 * rows_j
    per = chunk // LANES
    start = pl.multiple_of(c * chunk, chunk)
    cell = cell_ref[pl.ds(d, 1), pl.ds(start, chunk)]
    i, j, _ = split_cell(cell, cells_i, cells_j)
    slot = start + lax.broadcasted_iota(jnp.int32, cell.shape, 1)
    row = lax.shift_right_logical(i, 1) * rows_j + j
    row = jnp.where(slot < count, row, -1)
    pick = lax.broadcasted_iota(jnp.int32, (rows, chunk), 0) == row
    for f in range(fields):
        value = found_ref[f * rows : (f + 1) * rows, lane : lane + chunk]
        value = jnp.where(pick, value, 0.0)
        value = jnp.sum(value, axis=0, keepdims=True)
        for q in range(per):
            put(f, c * per + q, value[:, q * LANES : (q + 1) * LANES])


def gather_kernel(
    count_hbm,
    cell_hbm,
    field_hbm,
    out_hbm,
    high_ref,
    low_ref,
    cell_ref,
    field_ref,
    out_ref,
    place_ref,
    hot_ref,
    found_ref,
    list_ref,
    count_ref,
    count_sem,
    cell_sem,
    field_sem,
    out_sem,
    *,
    chunk,
    group,
):
    fields, cells_j, cells_i, _ = field_ref.shape
    owners, capacity = cell_ref.shape
    sizes = (fields, cells_j, cells_i)
    rows_j = 16
    half_i = cells_i // 2
    slot_rows = capacity // LANES
    steps = capacity // chunk
    loads = [
        pltpu.make_async_copy(field_hbm.at[f], field_ref.at[f], field_sem.at[f])
        for f in range(fields)
    ]
    cell_load = pltpu.make_async_copy(cell_hbm, cell_ref, cell_sem)
    count_load = pltpu.make_async_copy(count_hbm, count_ref, count_sem)
    count_load.start()
    cell_load.start()
    for load in loads:
        load.start()
    mine = lax.axis_index("block")

    def send(d):
        return pltpu.make_async_copy(out_ref.at[d], out_hbm.at[d], out_sem.at[d])

    out_ref[...] = jnp.zeros(out_ref.shape, F32)
    send(mine).start()
    place_ref[...] = places(2 * LANES, LANES)

    count_load.wait()

    def list_owner(d, total):
        live = jnp.maximum(lax.div(count_ref[d] + (chunk - 1), chunk), 1)
        live = jnp.where(d == mine, 0, live)

        def list_chunk(c, at):
            list_ref[at] = d * steps + c
            return at + 1

        return lax.fori_loop(0, live, list_chunk, total)

    total = lax.fori_loop(0, owners, list_owner, 0)
    groups = lax.div(total + (group - 1), group)

    def place_of(n):
        entry = list_ref[jnp.minimum(n, total - 1)]
        return lax.div(entry, steps), lax.rem(entry, steps)

    def build(n):
        for g in range(group):
            d, c = place_of(n * group + g)
            build_hot(hot_ref, g * chunk, cell_ref, place_ref[...], d, c, chunk, sizes)

    cell_load.wait()
    build(0)
    pad = jnp.zeros((rows_j - cells_j, LANES), F32)
    for f in range(fields):
        loads[f].wait()
        for i in range(cells_i):
            high, low = split(jnp.concatenate([field_ref[f, :, i, :], pad], axis=0))
            at = (f * half_i + i // 2) * rows_j
            lane = (i % 2) * LANES
            high_ref[at : at + rows_j, lane : lane + LANES] = high
            low_ref[at : at + rows_j, lane : lane + LANES] = low

    def pick(n):
        for g in range(group):
            d, c = place_of(n * group + g)

            def put(f, row, value, d=d):
                out_ref[d, pl.ds(f * slot_rows + row, 1), :] = value

            pick_rows(
                found_ref, g * chunk, cell_ref, d, c, count_ref[d], chunk, sizes, put
            )

    def body(n, carry):
        done = jnp.maximum(n - 1, 0)
        pick(done)
        hot = hot_ref[...]
        found_ref[...] = dot_nn(high_ref[...], hot) + dot_nn(low_ref[...], hot)
        build(n + 1)
        for g in range(group):
            here, _ = place_of(done * group + g)
            following, _ = place_of(done * group + g + 1)

            @pl.when((n > 0) & (here != following))
            def _(here=here):
                send(here).start()

        return carry

    lax.fori_loop(0, groups, body, 0)
    pick(groups - 1)
    for g in range(group):
        here, _ = place_of((groups - 1) * group + g)
        following, _ = place_of((groups - 1) * group + g + 1)

        @pl.when(here != following)
        def _(here=here):
            send(here).start()

    last, _ = place_of(total - 1)
    send(last).start()

    def wait_body(d, carry):
        send(d).wait()
        return carry

    lax.fori_loop(0, owners, wait_body, 0)


def gather(count, cell, field, chunk=256, group=4):
    fields, _, cells_i, _ = field.shape
    owners, capacity = cell.shape
    table = (fields * cells_i // 2 * 16, 2 * LANES)
    out = (owners, fields * capacity // LANES, LANES)
    vmem = pl.BlockSpec(memory_space=pltpu.VMEM)
    hbm = pl.BlockSpec(memory_space=pltpu.HBM)
    return pl.pallas_call(
        functools.partial(gather_kernel, chunk=chunk, group=group),
        out_shape=(
            jax.ShapeDtypeStruct(out, F32),
            pltpu.VMEM(table, BF16),
            pltpu.VMEM(table, BF16),
        ),
        in_specs=[hbm, hbm, hbm],
        out_specs=(hbm, vmem, vmem),
        scratch_shapes=[
            pltpu.VMEM(cell.shape, jnp.int32),
            pltpu.VMEM(field.shape, F32),
            pltpu.VMEM(out, F32),
            pltpu.VMEM((2 * LANES, LANES), BF16),
            pltpu.VMEM((2 * LANES, group * chunk), BF16),
            pltpu.VMEM((table[0], group * chunk), F32),
            pltpu.SMEM((owners * capacity // chunk,), jnp.int32),
            pltpu.SMEM((owners,), jnp.int32),
            pltpu.SemaphoreType.DMA(()),
            pltpu.SemaphoreType.DMA(()),
            pltpu.SemaphoreType.DMA((fields,)),
            pltpu.SemaphoreType.DMA((owners,)),
        ],
        compiler_params=PARAMS,
        name="gather",
    )(far(count), far(cell), far(field))


def lay_out(entries):
    lane = lax.broadcasted_iota(jnp.int32, (8, LANES), 1)
    tile = jnp.zeros((8, LANES), F32)
    for at, entry in enumerate(entries):
        tile = jnp.where(lane == at, entry, tile)
    return tile


def edge_entries(couple_ref, direction):
    row = lax.broadcasted_iota(jnp.int32, (8, LANES), 0)
    table = []
    for c in range(3):
        value = jnp.zeros((8, LANES), F32)
        for f in range(couple_ref.shape[2]):
            value = jnp.where(row == f, couple_ref[c, direction, f], value)
        table.append(value)
    return table


def prepare_i_kernel(couple_ref, i_ref, i_out, *, cells_i):
    lower, upper = i_ref[0], i_ref[1]

    def edges(matrix, direction):
        e0, e1, e2 = edge_entries(couple_ref, direction)
        table = []
        for p in range(cells_i):
            first, second = col(matrix, p * cells_i), col(matrix, p * cells_i + 1)
            table.append((first * e0 + second * e2, first * e1))
        return table

    low_edge = edges(lower, 0)
    up_edge = edges(upper, 1)
    through = []
    for p in range(cells_i):
        total = [jnp.zeros((8, LANES), F32), jnp.zeros((8, LANES), F32)]
        for q in range(p + 1):
            factor = col(upper, p * cells_i + q)
            for a in range(2):
                total[a] = total[a] + factor * low_edge[cells_i - 1 - q][a]
        through.append(total)
    last, prior = cells_i - 1, cells_i - 2
    entries = []
    for table in (through, up_edge):
        for p in range(cells_i):
            entries += [table[p][0], table[p][1]]
    entries += [-low_edge[last][0], -low_edge[last][1], -low_edge[prior][0], -low_edge[prior][1]]
    entries += [-up_edge[last][0], -up_edge[last][1], -up_edge[prior][0], -up_edge[prior][1]]
    entries += [through[last][0], through[last][1], through[prior][0], through[prior][1]]
    i_out[...] = lay_out(entries)


def prepare_i(couplings, i_tiles, cells_i):
    return pl.pallas_call(
        functools.partial(prepare_i_kernel, cells_i=cells_i),
        out_shape=pltpu.VMEM((8, LANES), F32),
        in_specs=[
            pl.BlockSpec(memory_space=pltpu.SMEM),
            pl.BlockSpec(memory_space=pltpu.VMEM),
        ],
        out_specs=pl.BlockSpec(memory_space=pltpu.VMEM),
        compiler_params=PARAMS,
        name="prepare_i",
    )(couplings, near(i_tiles))


def prepare_k_kernel(couple_ref, k_ref, k_tile, k_map, k_rows, k_carry):
    fields, length = k_ref.shape[1], k_ref.shape[2]
    row_n = lax.broadcasted_iota(jnp.int32, (length, length), 0)
    lane_n = lax.broadcasted_iota(jnp.int32, (length, length), 1)
    turn = jnp.where(row_n + lane_n == length - 1, 1.0, 0.0).astype(BF16)
    columns = jnp.zeros((length, length), F32)
    for f in range(fields):
        low, up = k_ref[0, f], k_ref[1, f]
        whole = product_nn(up, turn_rows(low, turn))
        k_map[f] = whole
        k_rows[f] = jnp.concatenate(
            [x[length - q : length - q + 1] for x in (low, whole) for q in (1, 2)]
            + [jnp.zeros((4, length), F32)],
            axis=0,
        )
        for m, matrix in enumerate((low, up, whole)):
            for q in range(2):
                value = jnp.broadcast_to(matrix[:, q : q + 1], (length, length))
                columns = jnp.where(lane_n == 16 * m + 8 * q + f, value, columns)
    columns = columns.T
    low0, low1, up0, up1, all0, all1 = (columns[8 * q : 8 * q + 8] for q in range(6))

    e0, e1, e2 = edge_entries(couple_ref, 2)
    d0, d1, d2 = edge_entries(couple_ref, 3)
    first = (low0 * e0 + low1 * e2, low0 * e1)
    through = (all0 * e0 + all1 * e2, all0 * e1)
    second = (up0 * d0 + up1 * d2, up0 * d1)
    turned = turn_lanes(jnp.concatenate(through + second, axis=0), turn)
    for a in range(4):
        k_carry[a] = turned[8 * a : 8 * a + 8]
    ends = [(pair, p) for p in (length - 1, length - 2) for pair in (0, 1)]
    k_tile[...] = lay_out(
        [-col(first[pair], p) for pair, p in ends]
        + [-col(second[pair], p) for pair, p in ends]
        + [col(through[pair], p) for pair, p in ends]
    )


def prepare_k(couplings, k_factors):
    fields, length = k_factors.shape[1], k_factors.shape[2]
    return pl.pallas_call(
        prepare_k_kernel,
        out_shape=(
            pltpu.VMEM((8, LANES), F32),
            pltpu.VMEM((fields, length, length), F32),
            pltpu.VMEM((fields, 8, length), F32),
            pltpu.VMEM((4, 8, length), F32),
        ),
        in_specs=[
            pl.BlockSpec(memory_space=pltpu.SMEM),
            pl.BlockSpec(memory_space=pltpu.VMEM),
        ],
        out_specs=(pl.BlockSpec(memory_space=pltpu.VMEM),) * 4,
        compiler_params=PARAMS,
        name="prepare_k",
    )(couplings, near(k_factors))


def mat2(a, b):
    return [
        a[0] * b[0] + a[1] * b[2],
        a[0] * b[1] + a[1] * b[3],
        a[2] * b[0] + a[3] * b[2],
        a[2] * b[1] + a[3] * b[3],
    ]


def downstream_map(tiles, base, mine):
    peers = len(tiles)
    total = [jnp.zeros((8, LANES), F32)] * 4
    for m in range(1, peers):
        entry = [col(tiles[m], base + c) for c in range(12)]
        step = mat2(mat2(entry[4:8], total), entry[0:4])
        total = [
            jnp.where(m > mine, new - back, old) for new, back, old in zip(step, entry[8:12], total)
        ]
    return total


def spread_slots(total_ref, place_ref, value_of, cell_ref, weight_ref, units, sizes, size):
    fields, cells_j, cells_i = sizes
    rows_j = 16
    chunk = size * len(units)
    per = chunk // LANES

    def joined(pick):
        return jnp.concatenate([pick(pl.ds(b, 1), pl.ds(at, size)) for b, at in units], axis=1)

    cell = joined(lambda b, at: cell_ref[b, at])
    x, y, z = (joined(lambda b, at, axis=axis: weight_ref[axis, b, at]) for axis in range(3))
    i, j, k = split_cell(cell, cells_i, cells_j)

    def hat(size, at, t):
        place = lax.broadcasted_iota(jnp.int32, (size, chunk), 0)
        return jnp.where(place == at, 1.0 - t, jnp.where(place == at + 1, t, 0.0))

    along_i = hat(cells_i, i, x)
    along_j = hat(rows_j, j, y)
    first = rows_of(k.astype(F32), 16, BF16)
    second = rows_of((k + 1).astype(F32), 16, BF16)
    remote = split(rows_of(z, 16, F32))
    close = split(rows_of(1.0 - z, 16, F32))
    zero = jnp.zeros((16, chunk), BF16)
    place = place_ref[:LANES]
    along_k = []
    for part in range(2):
        for r in range(LANES // 16):
            here = jnp.concatenate([place[16 * r : 16 * r + 16]] * per, axis=1)
            weight = jnp.where(here == second, remote[part], zero)
            along_k.append(jnp.where(here == first, close[part], weight))
    along_k = jnp.concatenate(along_k, axis=0)
    blocks = []
    for f in range(fields):
        value = jnp.concatenate(
            [
                value_of(f, b, at // LANES + q)
                for b, at in units
                for q in range(size // LANES)
            ],
            axis=1,
        )
        scaled = along_j * value
        blocks += [along_i * scaled[q : q + 1] for q in range(cells_j)]
    high, low = split(jnp.concatenate(blocks, axis=0))
    total_ref[...] += dot_nt(
        jnp.concatenate([high, low], axis=1), jnp.concatenate([along_k, along_k], axis=1)
    )


def scatter_own_kernel(
    count_ref,
    high_ref,
    low_ref,
    from_ref,
    cell_ref,
    weight_ref,
    total_ref,
    got_ref,
    place_ref,
    hot_ref,
    found_ref,
    *,
    sizes,
    gather_chunk,
):
    capacity = cell_ref.shape[1]
    slot_rows = capacity // LANES
    total_ref[...] = jnp.zeros(total_ref.shape, F32)
    got_ref[...] = jnp.zeros(got_ref.shape, F32)
    place_ref[...] = places(2 * LANES, LANES)
    mine = lax.axis_index("block")
    count = count_ref[mine]

    def put(f, row, value):
        got_ref[pl.ds(f * slot_rows + row, 1), :] = value

    def find_body(c, carry):
        build_hot(hot_ref, 0, from_ref, place_ref[...], mine, c, gather_chunk, sizes)
        hot = hot_ref[...]
        found_ref[...] = dot_nn(high_ref[...], hot) + dot_nn(low_ref[...], hot)
        pick_rows(found_ref, 0, from_ref, mine, c, count, gather_chunk, sizes, put)
        return carry

    lax.fori_loop(0, lax.div(count + (gather_chunk - 1), gather_chunk), find_body, 0)

    spread_slots(
        total_ref,
        place_ref,
        lambda f, b, q: got_ref[pl.ds(f * slot_rows + q, 1), :],
        cell_ref,
        weight_ref,
        [(mine, 0)],
        sizes,
        capacity,
    )


def scatter_own(count, tables, receptor, cell, weight, sizes, gather_chunk=512):
    vmem = pl.BlockSpec(memory_space=pltpu.VMEM)
    smem = pl.BlockSpec(memory_space=pltpu.SMEM)
    fields, cells_j, cells_i = sizes
    return pl.pallas_call(
        functools.partial(scatter_own_kernel, sizes=sizes, gather_chunk=gather_chunk),
        out_shape=pltpu.VMEM((fields * cells_i * cells_j, 2 * LANES), F32),
        in_specs=[smem] + [vmem] * 5,
        out_specs=vmem,
        scratch_shapes=[
            pltpu.VMEM((fields * cell.shape[1] // LANES, LANES), F32),
            pltpu.VMEM((2 * LANES, LANES), BF16),
            pltpu.VMEM((2 * LANES, gather_chunk), BF16),
            pltpu.VMEM((tables[0].shape[0], gather_chunk), F32),
        ],
        compiler_params=PARAMS,
        name="scatter_own",
    )(far(count), *map(near, (*tables, receptor, cell, weight)))


def scatter_kernel(*refs, peers, chunk, base):
    factor_ref, begun_ref, got_ref, cell_ref, weight_ref, residual_ref = refs[:6]
    refs = refs[6:]
    tile_refs = refs[:peers]
    start_ref = refs[peers]
    send_refs = refs[1 + peers : 1 + 2 * peers]
    total_ref, place_ref, fold_ref, solve_ref, solve_sem = refs[1 + 2 * peers :]
    fields, cells_j, cells_i, _ = residual_ref.shape
    sources, capacity = cell_ref.shape
    rows_j = 16
    slot_rows = capacity // LANES
    solve_load = pltpu.make_async_copy(factor_ref, solve_ref, solve_sem)
    solve_load.start()
    total_ref[...] = begun_ref[...]
    place_ref[...] = places(LANES, LANES)
    own = lax.axis_index("block")

    parts = capacity // chunk
    count = (sources - 1) * parts
    group = max(g for g in range(1, 8) if count % g == 0)

    def step_body(step, carry):
        units = []
        for g in range(group):
            unit = step * group + g
            b = lax.div(unit, parts)
            b = b + (b >= own).astype(jnp.int32)
            units.append((b, pl.multiple_of(lax.rem(unit, parts) * chunk, chunk)))
        spread_slots(
            total_ref,
            place_ref,
            lambda f, b, q: got_ref[b, pl.ds(f * slot_rows + q, 1), :],
            cell_ref,
            weight_ref,
            units,
            (fields, cells_j, cells_i),
            chunk,
        )
        return carry

    lax.fori_loop(0, count // group, step_body, 0)

    fold_ref[...] = total_ref[:, :LANES] + total_ref[:, LANES:]
    solve_load.wait()
    mine = lax.axis_index("line")
    tiles = [ref[...] for ref in tile_refs]
    onward = downstream_map(tiles, base, mine)
    turned = mat2([col(tiles[0], base + 4 + c) for c in range(4)], onward)
    pad = jnp.zeros((rows_j - cells_j, LANES), F32)
    for f in range(fields):
        data = []
        for i in range(cells_i):
            at = pl.ds(f * cells_i * cells_j + i, cells_j, stride=cells_i)
            data.append(jnp.concatenate([fold_ref[at, :] + residual_ref[f, :, i, :], pad], axis=0))

        def solve(direction, columns):
            result = []
            for p in range(cells_i):
                value = solve_ref[direction, f, p * cells_i] * columns[0]
                for q in range(1, p + 1):
                    value = value + solve_ref[direction, f, p * cells_i + q] * columns[q]
                result.append(value)
            return result

        first = solve(0, data)
        second = solve(1, first[::-1])
        e0, e1 = first[-1], first[-2]
        g0, g1 = second[-1], second[-2]
        m = [jnp.broadcast_to(entry[f : f + 1], (rows_j, LANES)) for entry in turned]
        h0 = g0 + m[0] * e0 + m[1] * e1
        h1 = g1 + m[2] * e0 + m[3] * e1
        for i in range(cells_i):
            at = (f * cells_i + i) * rows_j
            start_ref[at : at + rows_j] = second[cells_i - 1 - i]
        for shift in range(peers):
            ahead = mine + shift < peers
            at = f * rows_j
            send_refs[shift][at : at + rows_j] = jnp.where(ahead, e0, h0)
            at = (fields + f) * rows_j
            send_refs[shift][at : at + rows_j] = jnp.where(ahead, e1, h1)


def scatter(solve_tiles, begun, got, cell, weight, residual, tiles, base, chunk=1024):
    fields, cells_j, cells_i, _ = residual.shape
    peers = len(tiles)
    rows = fields * cells_i * 16
    vmem = pl.BlockSpec(memory_space=pltpu.VMEM)
    smem = pl.BlockSpec(memory_space=pltpu.SMEM)
    return pl.pallas_call(
        functools.partial(scatter_kernel, peers=peers, chunk=chunk, base=base),
        out_shape=(pltpu.VMEM((rows, LANES), F32),)
        + (pltpu.VMEM((2 * fields * 16, LANES), F32),) * peers,
        in_specs=[vmem] * (6 + peers),
        out_specs=(vmem,) * (1 + peers),
        scratch_shapes=[
            pltpu.VMEM((fields * cells_i * cells_j, 2 * LANES), F32),
            pltpu.VMEM((LANES, LANES), BF16),
            pltpu.VMEM((fields * cells_i * cells_j, LANES), F32),
            pltpu.SMEM(solve_tiles.shape, F32),
            pltpu.SemaphoreType.DMA(()),
        ],
        compiler_params=PARAMS,
        name="scatter",
    )(*map(near, (solve_tiles, begun, got, cell, weight, residual, *tiles)))


def middle_kernel(*refs, peers, base, fields, cells_i):
    start_ref, rows_ref, k_tile_ref = refs[:3]
    tile_refs = refs[3 : 3 + peers]
    got_refs = refs[3 + peers : 3 + 2 * peers]
    field_ref, send_hbm, end_ref, own_ref, own_sem, send_sem = refs[3 + 2 * peers :]
    own_load = pltpu.make_async_copy(tile_refs[0], own_ref, own_sem)
    own_load.start()
    rows_j = 16
    mine = lax.axis_index("line")
    tiles = [ref[...] for ref in tile_refs]
    onward = downstream_map(tiles, base, mine)
    forward = [[col(tile, base + c) for c in range(4)] for tile in tiles]
    backward = [[col(tile, base + 4 + c) for c in range(4)] for tile in tiles]
    end_ref[...] = jnp.zeros(end_ref.shape, F32)
    rows = cells_i * rows_j
    own_load.wait()
    for f in range(fields):

        def wide(entry):
            return jnp.broadcast_to(entry[f : f + 1], (rows_j, LANES))

        def advance(matrix, state, add):
            m = [wide(entry) for entry in matrix]
            return [
                m[0] * state[0] + m[1] * state[1] + add[0],
                m[2] * state[0] + m[3] * state[1] + add[1],
            ]

        got = []
        for shift in range(peers):
            low = got_refs[shift][f * rows_j : (f + 1) * rows_j]
            high = got_refs[shift][(fields + f) * rows_j : (fields + f + 1) * rows_j]
            got.append((low, high))
        zero = jnp.zeros((rows_j, LANES), F32)
        before = [zero, zero]
        for shift in range(peers - 1, 0, -1):
            new = advance(forward[shift], before, got[shift])
            before = [jnp.where(shift <= mine, n, o) for n, o in zip(new, before)]
        after = [zero, zero]
        for shift in range(1, peers):
            new = advance(backward[shift], after, got[shift])
            after = [jnp.where(shift > mine, n, o) for n, o in zip(new, after)]
        onto = advance(forward[0], before, got[0])
        after = advance(onward, onto, after)
        for p in range(cells_i):
            at = (f * cells_i + cells_i - 1 - p) * rows_j
            value = start_ref[at : at + rows_j]
            value = value - own_ref[f, 2 * p] * before[0] - own_ref[f, 2 * p + 1] * before[1]
            shift = 2 * cells_i
            value = value - own_ref[f, shift + 2 * p] * after[0]
            value = value - own_ref[f, shift + 2 * p + 1] * after[1]
            field_ref[at : at + rows_j] = value
        block = field_ref[f * rows : (f + 1) * rows]
        ends = product_nt(rows_ref[f], block)
        for a in range(4):
            end_ref[a * fields + f : a * fields + f + 1, :] = ends[a : a + 1]
    lane = lax.broadcasted_iota(jnp.int32, (fields, LANES), 1)
    for a in range(4):
        part = end_ref[a * fields : (a + 1) * fields]
        for q in range(3):
            entry = col(k_tile_ref[0:fields], 3 * a + q)
            part = jnp.where(lane == rows_j * q + rows_j - 1, entry, part)
        end_ref[a * fields : (a + 1) * fields] = part
    sends = [
        pltpu.make_async_copy(end_ref, send_hbm.at[d], send_sem.at[d])
        for d in range(send_hbm.shape[0])
    ]
    for copy in sends:
        copy.start()
    for copy in sends:
        copy.wait()


def middle(start, k_rows, k_tile, tiles, got, base, owners, fields, cells_i):
    peers = len(tiles)
    vmem = pl.BlockSpec(memory_space=pltpu.VMEM)
    smem = pl.BlockSpec(memory_space=pltpu.SMEM)
    return pl.pallas_call(
        functools.partial(middle_kernel, peers=peers, base=base, fields=fields, cells_i=cells_i),
        out_shape=(
            pltpu.VMEM(start.shape, F32),
            jax.ShapeDtypeStruct((owners, 4 * fields, LANES), F32),
        ),
        in_specs=[vmem] * (3 + 2 * peers),
        out_specs=(vmem, pl.BlockSpec(memory_space=pltpu.HBM)),
        scratch_shapes=[
            pltpu.VMEM((4 * fields, LANES), F32),
            pltpu.SMEM((8, LANES), F32),
            pltpu.SemaphoreType.DMA(()),
            pltpu.SemaphoreType.DMA((owners,)),
        ],
        compiler_params=PARAMS,
        name="middle",
    )(*map(near, (start, k_rows, k_tile, *tiles, *got)))


def apply_k_kernel(field_ref, map_ref, out_ref):
    fields = map_ref.shape[0]
    rows = field_ref.shape[0] // fields
    length = map_ref.shape[1]
    row_n = lax.broadcasted_iota(jnp.int32, (length, length), 0)
    lane_n = lax.broadcasted_iota(jnp.int32, (length, length), 1)
    turn = jnp.where(row_n + lane_n == length - 1, 1.0, 0.0).astype(BF16)
    for f in range(fields):
        at = slice(f * rows, (f + 1) * rows)
        out_ref[at] = turn_lanes(product_nt(field_ref[at], map_ref[f]), turn)


def apply_k(field, k_map):
    vmem = pl.BlockSpec(memory_space=pltpu.VMEM)
    return pl.pallas_call(
        apply_k_kernel,
        out_shape=pltpu.VMEM(field.shape, F32),
        in_specs=[vmem, vmem],
        out_specs=vmem,
        compiler_params=PARAMS,
        name="apply_k",
    )(near(field), near(k_map))


def finish_kernel(start_ref, got_ref, carry_ref, out_hbm, out_ref, out_sem):
    fields, cells_j, cells_i, _ = out_ref.shape
    rows_j = 16
    rows = cells_i * rows_j
    blocks = got_ref.shape[0]
    mine = lax.axis_index("block")
    zero = jnp.zeros((fields, LANES), F32)
    part = [
        [got_ref[m, fields * a : fields * (a + 1)] for a in range(4)] for m in range(blocks)
    ]
    entry = [
        [col(part[m][c // 3], rows_j * (c % 3) + rows_j - 1) for c in range(12)]
        for m in range(blocks)
    ]
    states = []
    state = [zero, zero]
    for m in range(blocks):
        states.append(state)
        p = entry[m]
        state = [
            p[0] * state[0] + p[1] * state[1] + part[m][0],
            p[2] * state[0] + p[3] * state[1] + part[m][1],
        ]
    before = [zero, zero]
    after = [zero, zero]
    state = [zero, zero]
    for m in range(blocks - 1, -1, -1):
        here = m == mine
        before = [jnp.where(here, n, o) for n, o in zip(states[m], before)]
        after = [jnp.where(here, n, o) for n, o in zip(state, after)]
        q, b = entry[m][4:8], entry[m][8:12]
        old = states[m]
        state = [
            q[0] * state[0] + q[1] * state[1] + part[m][2] - b[0] * old[0] - b[1] * old[1],
            q[2] * state[0] + q[3] * state[1] + part[m][3] - b[2] * old[0] - b[3] * old[1],
        ]
    for f in range(fields):
        carried = jnp.concatenate(
            [x[f : f + 1] for x in (before[0], before[1], after[0], after[1])]
            + [jnp.zeros((4, LANES), F32)],
            axis=0,
        )
        response = jnp.concatenate(
            [carry_ref[a, f : f + 1, :] for a in range(4)] + [jnp.zeros((4, LANES), F32)], axis=0
        )
        change = dot3(dot_tn, carried, response, 0, 0)
        value = start_ref[f * rows : (f + 1) * rows] - change
        for i in range(cells_i):
            out_ref[f, :, i, :] = value[i * rows_j : i * rows_j + cells_j]
        pltpu.make_async_copy(out_ref.at[f], out_hbm.at[f], out_sem.at[f]).start()
    for f in range(fields):
        pltpu.make_async_copy(out_ref.at[f], out_hbm.at[f], out_sem.at[f]).wait()


def finish(start, got, carry, shape):
    vmem = pl.BlockSpec(memory_space=pltpu.VMEM)
    smem = pl.BlockSpec(memory_space=pltpu.SMEM)
    return pl.pallas_call(
        finish_kernel,
        out_shape=jax.ShapeDtypeStruct(shape, F32),
        in_specs=[vmem, vmem, vmem],
        out_specs=pl.BlockSpec(memory_space=pltpu.HBM),
        scratch_shapes=[pltpu.VMEM(shape, F32), pltpu.SemaphoreType.DMA((shape[0],))],
        compiler_params=PARAMS,
        name="finish",
    )(near(start), near(got), near(carry))


def per_device(
    residual,
    adjoint,
    i_factors,
    k_factors,
    couplings,
    receptor_cell,
    send_count,
    donor_cell,
    donor_weight,
):
    fields, cells_i, cells_j, cells_k = adjoint.shape
    owners = receptor_cell.shape[2]
    peers = lax.axis_size("line")
    base = 4 * cells_i

    adjoint, residual = (x.transpose(0, 2, 1, 3) for x in (adjoint, residual))
    counts = send_count.reshape(owners)
    outgoing, *tables = gather(counts, receptor_cell[0, 0], adjoint)
    incoming = lax.all_to_all(outgoing, "block", split_axis=0, concat_axis=0, tiled=True)

    square = i_factors[0].reshape(2, fields, cells_i * cells_i)
    i_tiles = jnp.pad(square, ((0, 0), (0, 8 - fields), (0, LANES - cells_i * cells_i)))
    couple = couplings[0, 0].transpose(1, 0, 2)
    own = prepare_i(couple, i_tiles, cells_i)

    def shifted(value, shift):
        return lax.ppermute(value, "line", [(s, (s + shift) % peers) for s in range(peers)])

    tiles = [own] + [shifted(own, m) for m in range(1, peers)]
    begun = scatter_own(
        counts,
        tables,
        receptor_cell[0, 0],
        donor_cell[0, 0],
        donor_weight[0, 0],
        (fields, cells_j, cells_i),
    )
    start, *ends = scatter(
        i_tiles,
        begun,
        incoming,
        donor_cell[0, 0],
        donor_weight[0, 0],
        residual,
        tiles,
        base,
    )
    got = [ends[0]] + [shifted(ends[m], m) for m in range(1, peers)]
    couple, _ = lax.optimization_barrier((couple, ends[0]))
    k_tile, k_map, k_rows, k_carry = prepare_k(couple, k_factors[0])
    start, message = middle(
        start, k_rows, k_tile, tiles, got, base, owners, fields, cells_i
    )
    message = lax.all_to_all(message, "block", split_axis=0, concat_axis=0, tiled=True)
    start = apply_k(start, k_map)
    return finish(start, message, k_carry, residual.shape).transpose(0, 2, 1, 3)


def solution(mesh):
    return jax.shard_map(
        per_device,
        mesh=mesh,
        in_specs=(
            P(None, "line", None, "block"),
            P(None, "line", None, "block"),
            P("block", None, None, "line", None),
            P("line", None, None, "block", None),
            P("line", "block", None, None, None),
            P("line", "block", None, None),
            P("line", "block", None),
            P("line", "block", None, None),
            P("line", "block", None, None, None),
        ),
        out_specs=P(None, "line", None, "block"),
        check_vma=False,
    )
```

```python
import functools

import jax
import jax.numpy as jnp
from jax import lax
from jax.experimental import pallas as pl
from jax.experimental.pallas import tpu as pltpu
from jax.sharding import PartitionSpec as P

LANES = 128
F32 = jnp.float32
BF16 = jnp.bfloat16
PARAMS = pltpu.CompilerParams(vmem_limit_bytes=32 * 1024 * 1024)


def split(x):
    high = x.astype(BF16)
    return high, (x - high.astype(F32)).astype(BF16)


def dot_nt(a, b, precision=None):
    return lax.dot_general(
        a, b, (((1,), (1,)), ((), ())), precision=precision, preferred_element_type=F32
    )


def dot_nn(a, b, precision=None):
    return lax.dot_general(
        a, b, (((1,), (0,)), ((), ())), precision=precision, preferred_element_type=F32
    )


def dot_tn(a, b, precision=None):
    return lax.dot_general(
        a, b, (((0,), (0,)), ((), ())), precision=precision, preferred_element_type=F32
    )


def dot3(dot, a, b, axis_a, axis_b):
    a_high, a_low = split(a)
    b_high, b_low = split(b)
    left = jnp.concatenate([a_high, a_high, a_low], axis=axis_a)
    right = jnp.concatenate([b_high, b_low, b_high], axis=axis_b)
    return dot(left, right)


def product_nt(a, b):
    return dot3(dot_nt, a, b, 1, 1)


def product_nn(a, b):
    return dot3(dot_nn, a, b, 1, 0)


def turn_lanes(x, turn):
    return dot_nn(jnp.concatenate(split(x), axis=1), jnp.concatenate([turn, turn], axis=0))


def turn_rows(x, turn):
    return dot_nn(jnp.concatenate([turn, turn], axis=1), jnp.concatenate(split(x), axis=0))


def rows_of(value, count, dtype):
    return jnp.broadcast_to(value, (count, value.shape[1])).astype(dtype)


def places(size, width):
    place = lax.broadcasted_iota(jnp.int32, (size, width), 0)
    return place.astype(F32).astype(BF16)


def split_cell(cell, cells_i, cells_j):
    row = lax.shift_right_logical(cell, 7)
    k = lax.bitwise_and(cell, LANES - 1)
    i = jnp.zeros_like(row)
    for m in range(1, cells_i):
        i = i + (row >= m * cells_j).astype(jnp.int32)
    return i, row - i * cells_j, k


def near(x):
    return pltpu.with_memory_space_constraint(x, pltpu.VMEM)


def far(x):
    return pltpu.with_memory_space_constraint(x, pltpu.HBM)


def col(x, c):
    return jnp.broadcast_to(x[:, c : c + 1], x.shape)


def build_hot(hot_ref, lane, cell_ref, place, d, c, chunk, sizes):
    _, cells_j, cells_i = sizes
    start = pl.multiple_of(c * chunk, chunk)
    cell = cell_ref[pl.ds(d, 1), pl.ds(start, chunk)]
    i, _, k = split_cell(cell, cells_i, cells_j)
    column = (lax.bitwise_and(i, 1) * LANES + k).astype(F32)
    column = rows_of(column, 16, BF16)
    for r in range(2 * LANES // 16):
        here = jnp.concatenate([place[16 * r : 16 * r + 16]] * (chunk // LANES), axis=1)
        hot_ref[16 * r : 16 * r + 16, lane : lane + chunk] = jnp.where(
            here == column, jnp.asarray(1, BF16), jnp.asarray(0, BF16)
        )


def pick_rows(found_ref, lane, cell_ref, d, c, count, chunk, sizes, put):
    fields, cells_j, cells_i = sizes
    half_i = cells_i // 2
    rows = half_i * cells_j
    per = chunk // LANES
    start = pl.multiple_of(c * chunk, chunk)
    cell = cell_ref[pl.ds(d, 1), pl.ds(start, chunk)]
    i, j, _ = split_cell(cell, cells_i, cells_j)
    slot = start + lax.broadcasted_iota(jnp.int32, cell.shape, 1)
    row = j * half_i + lax.shift_right_logical(i, 1)
    row = jnp.where(slot < count, row, -8)
    picks = {}
    for f in range(fields):
        base = f * rows // 8 * 8
        offset = f * rows - base
        size = -(-(offset + rows) // 8) * 8
        if offset not in picks:
            place = lax.broadcasted_iota(jnp.int32, (size, chunk), 0)
            picks[offset] = place == row + offset
        value = found_ref[base : base + size, lane : lane + chunk]
        value = jnp.where(picks[offset], value, 0.0)
        value = jnp.sum(value, axis=0, keepdims=True)
        for q in range(per):
            put(f, c * per + q, value[:, q * LANES : (q + 1) * LANES])


def gather_kernel(
    count_hbm,
    cell_hbm,
    field_hbm,
    out_hbm,
    high_ref,
    low_ref,
    cell_ref,
    field_ref,
    out_ref,
    place_ref,
    hot_ref,
    found_ref,
    list_ref,
    count_ref,
    count_sem,
    cell_sem,
    field_sem,
    out_sem,
    *,
    chunk,
    group,
    sizes,
):
    fields, cells_j, cells_i = sizes
    owners, capacity = cell_ref.shape
    rows = cells_j * cells_i
    slot_rows = capacity // LANES
    steps = capacity // chunk
    loads = [
        pltpu.make_async_copy(
            field_hbm.at[pl.ds(f * rows, rows)], field_ref.at[pl.ds(f * rows, rows)], field_sem.at[f]
        )
        for f in range(fields)
    ]
    cell_load = pltpu.make_async_copy(cell_hbm, cell_ref, cell_sem)
    count_load = pltpu.make_async_copy(count_hbm, count_ref, count_sem)
    count_load.start()
    cell_load.start()
    for load in loads:
        load.start()
    mine = lax.axis_index("block")

    def send(d):
        return pltpu.make_async_copy(out_ref.at[d], out_hbm.at[d], out_sem.at[d])

    out_ref[...] = jnp.zeros(out_ref.shape, F32)
    send(mine).start()
    place_ref[...] = places(2 * LANES, LANES)

    count_load.wait()

    def list_owner(d, total):
        live = jnp.maximum(lax.div(count_ref[d] + (chunk - 1), chunk), 1)
        live = jnp.where(d == mine, 0, live)

        def list_chunk(c, at):
            list_ref[at] = d * steps + c
            return at + 1

        return lax.fori_loop(0, live, list_chunk, total)

    total = lax.fori_loop(0, owners, list_owner, 0)
    groups = lax.div(total + (group - 1), group)

    def place_of(n):
        entry = list_ref[jnp.minimum(n, total - 1)]
        return lax.div(entry, steps), lax.rem(entry, steps)

    def build(n):
        for g in range(group):
            d, c = place_of(n * group + g)
            build_hot(hot_ref, g * chunk, cell_ref, place_ref[...], d, c, chunk, sizes)

    cell_load.wait()
    build(0)
    for load in loads:
        load.wait()
    for parity in range(2):
        part = field_ref[pl.ds(parity, fields * rows // 2, stride=2), :]
        high, low = split(part)
        high_ref[:, parity * LANES : (parity + 1) * LANES] = high
        low_ref[:, parity * LANES : (parity + 1) * LANES] = low

    def pick(n):
        for g in range(group):
            d, c = place_of(n * group + g)

            def put(f, row, value, d=d):
                out_ref[d, pl.ds(f * slot_rows + row, 1), :] = value

            pick_rows(
                found_ref, g * chunk, cell_ref, d, c, count_ref[d], chunk, sizes, put
            )

    def body(n, carry):
        done = jnp.maximum(n - 1, 0)
        pick(done)
        hot = hot_ref[...]
        found_ref[...] = dot_nn(high_ref[...], hot) + dot_nn(low_ref[...], hot)
        build(n + 1)
        for g in range(group):
            here, _ = place_of(done * group + g)
            following, _ = place_of(done * group + g + 1)

            @pl.when((n > 0) & (here != following))
            def _(here=here):
                send(here).start()

        return carry

    lax.fori_loop(0, groups, body, 0)
    pick(groups - 1)
    for g in range(group):
        here, _ = place_of((groups - 1) * group + g)
        following, _ = place_of((groups - 1) * group + g + 1)

        @pl.when(here != following)
        def _(here=here):
            send(here).start()

    last, _ = place_of(total - 1)
    send(last).start()

    def wait_body(d, carry):
        send(d).wait()
        return carry

    lax.fori_loop(0, owners, wait_body, 0)


def gather(count, cell, field, chunk=256, group=6):
    fields, cells_j, cells_i, _ = field.shape
    owners, capacity = cell.shape
    field = field.reshape(-1, LANES)
    table = (field.shape[0] // 2, 2 * LANES)
    out = (owners, fields * capacity // LANES, LANES)
    vmem = pl.BlockSpec(memory_space=pltpu.VMEM)
    hbm = pl.BlockSpec(memory_space=pltpu.HBM)
    return pl.pallas_call(
        functools.partial(
            gather_kernel, chunk=chunk, group=group, sizes=(fields, cells_j, cells_i)
        ),
        out_shape=(
            jax.ShapeDtypeStruct(out, F32),
            pltpu.VMEM(table, BF16),
            pltpu.VMEM(table, BF16),
        ),
        in_specs=[hbm, hbm, hbm],
        out_specs=(hbm, vmem, vmem),
        scratch_shapes=[
            pltpu.VMEM(cell.shape, jnp.int32),
            pltpu.VMEM(field.shape, F32),
            pltpu.VMEM(out, F32),
            pltpu.VMEM((2 * LANES, LANES), BF16),
            pltpu.VMEM((2 * LANES, group * chunk), BF16),
            pltpu.VMEM((table[0], group * chunk), F32),
            pltpu.SMEM((owners * capacity // chunk,), jnp.int32),
            pltpu.SMEM((owners,), jnp.int32),
            pltpu.SemaphoreType.DMA(()),
            pltpu.SemaphoreType.DMA(()),
            pltpu.SemaphoreType.DMA((fields,)),
            pltpu.SemaphoreType.DMA((owners,)),
        ],
        compiler_params=PARAMS,
        name="gather",
    )(far(count), far(cell), far(field))


def lay_out(entries):
    lane = lax.broadcasted_iota(jnp.int32, (8, LANES), 1)
    tile = jnp.zeros((8, LANES), F32)
    for at, entry in enumerate(entries):
        tile = jnp.where(lane == at, entry, tile)
    return tile


def edge_entries(couple_ref, direction):
    row = lax.broadcasted_iota(jnp.int32, (8, LANES), 0)
    table = []
    for c in range(3):
        value = jnp.zeros((8, LANES), F32)
        for f in range(couple_ref.shape[2]):
            value = jnp.where(row == f, couple_ref[c, direction, f], value)
        table.append(value)
    return table


def prepare_i_kernel(couple_ref, i_ref, i_out, *, cells_i):
    lower, upper = i_ref[0], i_ref[1]

    def edges(matrix, direction):
        e0, e1, e2 = edge_entries(couple_ref, direction)
        table = []
        for p in range(cells_i):
            first, second = col(matrix, p * cells_i), col(matrix, p * cells_i + 1)
            table.append((first * e0 + second * e2, first * e1))
        return table

    low_edge = edges(lower, 0)
    up_edge = edges(upper, 1)
    through = []
    for p in range(cells_i):
        total = [jnp.zeros((8, LANES), F32), jnp.zeros((8, LANES), F32)]
        for q in range(p + 1):
            factor = col(upper, p * cells_i + q)
            for a in range(2):
                total[a] = total[a] + factor * low_edge[cells_i - 1 - q][a]
        through.append(total)
    last, prior = cells_i - 1, cells_i - 2
    entries = []
    for table in (through, up_edge):
        for p in range(cells_i):
            entries += [table[p][0], table[p][1]]
    entries += [-low_edge[last][0], -low_edge[last][1], -low_edge[prior][0], -low_edge[prior][1]]
    entries += [-up_edge[last][0], -up_edge[last][1], -up_edge[prior][0], -up_edge[prior][1]]
    entries += [through[last][0], through[last][1], through[prior][0], through[prior][1]]
    i_out[...] = lay_out(entries)


def prepare_i(couplings, i_tiles, cells_i):
    return pl.pallas_call(
        functools.partial(prepare_i_kernel, cells_i=cells_i),
        out_shape=pltpu.VMEM((8, LANES), F32),
        in_specs=[
            pl.BlockSpec(memory_space=pltpu.SMEM),
            pl.BlockSpec(memory_space=pltpu.VMEM),
        ],
        out_specs=pl.BlockSpec(memory_space=pltpu.VMEM),
        compiler_params=PARAMS,
        name="prepare_i",
    )(couplings, near(i_tiles))


def prepare_k_kernel(couple_ref, k_ref, k_tile, k_map, k_rows, k_carry):
    fields, length = k_ref.shape[1], k_ref.shape[2]
    row_n = lax.broadcasted_iota(jnp.int32, (length, length), 0)
    lane_n = lax.broadcasted_iota(jnp.int32, (length, length), 1)
    turn = jnp.where(row_n + lane_n == length - 1, 1.0, 0.0).astype(BF16)
    columns = jnp.zeros((length, length), F32)
    for f in range(fields):
        low, up = k_ref[0, f], k_ref[1, f]
        whole = product_nn(up, turn_rows(low, turn))
        k_map[f] = whole
        k_rows[f] = jnp.concatenate(
            [x[length - q : length - q + 1] for x in (low, whole) for q in (1, 2)]
            + [jnp.zeros((4, length), F32)],
            axis=0,
        )
        for m, matrix in enumerate((low, up, whole)):
            for q in range(2):
                value = jnp.broadcast_to(matrix[:, q : q + 1], (length, length))
                columns = jnp.where(lane_n == 16 * m + 8 * q + f, value, columns)
    columns = columns.T
    low0, low1, up0, up1, all0, all1 = (columns[8 * q : 8 * q + 8] for q in range(6))

    e0, e1, e2 = edge_entries(couple_ref, 2)
    d0, d1, d2 = edge_entries(couple_ref, 3)
    first = (low0 * e0 + low1 * e2, low0 * e1)
    through = (all0 * e0 + all1 * e2, all0 * e1)
    second = (up0 * d0 + up1 * d2, up0 * d1)
    turned = turn_lanes(jnp.concatenate(through + second, axis=0), turn)
    for a in range(4):
        k_carry[a] = turned[8 * a : 8 * a + 8]
    ends = [(pair, p) for p in (length - 1, length - 2) for pair in (0, 1)]
    k_tile[...] = lay_out(
        [-col(first[pair], p) for pair, p in ends]
        + [-col(second[pair], p) for pair, p in ends]
        + [col(through[pair], p) for pair, p in ends]
    )


def prepare_k(couplings, k_factors):
    fields, length = k_factors.shape[1], k_factors.shape[2]
    return pl.pallas_call(
        prepare_k_kernel,
        out_shape=(
            pltpu.VMEM((8, LANES), F32),
            pltpu.VMEM((fields, length, length), F32),
            pltpu.VMEM((fields, 8, length), F32),
            pltpu.VMEM((4, 8, length), F32),
        ),
        in_specs=[
            pl.BlockSpec(memory_space=pltpu.SMEM),
            pl.BlockSpec(memory_space=pltpu.VMEM),
        ],
        out_specs=(pl.BlockSpec(memory_space=pltpu.VMEM),) * 4,
        compiler_params=PARAMS,
        name="prepare_k",
    )(couplings, near(k_factors))


def mat2(a, b):
    return [
        a[0] * b[0] + a[1] * b[2],
        a[0] * b[1] + a[1] * b[3],
        a[2] * b[0] + a[3] * b[2],
        a[2] * b[1] + a[3] * b[3],
    ]


def downstream_map(tiles, base, mine):
    peers = len(tiles)
    total = [jnp.zeros((8, LANES), F32)] * 4
    for m in range(1, peers):
        entry = [col(tiles[m], base + c) for c in range(12)]
        step = mat2(mat2(entry[4:8], total), entry[0:4])
        total = [
            jnp.where(m > mine, new - back, old) for new, back, old in zip(step, entry[8:12], total)
        ]
    return total


def spread_slots(total_ref, place_ref, value_of, cell_ref, weight_ref, units, sizes, size):
    fields, cells_j, cells_i = sizes
    rows_j = 16
    chunk = size * len(units)
    per = chunk // LANES

    def joined(pick):
        return jnp.concatenate([pick(pl.ds(b, 1), pl.ds(at, size)) for b, at in units], axis=1)

    cell = joined(lambda b, at: cell_ref[b, at])
    x, y, z = (joined(lambda b, at, axis=axis: weight_ref[axis, b, at]) for axis in range(3))
    i, j, k = split_cell(cell, cells_i, cells_j)

    def hat(size, at, t):
        place = lax.broadcasted_iota(jnp.int32, (size, chunk), 0)
        return jnp.where(place == at, 1.0 - t, jnp.where(place == at + 1, t, 0.0))

    along_i = hat(cells_i, i, x)
    along_j = hat(rows_j, j, y)
    first = rows_of(k.astype(F32), 16, BF16)
    second = rows_of((k + 1).astype(F32), 16, BF16)
    remote = split(rows_of(z, 16, F32))
    close = split(rows_of(1.0 - z, 16, F32))
    zero = jnp.zeros((16, chunk), BF16)
    place = place_ref[:LANES]
    along_k = []
    for part in range(2):
        for r in range(LANES // 16):
            here = jnp.concatenate([place[16 * r : 16 * r + 16]] * per, axis=1)
            weight = jnp.where(here == second, remote[part], zero)
            along_k.append(jnp.where(here == first, close[part], weight))
    along_k = jnp.concatenate(along_k, axis=0)
    blocks = []
    for f in range(fields):
        value = jnp.concatenate(
            [
                value_of(f, b, at // LANES + q)
                for b, at in units
                for q in range(size // LANES)
            ],
            axis=1,
        )
        scaled = along_j * value
        blocks += [along_i * scaled[q : q + 1] for q in range(cells_j)]
    high, low = split(jnp.concatenate(blocks, axis=0))
    total_ref[...] += dot_nt(
        jnp.concatenate([high, low], axis=1), jnp.concatenate([along_k, along_k], axis=1)
    )


def scatter_own_kernel(
    count_ref,
    high_ref,
    low_ref,
    from_ref,
    cell_ref,
    weight_ref,
    total_ref,
    got_ref,
    place_ref,
    hot_ref,
    found_ref,
    *,
    sizes,
    gather_chunk,
):
    capacity = cell_ref.shape[1]
    slot_rows = capacity // LANES
    total_ref[...] = jnp.zeros(total_ref.shape, F32)
    got_ref[...] = jnp.zeros(got_ref.shape, F32)
    place_ref[...] = places(2 * LANES, LANES)
    mine = lax.axis_index("block")
    count = count_ref[mine]

    def put(f, row, value):
        got_ref[pl.ds(f * slot_rows + row, 1), :] = value

    def find_body(c, carry):
        build_hot(hot_ref, 0, from_ref, place_ref[...], mine, c, gather_chunk, sizes)
        hot = hot_ref[...]
        found_ref[...] = dot_nn(high_ref[...], hot) + dot_nn(low_ref[...], hot)
        pick_rows(found_ref, 0, from_ref, mine, c, count, gather_chunk, sizes, put)
        return carry

    lax.fori_loop(0, lax.div(count + (gather_chunk - 1), gather_chunk), find_body, 0)

    spread_slots(
        total_ref,
        place_ref,
        lambda f, b, q: got_ref[pl.ds(f * slot_rows + q, 1), :],
        cell_ref,
        weight_ref,
        [(mine, 0)],
        sizes,
        capacity,
    )


def scatter_own(count, tables, receptor, cell, weight, sizes, gather_chunk=512):
    vmem = pl.BlockSpec(memory_space=pltpu.VMEM)
    smem = pl.BlockSpec(memory_space=pltpu.SMEM)
    fields, cells_j, cells_i = sizes
    return pl.pallas_call(
        functools.partial(scatter_own_kernel, sizes=sizes, gather_chunk=gather_chunk),
        out_shape=pltpu.VMEM((fields * cells_i * cells_j, 2 * LANES), F32),
        in_specs=[smem] + [vmem] * 5,
        out_specs=vmem,
        scratch_shapes=[
            pltpu.VMEM((fields * cell.shape[1] // LANES, LANES), F32),
            pltpu.VMEM((2 * LANES, LANES), BF16),
            pltpu.VMEM((2 * LANES, gather_chunk), BF16),
            pltpu.VMEM((tables[0].shape[0], gather_chunk), F32),
        ],
        compiler_params=PARAMS,
        name="scatter_own",
    )(far(count), *map(near, (*tables, receptor, cell, weight)))


def scatter_kernel(*refs, peers, chunk, base):
    factor_ref, begun_ref, got_ref, cell_ref, weight_ref, residual_ref = refs[:6]
    refs = refs[6:]
    tile_refs = refs[:peers]
    start_ref = refs[peers]
    send_refs = refs[1 + peers : 1 + 2 * peers]
    total_ref, place_ref, fold_ref, solve_ref, solve_sem = refs[1 + 2 * peers :]
    fields, cells_j, cells_i, _ = residual_ref.shape
    sources, capacity = cell_ref.shape
    rows_j = 16
    slot_rows = capacity // LANES
    solve_load = pltpu.make_async_copy(factor_ref, solve_ref, solve_sem)
    solve_load.start()
    total_ref[...] = begun_ref[...]
    place_ref[...] = places(LANES, LANES)
    own = lax.axis_index("block")

    parts = capacity // chunk
    count = (sources - 1) * parts
    group = max(g for g in range(1, 8) if count % g == 0)

    def step_body(step, carry):
        units = []
        for g in range(group):
            unit = step * group + g
            b = lax.div(unit, parts)
            b = b + (b >= own).astype(jnp.int32)
            units.append((b, pl.multiple_of(lax.rem(unit, parts) * chunk, chunk)))
        spread_slots(
            total_ref,
            place_ref,
            lambda f, b, q: got_ref[b, pl.ds(f * slot_rows + q, 1), :],
            cell_ref,
            weight_ref,
            units,
            (fields, cells_j, cells_i),
            chunk,
        )
        return carry

    lax.fori_loop(0, count // group, step_body, 0)

    fold_ref[...] = total_ref[:, :LANES] + total_ref[:, LANES:]
    solve_load.wait()
    mine = lax.axis_index("line")
    tiles = [ref[...] for ref in tile_refs]
    onward = downstream_map(tiles, base, mine)
    turned = mat2([col(tiles[0], base + 4 + c) for c in range(4)], onward)
    pad = jnp.zeros((rows_j - cells_j, LANES), F32)
    for f in range(fields):
        data = []
        for i in range(cells_i):
            at = pl.ds(f * cells_i * cells_j + i, cells_j, stride=cells_i)
            data.append(jnp.concatenate([fold_ref[at, :] + residual_ref[f, :, i, :], pad], axis=0))

        def solve(direction, columns):
            result = []
            for p in range(cells_i):
                value = solve_ref[direction, f, p * cells_i] * columns[0]
                for q in range(1, p + 1):
                    value = value + solve_ref[direction, f, p * cells_i + q] * columns[q]
                result.append(value)
            return result

        first = solve(0, data)
        second = solve(1, first[::-1])
        e0, e1 = first[-1], first[-2]
        g0, g1 = second[-1], second[-2]
        m = [jnp.broadcast_to(entry[f : f + 1], (rows_j, LANES)) for entry in turned]
        h0 = g0 + m[0] * e0 + m[1] * e1
        h1 = g1 + m[2] * e0 + m[3] * e1
        for i in range(cells_i):
            at = (f * cells_i + i) * rows_j
            start_ref[at : at + rows_j] = second[cells_i - 1 - i]
        for shift in range(peers):
            ahead = mine + shift < peers
            at = f * rows_j
            send_refs[shift][at : at + rows_j] = jnp.where(ahead, e0, h0)
            at = (fields + f) * rows_j
            send_refs[shift][at : at + rows_j] = jnp.where(ahead, e1, h1)


def scatter(solve_tiles, begun, got, cell, weight, residual, tiles, base, chunk=1024):
    fields, cells_j, cells_i, _ = residual.shape
    peers = len(tiles)
    rows = fields * cells_i * 16
    vmem = pl.BlockSpec(memory_space=pltpu.VMEM)
    smem = pl.BlockSpec(memory_space=pltpu.SMEM)
    return pl.pallas_call(
        functools.partial(scatter_kernel, peers=peers, chunk=chunk, base=base),
        out_shape=(pltpu.VMEM((rows, LANES), F32),)
        + (pltpu.VMEM((2 * fields * 16, LANES), F32),) * peers,
        in_specs=[vmem] * (6 + peers),
        out_specs=(vmem,) * (1 + peers),
        scratch_shapes=[
            pltpu.VMEM((fields * cells_i * cells_j, 2 * LANES), F32),
            pltpu.VMEM((LANES, LANES), BF16),
            pltpu.VMEM((fields * cells_i * cells_j, LANES), F32),
            pltpu.SMEM(solve_tiles.shape, F32),
            pltpu.SemaphoreType.DMA(()),
        ],
        compiler_params=PARAMS,
        name="scatter",
    )(*map(near, (solve_tiles, begun, got, cell, weight, residual, *tiles)))


def middle_kernel(*refs, peers, base, fields, cells_i):
    start_ref, rows_ref, k_tile_ref = refs[:3]
    tile_refs = refs[3 : 3 + peers]
    got_refs = refs[3 + peers : 3 + 2 * peers]
    field_ref, send_hbm, end_ref, own_ref, own_sem, send_sem = refs[3 + 2 * peers :]
    own_load = pltpu.make_async_copy(tile_refs[0], own_ref, own_sem)
    own_load.start()
    rows_j = 16
    mine = lax.axis_index("line")
    tiles = [ref[...] for ref in tile_refs]
    onward = downstream_map(tiles, base, mine)
    forward = [[col(tile, base + c) for c in range(4)] for tile in tiles]
    backward = [[col(tile, base + 4 + c) for c in range(4)] for tile in tiles]
    end_ref[...] = jnp.zeros(end_ref.shape, F32)
    rows = cells_i * rows_j
    own_load.wait()
    for f in range(fields):

        def wide(entry):
            return jnp.broadcast_to(entry[f : f + 1], (rows_j, LANES))

        def advance(matrix, state, add):
            m = [wide(entry) for entry in matrix]
            return [
                m[0] * state[0] + m[1] * state[1] + add[0],
                m[2] * state[0] + m[3] * state[1] + add[1],
            ]

        got = []
        for shift in range(peers):
            low = got_refs[shift][f * rows_j : (f + 1) * rows_j]
            high = got_refs[shift][(fields + f) * rows_j : (fields + f + 1) * rows_j]
            got.append((low, high))
        zero = jnp.zeros((rows_j, LANES), F32)
        before = [zero, zero]
        for shift in range(peers - 1, 0, -1):
            new = advance(forward[shift], before, got[shift])
            before = [jnp.where(shift <= mine, n, o) for n, o in zip(new, before)]
        after = [zero, zero]
        for shift in range(1, peers):
            new = advance(backward[shift], after, got[shift])
            after = [jnp.where(shift > mine, n, o) for n, o in zip(new, after)]
        onto = advance(forward[0], before, got[0])
        after = advance(onward, onto, after)
        for p in range(cells_i):
            at = (f * cells_i + cells_i - 1 - p) * rows_j
            value = start_ref[at : at + rows_j]
            value = value - own_ref[f, 2 * p] * before[0] - own_ref[f, 2 * p + 1] * before[1]
            shift = 2 * cells_i
            value = value - own_ref[f, shift + 2 * p] * after[0]
            value = value - own_ref[f, shift + 2 * p + 1] * after[1]
            field_ref[at : at + rows_j] = value
        block = field_ref[f * rows : (f + 1) * rows]
        r_high, r_low = split(rows_ref[f])
        both = dot_nt(
            jnp.concatenate([r_high, r_low], axis=0), jnp.concatenate(split(block), axis=0)
        )
        ends = both[:8, :rows] + both[:8, rows:] + both[8:, :rows]
        for a in range(4):
            end_ref[a * fields + f : a * fields + f + 1, :] = ends[a : a + 1]
    lane = lax.broadcasted_iota(jnp.int32, (fields, LANES), 1)
    for a in range(4):
        part = end_ref[a * fields : (a + 1) * fields]
        for q in range(3):
            entry = col(k_tile_ref[0:fields], 3 * a + q)
            part = jnp.where(lane == rows_j * q + rows_j - 1, entry, part)
        end_ref[a * fields : (a + 1) * fields] = part
    sends = [
        pltpu.make_async_copy(end_ref, send_hbm.at[d], send_sem.at[d])
        for d in range(send_hbm.shape[0])
    ]
    for copy in sends:
        copy.start()
    for copy in sends:
        copy.wait()


def middle(start, k_rows, k_tile, tiles, got, base, owners, fields, cells_i):
    peers = len(tiles)
    vmem = pl.BlockSpec(memory_space=pltpu.VMEM)
    smem = pl.BlockSpec(memory_space=pltpu.SMEM)
    return pl.pallas_call(
        functools.partial(middle_kernel, peers=peers, base=base, fields=fields, cells_i=cells_i),
        out_shape=(
            pltpu.VMEM(start.shape, F32),
            jax.ShapeDtypeStruct((owners, 4 * fields, LANES), F32),
        ),
        in_specs=[vmem] * (3 + 2 * peers),
        out_specs=(vmem, pl.BlockSpec(memory_space=pltpu.HBM)),
        scratch_shapes=[
            pltpu.VMEM((4 * fields, LANES), F32),
            pltpu.SMEM((8, LANES), F32),
            pltpu.SemaphoreType.DMA(()),
            pltpu.SemaphoreType.DMA((owners,)),
        ],
        compiler_params=PARAMS,
        name="middle",
    )(*map(near, (start, k_rows, k_tile, *tiles, *got)))


def apply_k_kernel(field_ref, map_ref, out_ref):
    fields = map_ref.shape[0]
    rows = field_ref.shape[0] // fields
    length = map_ref.shape[1]
    row_n = lax.broadcasted_iota(jnp.int32, (length, length), 0)
    lane_n = lax.broadcasted_iota(jnp.int32, (length, length), 1)
    turn = jnp.where(row_n + lane_n == length - 1, 1.0, 0.0).astype(BF16)
    for f in range(fields):
        at = slice(f * rows, (f + 1) * rows)
        out_ref[at] = turn_lanes(product_nt(field_ref[at], map_ref[f]), turn)


def apply_k(field, k_map):
    vmem = pl.BlockSpec(memory_space=pltpu.VMEM)
    return pl.pallas_call(
        apply_k_kernel,
        out_shape=pltpu.VMEM(field.shape, F32),
        in_specs=[vmem, vmem],
        out_specs=vmem,
        compiler_params=PARAMS,
        name="apply_k",
    )(near(field), near(k_map))


def finish_kernel(start_ref, got_ref, carry_ref, out_hbm, out_ref, out_sem):
    fields, cells_j, cells_i, _ = out_ref.shape
    rows_j = 16
    rows = cells_i * rows_j
    blocks = got_ref.shape[0]
    mine = lax.axis_index("block")
    zero = jnp.zeros((fields, LANES), F32)
    part = [
        [got_ref[m, fields * a : fields * (a + 1)] for a in range(4)] for m in range(blocks)
    ]
    entry = [
        [col(part[m][c // 3], rows_j * (c % 3) + rows_j - 1) for c in range(12)]
        for m in range(blocks)
    ]
    states = []
    state = [zero, zero]
    for m in range(blocks):
        states.append(state)
        p = entry[m]
        state = [
            p[0] * state[0] + p[1] * state[1] + part[m][0],
            p[2] * state[0] + p[3] * state[1] + part[m][1],
        ]
    before = [zero, zero]
    after = [zero, zero]
    state = [zero, zero]
    for m in range(blocks - 1, -1, -1):
        here = m == mine
        before = [jnp.where(here, n, o) for n, o in zip(states[m], before)]
        after = [jnp.where(here, n, o) for n, o in zip(state, after)]
        q, b = entry[m][4:8], entry[m][8:12]
        old = states[m]
        state = [
            q[0] * state[0] + q[1] * state[1] + part[m][2] - b[0] * old[0] - b[1] * old[1],
            q[2] * state[0] + q[3] * state[1] + part[m][3] - b[2] * old[0] - b[3] * old[1],
        ]
    for f in range(fields):
        carried = jnp.concatenate(
            [x[f : f + 1] for x in (before[0], before[1], after[0], after[1])]
            + [jnp.zeros((4, LANES), F32)],
            axis=0,
        )
        response = jnp.concatenate(
            [carry_ref[a, f : f + 1, :] for a in range(4)] + [jnp.zeros((4, LANES), F32)], axis=0
        )
        change = dot3(dot_tn, carried, response, 0, 0)
        value = start_ref[f * rows : (f + 1) * rows] - change
        for i in range(cells_i):
            out_ref[f, :, i, :] = value[i * rows_j : i * rows_j + cells_j]
        pltpu.make_async_copy(out_ref.at[f], out_hbm.at[f], out_sem.at[f]).start()
    for f in range(fields):
        pltpu.make_async_copy(out_ref.at[f], out_hbm.at[f], out_sem.at[f]).wait()


def finish(start, got, carry, shape):
    vmem = pl.BlockSpec(memory_space=pltpu.VMEM)
    smem = pl.BlockSpec(memory_space=pltpu.SMEM)
    return pl.pallas_call(
        finish_kernel,
        out_shape=jax.ShapeDtypeStruct(shape, F32),
        in_specs=[vmem, vmem, vmem],
        out_specs=pl.BlockSpec(memory_space=pltpu.HBM),
        scratch_shapes=[pltpu.VMEM(shape, F32), pltpu.SemaphoreType.DMA((shape[0],))],
        compiler_params=PARAMS,
        name="finish",
    )(near(start), near(got), near(carry))


def per_device(
    residual,
    adjoint,
    i_factors,
    k_factors,
    couplings,
    receptor_cell,
    send_count,
    donor_cell,
    donor_weight,
):
    fields, cells_i, cells_j, cells_k = adjoint.shape
    owners = receptor_cell.shape[2]
    peers = lax.axis_size("line")
    base = 4 * cells_i

    adjoint, residual = (x.transpose(0, 2, 1, 3) for x in (adjoint, residual))
    counts = send_count.reshape(owners)
    outgoing, *tables = gather(counts, receptor_cell[0, 0], adjoint)
    incoming = lax.all_to_all(outgoing, "block", split_axis=0, concat_axis=0, tiled=True)

    square = i_factors[0].reshape(2, fields, cells_i * cells_i)
    i_tiles = jnp.pad(square, ((0, 0), (0, 8 - fields), (0, LANES - cells_i * cells_i)))
    couple = couplings[0, 0].transpose(1, 0, 2)
    own = prepare_i(couple, i_tiles, cells_i)

    def shifted(value, shift):
        return lax.ppermute(value, "line", [(s, (s + shift) % peers) for s in range(peers)])

    tiles = [own] + [shifted(own, m) for m in range(1, peers)]
    begun = scatter_own(
        counts,
        tables,
        receptor_cell[0, 0],
        donor_cell[0, 0],
        donor_weight[0, 0],
        (fields, cells_j, cells_i),
    )
    start, *ends = scatter(
        i_tiles,
        begun,
        incoming,
        donor_cell[0, 0],
        donor_weight[0, 0],
        residual,
        tiles,
        base,
    )
    got = [ends[0]] + [shifted(ends[m], m) for m in range(1, peers)]
    couple, _ = lax.optimization_barrier((couple, ends[0]))
    k_tile, k_map, k_rows, k_carry = prepare_k(couple, k_factors[0])
    start, message = middle(
        start, k_rows, k_tile, tiles, got, base, owners, fields, cells_i
    )
    message = lax.all_to_all(message, "block", split_axis=0, concat_axis=0, tiled=True)
    start = apply_k(start, k_map)
    return finish(start, message, k_carry, residual.shape).transpose(0, 2, 1, 3)


def solution(mesh):
    return jax.shard_map(
        per_device,
        mesh=mesh,
        in_specs=(
            P(None, "line", None, "block"),
            P(None, "line", None, "block"),
            P("block", None, None, "line", None),
            P("line", None, None, "block", None),
            P("line", "block", None, None, None),
            P("line", "block", None, None),
            P("line", "block", None),
            P("line", "block", None, None),
            P("line", "block", None, None, None),
        ),
        out_specs=P(None, "line", None, "block"),
        check_vma=False,
    )
```

```python
import functools

import jax
import jax.numpy as jnp
from jax import lax
from jax.experimental import pallas as pl
from jax.experimental.pallas import tpu as pltpu
from jax.sharding import PartitionSpec as P

LANES = 128
F32 = jnp.float32
BF16 = jnp.bfloat16
PARAMS = pltpu.CompilerParams(vmem_limit_bytes=32 * 1024 * 1024)


def split(x):
    high = x.astype(BF16)
    return high, (x - high.astype(F32)).astype(BF16)


def dot_nt(a, b, precision=None):
    return lax.dot_general(
        a, b, (((1,), (1,)), ((), ())), precision=precision, preferred_element_type=F32
    )


def dot_nn(a, b, precision=None):
    return lax.dot_general(
        a, b, (((1,), (0,)), ((), ())), precision=precision, preferred_element_type=F32
    )


def dot_tn(a, b, precision=None):
    return lax.dot_general(
        a, b, (((0,), (0,)), ((), ())), precision=precision, preferred_element_type=F32
    )


def dot3(dot, a, b, axis_a, axis_b):
    a_high, a_low = split(a)
    b_high, b_low = split(b)
    left = jnp.concatenate([a_high, a_high, a_low], axis=axis_a)
    right = jnp.concatenate([b_high, b_low, b_high], axis=axis_b)
    return dot(left, right)


def product_nt(a, b):
    return dot3(dot_nt, a, b, 1, 1)


def product_nn(a, b):
    return dot3(dot_nn, a, b, 1, 0)


def turn_lanes(x, turn):
    return dot_nn(jnp.concatenate(split(x), axis=1), jnp.concatenate([turn, turn], axis=0))


def turn_rows(x, turn):
    return dot_nn(jnp.concatenate([turn, turn], axis=1), jnp.concatenate(split(x), axis=0))


def rows_of(value, count, dtype):
    return jnp.broadcast_to(value, (count, value.shape[1])).astype(dtype)


def places(size, width):
    place = lax.broadcasted_iota(jnp.int32, (size, width), 0)
    return place.astype(F32).astype(BF16)


def split_cell(cell, cells_i, cells_j):
    row = lax.shift_right_logical(cell, 7)
    k = lax.bitwise_and(cell, LANES - 1)
    i = jnp.zeros_like(row)
    for m in range(1, cells_i):
        i = i + (row >= m * cells_j).astype(jnp.int32)
    return i, row - i * cells_j, k


def near(x):
    return pltpu.with_memory_space_constraint(x, pltpu.VMEM)


def far(x):
    return pltpu.with_memory_space_constraint(x, pltpu.HBM)


def col(x, c):
    return jnp.broadcast_to(x[:, c : c + 1], x.shape)


def build_hot(hot_ref, lane, cell_ref, place, d, c, chunk, sizes):
    _, cells_j, cells_i = sizes
    start = pl.multiple_of(c * chunk, chunk)
    cell = cell_ref[pl.ds(d, 1), pl.ds(start, chunk)]
    i, _, k = split_cell(cell, cells_i, cells_j)
    column = (lax.bitwise_and(i, 1) * LANES + k).astype(F32)
    column = rows_of(column, 16, BF16)
    for r in range(2 * LANES // 16):
        here = jnp.concatenate([place[16 * r : 16 * r + 16]] * (chunk // LANES), axis=1)
        hot_ref[16 * r : 16 * r + 16, lane : lane + chunk] = jnp.where(
            here == column, jnp.asarray(1, BF16), jnp.asarray(0, BF16)
        )


def pick_rows(found_ref, lane, cell_ref, d, c, count, chunk, sizes, put):
    fields, cells_j, cells_i = sizes
    half_i = cells_i // 2
    rows = half_i * cells_j
    per = chunk // LANES
    start = pl.multiple_of(c * chunk, chunk)
    cell = cell_ref[pl.ds(d, 1), pl.ds(start, chunk)]
    i, j, _ = split_cell(cell, cells_i, cells_j)
    slot = start + lax.broadcasted_iota(jnp.int32, cell.shape, 1)
    row = j * half_i + lax.shift_right_logical(i, 1)
    row = jnp.where(slot < count, row, -8)
    picks = {}
    for f in range(fields):
        base = f * rows // 8 * 8
        offset = f * rows - base
        size = -(-(offset + rows) // 8) * 8
        if offset not in picks:
            place = lax.broadcasted_iota(jnp.int32, (size, chunk), 0)
            picks[offset] = place == row + offset
        value = found_ref[base : base + size, lane : lane + chunk]
        value = jnp.where(picks[offset], value, 0.0)
        value = jnp.sum(value, axis=0, keepdims=True)
        for q in range(per):
            put(f, c * per + q, value[:, q * LANES : (q + 1) * LANES])


def gather_kernel(
    count_hbm,
    cell_hbm,
    field_hbm,
    out_hbm,
    high_ref,
    low_ref,
    cell_ref,
    field_ref,
    out_ref,
    place_ref,
    hot_ref,
    found_ref,
    list_ref,
    count_ref,
    count_sem,
    cell_sem,
    field_sem,
    out_sem,
    *,
    chunk,
    group,
    sizes,
):
    fields, cells_j, cells_i = sizes
    owners, capacity = cell_ref.shape
    rows = cells_j * cells_i
    slot_rows = capacity // LANES
    steps = capacity // chunk
    loads = [
        pltpu.make_async_copy(
            field_hbm.at[pl.ds(f * rows, rows)], field_ref.at[pl.ds(f * rows, rows)], field_sem.at[f]
        )
        for f in range(fields)
    ]
    cell_load = pltpu.make_async_copy(cell_hbm, cell_ref, cell_sem)
    count_load = pltpu.make_async_copy(count_hbm, count_ref, count_sem)
    count_load.start()
    cell_load.start()
    for load in loads:
        load.start()
    mine = lax.axis_index("block")

    def send(d):
        part = out_ref.at[d, pl.ds(0, out_hbm.shape[1])]
        return pltpu.make_async_copy(part, out_hbm.at[d], out_sem.at[d])

    out_ref[...] = jnp.zeros(out_ref.shape, F32)
    send(mine).start()
    place_ref[...] = places(2 * LANES, LANES)

    count_load.wait()

    def list_owner(d, total):
        live = jnp.maximum(lax.div(count_ref[d] + (chunk - 1), chunk), 1)
        live = jnp.where(d == mine, 0, live)

        def list_chunk(c, at):
            list_ref[at] = d * steps + c
            return at + 1

        return lax.fori_loop(0, live, list_chunk, total)

    total = lax.fori_loop(0, owners, list_owner, 0)
    groups = lax.div(total + (group - 1), group)

    def place_of(n):
        entry = list_ref[jnp.minimum(n, total - 1)]
        return lax.div(entry, steps), lax.rem(entry, steps)

    def build(n):
        for g in range(group):
            d, c = place_of(n * group + g)
            build_hot(hot_ref, g * chunk, cell_ref, place_ref[...], d, c, chunk, sizes)

    cell_load.wait()
    build(0)
    for load in loads:
        load.wait()
    for parity in range(2):
        part = field_ref[pl.ds(parity, fields * rows // 2, stride=2), :]
        high, low = split(part)
        high_ref[:, parity * LANES : (parity + 1) * LANES] = high
        low_ref[:, parity * LANES : (parity + 1) * LANES] = low

    def pick(n):
        for g in range(group):
            d, c = place_of(n * group + g)

            def put(f, row, value, d=d):
                out_ref[d, pl.ds(f * slot_rows + row, 1), :] = value

            pick_rows(
                found_ref, g * chunk, cell_ref, d, c, count_ref[d], chunk, sizes, put
            )

    def body(n, carry):
        done = jnp.maximum(n - 1, 0)
        pick(done)
        hot = hot_ref[...]
        found_ref[...] = dot_nn(high_ref[...], hot) + dot_nn(low_ref[...], hot)
        build(n + 1)
        for g in range(group):
            here, _ = place_of(done * group + g)
            following, _ = place_of(done * group + g + 1)

            @pl.when((n > 0) & (here != following))
            def _(here=here):
                send(here).start()

        return carry

    lax.fori_loop(0, groups, body, 0)
    pick(groups - 1)
    for g in range(group):
        here, _ = place_of((groups - 1) * group + g)
        following, _ = place_of((groups - 1) * group + g + 1)

        @pl.when(here != following)
        def _(here=here):
            send(here).start()

    last, _ = place_of(total - 1)
    send(last).start()

    def wait_body(d, carry):
        send(d).wait()
        return carry

    lax.fori_loop(0, owners, wait_body, 0)


def gather(count, cell, field, chunk=256, group=6):
    fields, cells_j, cells_i, _ = field.shape
    owners, capacity = cell.shape
    field = field.reshape(-1, LANES)
    table = (field.shape[0] // 2, 2 * LANES)
    out = (owners, fields * capacity // LANES, LANES)
    vmem = pl.BlockSpec(memory_space=pltpu.VMEM)
    hbm = pl.BlockSpec(memory_space=pltpu.HBM)
    return pl.pallas_call(
        functools.partial(
            gather_kernel, chunk=chunk, group=group, sizes=(fields, cells_j, cells_i)
        ),
        out_shape=(
            jax.ShapeDtypeStruct(out, F32),
            pltpu.VMEM(table, BF16),
            pltpu.VMEM(table, BF16),
        ),
        in_specs=[hbm, hbm, hbm],
        out_specs=(hbm, vmem, vmem),
        scratch_shapes=[
            pltpu.VMEM(cell.shape, jnp.int32),
            pltpu.VMEM(field.shape, F32),
            pltpu.VMEM((out[0], out[1] + 8, LANES), F32),
            pltpu.VMEM((2 * LANES, LANES), BF16),
            pltpu.VMEM((2 * LANES, group * chunk), BF16),
            pltpu.VMEM((table[0], group * chunk), F32),
            pltpu.SMEM((owners * capacity // chunk,), jnp.int32),
            pltpu.SMEM((owners,), jnp.int32),
            pltpu.SemaphoreType.DMA(()),
            pltpu.SemaphoreType.DMA(()),
            pltpu.SemaphoreType.DMA((fields,)),
            pltpu.SemaphoreType.DMA((owners,)),
        ],
        compiler_params=PARAMS,
        name="gather",
    )(far(count), far(cell), far(field))


def lay_out(entries):
    lane = lax.broadcasted_iota(jnp.int32, (8, LANES), 1)
    tile = jnp.zeros((8, LANES), F32)
    for at, entry in enumerate(entries):
        tile = jnp.where(lane == at, entry, tile)
    return tile


def edge_entries(couple_ref, direction):
    row = lax.broadcasted_iota(jnp.int32, (8, LANES), 0)
    table = []
    for c in range(3):
        value = jnp.zeros((8, LANES), F32)
        for f in range(couple_ref.shape[2]):
            value = jnp.where(row == f, couple_ref[c, direction, f], value)
        table.append(value)
    return table


def prepare_i_kernel(couple_ref, i_ref, i_out, *, cells_i):
    lower, upper = i_ref[0], i_ref[1]

    def edges(matrix, direction):
        e0, e1, e2 = edge_entries(couple_ref, direction)
        table = []
        for p in range(cells_i):
            first, second = col(matrix, p * cells_i), col(matrix, p * cells_i + 1)
            table.append((first * e0 + second * e2, first * e1))
        return table

    low_edge = edges(lower, 0)
    up_edge = edges(upper, 1)
    through = []
    for p in range(cells_i):
        total = [jnp.zeros((8, LANES), F32), jnp.zeros((8, LANES), F32)]
        for q in range(p + 1):
            factor = col(upper, p * cells_i + q)
            for a in range(2):
                total[a] = total[a] + factor * low_edge[cells_i - 1 - q][a]
        through.append(total)
    last, prior = cells_i - 1, cells_i - 2
    entries = []
    for table in (through, up_edge):
        for p in range(cells_i):
            entries += [table[p][0], table[p][1]]
    entries += [-low_edge[last][0], -low_edge[last][1], -low_edge[prior][0], -low_edge[prior][1]]
    entries += [-up_edge[last][0], -up_edge[last][1], -up_edge[prior][0], -up_edge[prior][1]]
    entries += [through[last][0], through[last][1], through[prior][0], through[prior][1]]
    i_out[...] = lay_out(entries)


def prepare_i(couplings, i_tiles, cells_i):
    return pl.pallas_call(
        functools.partial(prepare_i_kernel, cells_i=cells_i),
        out_shape=pltpu.VMEM((8, LANES), F32),
        in_specs=[
            pl.BlockSpec(memory_space=pltpu.SMEM),
            pl.BlockSpec(memory_space=pltpu.VMEM),
        ],
        out_specs=pl.BlockSpec(memory_space=pltpu.VMEM),
        compiler_params=PARAMS,
        name="prepare_i",
    )(couplings, near(i_tiles))


def prepare_k_kernel(couple_ref, k_ref, k_tile, k_map, k_rows, k_carry):
    fields, length = k_ref.shape[1], k_ref.shape[2]
    row_n = lax.broadcasted_iota(jnp.int32, (length, length), 0)
    lane_n = lax.broadcasted_iota(jnp.int32, (length, length), 1)
    turn = jnp.where(row_n + lane_n == length - 1, 1.0, 0.0).astype(BF16)
    columns = jnp.zeros((length, length), F32)
    for f in range(fields):
        low, up = k_ref[0, f], k_ref[1, f]
        whole = product_nn(up, turn_rows(low, turn))
        k_map[f] = whole
        k_rows[f] = jnp.concatenate(
            [x[length - q : length - q + 1] for x in (low, whole) for q in (1, 2)]
            + [jnp.zeros((4, length), F32)],
            axis=0,
        )
        for m, matrix in enumerate((low, up, whole)):
            for q in range(2):
                value = jnp.broadcast_to(matrix[:, q : q + 1], (length, length))
                columns = jnp.where(lane_n == 16 * m + 8 * q + f, value, columns)
    columns = columns.T
    low0, low1, up0, up1, all0, all1 = (columns[8 * q : 8 * q + 8] for q in range(6))

    e0, e1, e2 = edge_entries(couple_ref, 2)
    d0, d1, d2 = edge_entries(couple_ref, 3)
    first = (low0 * e0 + low1 * e2, low0 * e1)
    through = (all0 * e0 + all1 * e2, all0 * e1)
    second = (up0 * d0 + up1 * d2, up0 * d1)
    turned = turn_lanes(jnp.concatenate(through + second, axis=0), turn)
    for a in range(4):
        k_carry[a] = turned[8 * a : 8 * a + 8]
    ends = [(pair, p) for p in (length - 1, length - 2) for pair in (0, 1)]
    k_tile[...] = lay_out(
        [-col(first[pair], p) for pair, p in ends]
        + [-col(second[pair], p) for pair, p in ends]
        + [col(through[pair], p) for pair, p in ends]
    )


def prepare_k(couplings, k_factors):
    fields, length = k_factors.shape[1], k_factors.shape[2]
    return pl.pallas_call(
        prepare_k_kernel,
        out_shape=(
            pltpu.VMEM((8, LANES), F32),
            pltpu.VMEM((fields, length, length), F32),
            pltpu.VMEM((fields, 8, length), F32),
            pltpu.VMEM((4, 8, length), F32),
        ),
        in_specs=[
            pl.BlockSpec(memory_space=pltpu.SMEM),
            pl.BlockSpec(memory_space=pltpu.VMEM),
        ],
        out_specs=(pl.BlockSpec(memory_space=pltpu.VMEM),) * 4,
        compiler_params=PARAMS,
        name="prepare_k",
    )(couplings, near(k_factors))


def mat2(a, b):
    return [
        a[0] * b[0] + a[1] * b[2],
        a[0] * b[1] + a[1] * b[3],
        a[2] * b[0] + a[3] * b[2],
        a[2] * b[1] + a[3] * b[3],
    ]


def downstream_map(tiles, base, mine):
    peers = len(tiles)
    total = [jnp.zeros((8, LANES), F32)] * 4
    for m in range(1, peers):
        entry = [col(tiles[m], base + c) for c in range(12)]
        step = mat2(mat2(entry[4:8], total), entry[0:4])
        total = [
            jnp.where(m > mine, new - back, old) for new, back, old in zip(step, entry[8:12], total)
        ]
    return total


def spread_slots(total_ref, place_ref, value_of, cell_ref, weight_ref, units, sizes, size):
    fields, cells_j, cells_i = sizes
    rows_j = 16
    chunk = size * len(units)
    per = chunk // LANES

    def joined(pick):
        return jnp.concatenate([pick(pl.ds(b, 1), pl.ds(at, size)) for b, at in units], axis=1)

    cell = joined(lambda b, at: cell_ref[b, at])
    x, y, z = (joined(lambda b, at, axis=axis: weight_ref[axis, b, at]) for axis in range(3))
    i, j, k = split_cell(cell, cells_i, cells_j)

    def hat(size, at, t):
        place = lax.broadcasted_iota(jnp.int32, (size, chunk), 0)
        return jnp.where(place == at, 1.0 - t, jnp.where(place == at + 1, t, 0.0))

    along_i = hat(cells_i, i, x)
    along_j = hat(rows_j, j, y)
    first = rows_of(k.astype(F32), 16, BF16)
    second = rows_of((k + 1).astype(F32), 16, BF16)
    remote = split(rows_of(z, 16, F32))
    close = split(rows_of(1.0 - z, 16, F32))
    zero = jnp.zeros((16, chunk), BF16)
    place = place_ref[:LANES]
    along_k = []
    for part in range(2):
        for r in range(LANES // 16):
            here = jnp.concatenate([place[16 * r : 16 * r + 16]] * per, axis=1)
            weight = jnp.where(here == second, remote[part], zero)
            along_k.append(jnp.where(here == first, close[part], weight))
    along_k = jnp.concatenate(along_k, axis=0)
    blocks = []
    for f in range(fields):
        rows = []
        for b, at in units:
            for q in range(0, size // LANES, 8):
                block = value_of(f, b, lax.div(at, LANES) + q)
                rows += [block[r : r + 1] for r in range(8)]
        value = jnp.concatenate(rows, axis=1)
        scaled = along_j * value
        blocks += [along_i * scaled[q : q + 1] for q in range(cells_j)]
    high, low = split(jnp.concatenate(blocks, axis=0))
    total_ref[...] += dot_nt(
        jnp.concatenate([high, low], axis=1), jnp.concatenate([along_k, along_k], axis=1)
    )


def scatter_own_kernel(
    count_ref,
    high_ref,
    low_ref,
    from_ref,
    cell_ref,
    weight_ref,
    total_ref,
    got_ref,
    place_ref,
    hot_ref,
    found_ref,
    *,
    sizes,
    gather_chunk,
):
    capacity = cell_ref.shape[1]
    slot_rows = capacity // LANES
    total_ref[...] = jnp.zeros(total_ref.shape, F32)
    got_ref[...] = jnp.zeros(got_ref.shape, F32)
    place_ref[...] = places(2 * LANES, LANES)
    mine = lax.axis_index("block")
    count = count_ref[mine]

    def put(f, row, value):
        got_ref[pl.ds(f * slot_rows + row, 1), :] = value

    def find_body(c, carry):
        build_hot(hot_ref, 0, from_ref, place_ref[...], mine, c, gather_chunk, sizes)
        hot = hot_ref[...]
        found_ref[...] = dot_nn(high_ref[...], hot) + dot_nn(low_ref[...], hot)
        pick_rows(found_ref, 0, from_ref, mine, c, count, gather_chunk, sizes, put)
        return carry

    lax.fori_loop(0, lax.div(count + (gather_chunk - 1), gather_chunk), find_body, 0)

    spread_slots(
        total_ref,
        place_ref,
        lambda f, b, q: got_ref[pl.ds(pl.multiple_of(f * slot_rows + q, 8), 8), :],
        cell_ref,
        weight_ref,
        [(mine, 0)],
        sizes,
        capacity,
    )


def scatter_own(count, tables, receptor, cell, weight, sizes, gather_chunk=512):
    vmem = pl.BlockSpec(memory_space=pltpu.VMEM)
    smem = pl.BlockSpec(memory_space=pltpu.SMEM)
    fields, cells_j, cells_i = sizes
    return pl.pallas_call(
        functools.partial(scatter_own_kernel, sizes=sizes, gather_chunk=gather_chunk),
        out_shape=pltpu.VMEM((fields * cells_i * cells_j, 2 * LANES), F32),
        in_specs=[smem] + [vmem] * 5,
        out_specs=vmem,
        scratch_shapes=[
            pltpu.VMEM((fields * cell.shape[1] // LANES + 8, LANES), F32),
            pltpu.VMEM((2 * LANES, LANES), BF16),
            pltpu.VMEM((2 * LANES, gather_chunk), BF16),
            pltpu.VMEM((tables[0].shape[0], gather_chunk), F32),
        ],
        compiler_params=PARAMS,
        name="scatter_own",
    )(far(count), *map(near, (*tables, receptor, cell, weight)))


def scatter_kernel(*refs, peers, chunk, base, sizes):
    factor_ref, begun_ref, got_ref, cell_ref, weight_ref, residual_ref = refs[:6]
    refs = refs[6:]
    tile_refs = refs[:peers]
    start_ref = refs[peers]
    send_refs = refs[1 + peers : 1 + 2 * peers]
    total_ref, place_ref, fold_ref, solve_ref, solve_sem = refs[1 + 2 * peers :]
    fields, cells_j, cells_i = sizes
    sources, capacity = cell_ref.shape
    rows_j = 16
    slot_rows = capacity // LANES
    solve_load = pltpu.make_async_copy(factor_ref, solve_ref, solve_sem)
    solve_load.start()
    total_ref[...] = begun_ref[...]
    place_ref[...] = places(LANES, LANES)
    own = lax.axis_index("block")

    parts = capacity // chunk
    count = (sources - 1) * parts
    group = max(g for g in range(1, 8) if count % g == 0)

    def step_body(step, carry):
        units = []
        for g in range(group):
            unit = step * group + g
            b = lax.div(unit, parts)
            b = b + (b >= own).astype(jnp.int32)
            units.append((b, pl.multiple_of(lax.rem(unit, parts) * chunk, chunk)))
        spread_slots(
            total_ref,
            place_ref,
            lambda f, b, q: got_ref[b, pl.ds(pl.multiple_of(f * slot_rows + q, 8), 8), :],
            cell_ref,
            weight_ref,
            units,
            (fields, cells_j, cells_i),
            chunk,
        )
        return carry

    lax.fori_loop(0, count // group, step_body, 0)

    count = fields * cells_j * cells_i
    fold_ref[:count] = total_ref[:, :LANES] + total_ref[:, LANES:] + residual_ref[...]
    solve_load.wait()
    mine = lax.axis_index("line")
    tiles = [ref[...] for ref in tile_refs]
    onward = downstream_map(tiles, base, mine)
    turned = mat2([col(tiles[0], base + 4 + c) for c in range(4)], onward)
    pad = jnp.zeros((rows_j - cells_j, LANES), F32)
    for f in range(fields):
        data = []
        for i in range(cells_i):
            at = pl.ds(f * cells_i * cells_j + i, cells_j, stride=cells_i)
            data.append(jnp.concatenate([fold_ref[at, :], pad], axis=0))

        def solve(direction, columns):
            result = []
            for p in range(cells_i):
                value = solve_ref[direction, f, p * cells_i] * columns[0]
                for q in range(1, p + 1):
                    value = value + solve_ref[direction, f, p * cells_i + q] * columns[q]
                result.append(value)
            return result

        first = solve(0, data)
        second = solve(1, first[::-1])
        e0, e1 = first[-1], first[-2]
        g0, g1 = second[-1], second[-2]
        m = [jnp.broadcast_to(entry[f : f + 1], (rows_j, LANES)) for entry in turned]
        h0 = g0 + m[0] * e0 + m[1] * e1
        h1 = g1 + m[2] * e0 + m[3] * e1
        for i in range(cells_i):
            at = (f * cells_i + i) * rows_j
            start_ref[at : at + rows_j] = second[cells_i - 1 - i]
        for shift in range(peers):
            ahead = mine + shift < peers
            at = f * rows_j
            send_refs[shift][at : at + rows_j] = jnp.where(ahead, e0, h0)
            at = (fields + f) * rows_j
            send_refs[shift][at : at + rows_j] = jnp.where(ahead, e1, h1)


def scatter(solve_tiles, begun, got, cell, weight, residual, tiles, base, chunk=1024):
    fields, cells_j, cells_i, _ = residual.shape
    peers = len(tiles)
    rows = fields * cells_i * 16
    vmem = pl.BlockSpec(memory_space=pltpu.VMEM)
    smem = pl.BlockSpec(memory_space=pltpu.SMEM)
    return pl.pallas_call(
        functools.partial(
            scatter_kernel,
            peers=peers,
            chunk=chunk,
            base=base,
            sizes=(fields, cells_j, cells_i),
        ),
        out_shape=(pltpu.VMEM((rows, LANES), F32),)
        + (pltpu.VMEM((2 * fields * 16, LANES), F32),) * peers,
        in_specs=[vmem] * (6 + peers),
        out_specs=(vmem,) * (1 + peers),
        scratch_shapes=[
            pltpu.VMEM((fields * cells_i * cells_j, 2 * LANES), F32),
            pltpu.VMEM((LANES, LANES), BF16),
            pltpu.VMEM((fields * cells_i * cells_j + 8 * cells_i, LANES), F32),
            pltpu.SMEM(solve_tiles.shape, F32),
            pltpu.SemaphoreType.DMA(()),
        ],
        compiler_params=PARAMS,
        name="scatter",
    )(*map(near, (solve_tiles, begun, got, cell, weight, residual.reshape(-1, LANES), *tiles)))


def middle_kernel(*refs, peers, base, fields, cells_i):
    start_ref, rows_ref, k_tile_ref = refs[:3]
    tile_refs = refs[3 : 3 + peers]
    got_refs = refs[3 + peers : 3 + 2 * peers]
    field_ref, send_hbm, end_ref, own_ref, own_sem, send_sem = refs[3 + 2 * peers :]
    own_load = pltpu.make_async_copy(tile_refs[0], own_ref, own_sem)
    own_load.start()
    rows_j = 16
    mine = lax.axis_index("line")
    tiles = [ref[...] for ref in tile_refs]
    onward = downstream_map(tiles, base, mine)
    forward = [[col(tile, base + c) for c in range(4)] for tile in tiles]
    backward = [[col(tile, base + 4 + c) for c in range(4)] for tile in tiles]
    end_ref[...] = jnp.zeros(end_ref.shape, F32)
    rows = cells_i * rows_j
    own_load.wait()
    for f in range(fields):

        def wide(entry):
            return jnp.broadcast_to(entry[f : f + 1], (rows_j, LANES))

        def advance(matrix, state, add):
            m = [wide(entry) for entry in matrix]
            return [
                m[0] * state[0] + m[1] * state[1] + add[0],
                m[2] * state[0] + m[3] * state[1] + add[1],
            ]

        got = []
        for shift in range(peers):
            low = got_refs[shift][f * rows_j : (f + 1) * rows_j]
            high = got_refs[shift][(fields + f) * rows_j : (fields + f + 1) * rows_j]
            got.append((low, high))
        zero = jnp.zeros((rows_j, LANES), F32)
        before = [zero, zero]
        for shift in range(peers - 1, 0, -1):
            new = advance(forward[shift], before, got[shift])
            before = [jnp.where(shift <= mine, n, o) for n, o in zip(new, before)]
        after = [zero, zero]
        for shift in range(1, peers):
            new = advance(backward[shift], after, got[shift])
            after = [jnp.where(shift > mine, n, o) for n, o in zip(new, after)]
        onto = advance(forward[0], before, got[0])
        after = advance(onward, onto, after)
        for p in range(cells_i):
            at = (f * cells_i + cells_i - 1 - p) * rows_j
            value = start_ref[at : at + rows_j]
            value = value - own_ref[f, 2 * p] * before[0] - own_ref[f, 2 * p + 1] * before[1]
            shift = 2 * cells_i
            value = value - own_ref[f, shift + 2 * p] * after[0]
            value = value - own_ref[f, shift + 2 * p + 1] * after[1]
            field_ref[at : at + rows_j] = value
        block = field_ref[f * rows : (f + 1) * rows]
        r_high, r_low = split(rows_ref[f])
        both = dot_nt(
            jnp.concatenate([r_high, r_low], axis=0), jnp.concatenate(split(block), axis=0)
        )
        ends = both[:8, :rows] + both[:8, rows:] + both[8:, :rows]
        for a in range(4):
            end_ref[a * fields + f : a * fields + f + 1, :] = ends[a : a + 1]
    lane = lax.broadcasted_iota(jnp.int32, (fields, LANES), 1)
    for a in range(4):
        part = end_ref[a * fields : (a + 1) * fields]
        for q in range(3):
            entry = col(k_tile_ref[0:fields], 3 * a + q)
            part = jnp.where(lane == rows_j * q + rows_j - 1, entry, part)
        end_ref[a * fields : (a + 1) * fields] = part
    sends = [
        pltpu.make_async_copy(
            end_ref.at[pl.ds(0, 4 * fields)], send_hbm.at[d], send_sem.at[d]
        )
        for d in range(send_hbm.shape[0])
    ]
    for copy in sends:
        copy.start()
    for copy in sends:
        copy.wait()


def middle(start, k_rows, k_tile, tiles, got, base, owners, fields, cells_i):
    peers = len(tiles)
    vmem = pl.BlockSpec(memory_space=pltpu.VMEM)
    smem = pl.BlockSpec(memory_space=pltpu.SMEM)
    return pl.pallas_call(
        functools.partial(middle_kernel, peers=peers, base=base, fields=fields, cells_i=cells_i),
        out_shape=(
            pltpu.VMEM(start.shape, F32),
            jax.ShapeDtypeStruct((owners, 4 * fields, LANES), F32),
        ),
        in_specs=[vmem] * (3 + 2 * peers),
        out_specs=(vmem, pl.BlockSpec(memory_space=pltpu.HBM)),
        scratch_shapes=[
            pltpu.VMEM((4 * fields + 8, LANES), F32),
            pltpu.SMEM((8, LANES), F32),
            pltpu.SemaphoreType.DMA(()),
            pltpu.SemaphoreType.DMA((owners,)),
        ],
        compiler_params=PARAMS,
        name="middle",
    )(*map(near, (start, k_rows, k_tile, *tiles, *got)))


def apply_k_kernel(field_ref, map_ref, out_ref):
    fields = map_ref.shape[0]
    rows = field_ref.shape[0] // fields
    length = map_ref.shape[1]
    row_n = lax.broadcasted_iota(jnp.int32, (length, length), 0)
    lane_n = lax.broadcasted_iota(jnp.int32, (length, length), 1)
    turn = jnp.where(row_n + lane_n == length - 1, 1.0, 0.0).astype(BF16)
    for f in range(fields):
        at = slice(f * rows, (f + 1) * rows)
        out_ref[at] = turn_lanes(product_nt(field_ref[at], map_ref[f]), turn)


def apply_k(field, k_map):
    vmem = pl.BlockSpec(memory_space=pltpu.VMEM)
    return pl.pallas_call(
        apply_k_kernel,
        out_shape=pltpu.VMEM(field.shape, F32),
        in_specs=[vmem, vmem],
        out_specs=vmem,
        compiler_params=PARAMS,
        name="apply_k",
    )(near(field), near(k_map))


def finish_kernel(start_ref, got_ref, carry_ref, out_hbm, out_ref, out_sem):
    fields, cells_j, cells_i, _ = out_hbm.shape
    rows_j = 16
    rows = cells_i * rows_j
    blocks = got_ref.shape[0]

    def send(f):
        part = out_ref.at[f, pl.ds(0, cells_j)]
        return pltpu.make_async_copy(part, out_hbm.at[f], out_sem.at[f])

    mine = lax.axis_index("block")
    zero = jnp.zeros((fields, LANES), F32)
    part = [
        [got_ref[m, fields * a : fields * (a + 1)] for a in range(4)] for m in range(blocks)
    ]
    entry = [
        [col(part[m][c // 3], rows_j * (c % 3) + rows_j - 1) for c in range(12)]
        for m in range(blocks)
    ]
    states = []
    state = [zero, zero]
    for m in range(blocks):
        states.append(state)
        p = entry[m]
        state = [
            p[0] * state[0] + p[1] * state[1] + part[m][0],
            p[2] * state[0] + p[3] * state[1] + part[m][1],
        ]
    before = [zero, zero]
    after = [zero, zero]
    state = [zero, zero]
    for m in range(blocks - 1, -1, -1):
        here = m == mine
        before = [jnp.where(here, n, o) for n, o in zip(states[m], before)]
        after = [jnp.where(here, n, o) for n, o in zip(state, after)]
        q, b = entry[m][4:8], entry[m][8:12]
        old = states[m]
        state = [
            q[0] * state[0] + q[1] * state[1] + part[m][2] - b[0] * old[0] - b[1] * old[1],
            q[2] * state[0] + q[3] * state[1] + part[m][3] - b[2] * old[0] - b[3] * old[1],
        ]
    for f in range(fields):
        carried = jnp.concatenate(
            [x[f : f + 1] for x in (before[0], before[1], after[0], after[1])]
            + [jnp.zeros((4, LANES), F32)],
            axis=0,
        )
        response = jnp.concatenate(
            [carry_ref[a, f : f + 1, :] for a in range(4)] + [jnp.zeros((4, LANES), F32)], axis=0
        )
        change = dot3(dot_tn, carried, response, 0, 0)
        value = start_ref[f * rows : (f + 1) * rows] - change
        for i in range(cells_i):
            out_ref[f, :, i, :] = value[i * rows_j : (i + 1) * rows_j]
        send(f).start()
    for f in range(fields):
        send(f).wait()


def finish(start, got, carry, shape):
    vmem = pl.BlockSpec(memory_space=pltpu.VMEM)
    smem = pl.BlockSpec(memory_space=pltpu.SMEM)
    return pl.pallas_call(
        finish_kernel,
        out_shape=jax.ShapeDtypeStruct(shape, F32),
        in_specs=[vmem, vmem, vmem],
        out_specs=pl.BlockSpec(memory_space=pltpu.HBM),
        scratch_shapes=[
            pltpu.VMEM((shape[0], 16) + shape[2:], F32),
            pltpu.SemaphoreType.DMA((shape[0],)),
        ],
        compiler_params=PARAMS,
        name="finish",
    )(near(start), near(got), near(carry))


def per_device(
    residual,
    adjoint,
    i_factors,
    k_factors,
    couplings,
    receptor_cell,
    send_count,
    donor_cell,
    donor_weight,
):
    fields, cells_i, cells_j, cells_k = adjoint.shape
    owners = receptor_cell.shape[2]
    peers = lax.axis_size("line")
    base = 4 * cells_i

    adjoint, residual = (x.transpose(0, 2, 1, 3) for x in (adjoint, residual))
    counts = send_count.reshape(owners)
    outgoing, *tables = gather(counts, receptor_cell[0, 0], adjoint)
    incoming = lax.all_to_all(outgoing, "block", split_axis=0, concat_axis=0, tiled=True)

    square = i_factors[0].reshape(2, fields, cells_i * cells_i)
    i_tiles = jnp.pad(square, ((0, 0), (0, 8 - fields), (0, LANES - cells_i * cells_i)))
    couple = couplings[0, 0].transpose(1, 0, 2)
    own = prepare_i(couple, i_tiles, cells_i)

    def shifted(value, shift):
        return lax.ppermute(value, "line", [(s, (s + shift) % peers) for s in range(peers)])

    tiles = [own] + [shifted(own, m) for m in range(1, peers)]
    begun = scatter_own(
        counts,
        tables,
        receptor_cell[0, 0],
        donor_cell[0, 0],
        donor_weight[0, 0],
        (fields, cells_j, cells_i),
    )
    start, *ends = scatter(
        i_tiles,
        begun,
        incoming,
        donor_cell[0, 0],
        donor_weight[0, 0],
        residual,
        tiles,
        base,
    )
    got = [ends[0]] + [shifted(ends[m], m) for m in range(1, peers)]
    couple, _ = lax.optimization_barrier((couple, ends[0]))
    k_tile, k_map, k_rows, k_carry = prepare_k(couple, k_factors[0])
    start, message = middle(
        start, k_rows, k_tile, tiles, got, base, owners, fields, cells_i
    )
    message = lax.all_to_all(message, "block", split_axis=0, concat_axis=0, tiled=True)
    start = apply_k(start, k_map)
    return finish(start, message, k_carry, residual.shape).transpose(0, 2, 1, 3)


def solution(mesh):
    return jax.shard_map(
        per_device,
        mesh=mesh,
        in_specs=(
            P(None, "line", None, "block"),
            P(None, "line", None, "block"),
            P("block", None, None, "line", None),
            P("line", None, None, "block", None),
            P("line", "block", None, None, None),
            P("line", "block", None, None),
            P("line", "block", None),
            P("line", "block", None, None),
            P("line", "block", None, None, None),
        ),
        out_specs=P(None, "line", None, "block"),
        check_vma=False,
    )
```

```python
import functools

import jax
import jax.numpy as jnp
from jax import lax
from jax.experimental import pallas as pl
from jax.experimental.pallas import tpu as pltpu
from jax.sharding import PartitionSpec as P

LANES = 128
F32 = jnp.float32
BF16 = jnp.bfloat16
PARAMS = pltpu.CompilerParams(vmem_limit_bytes=32 * 1024 * 1024)


def split(x):
    high = x.astype(BF16)
    return high, (x - high.astype(F32)).astype(BF16)


def dot_nt(a, b, precision=None):
    return lax.dot_general(
        a, b, (((1,), (1,)), ((), ())), precision=precision, preferred_element_type=F32
    )


def dot_nn(a, b, precision=None):
    return lax.dot_general(
        a, b, (((1,), (0,)), ((), ())), precision=precision, preferred_element_type=F32
    )


def dot_tn(a, b, precision=None):
    return lax.dot_general(
        a, b, (((0,), (0,)), ((), ())), precision=precision, preferred_element_type=F32
    )


def dot3(dot, a, b, axis_a, axis_b):
    a_high, a_low = split(a)
    b_high, b_low = split(b)
    left = jnp.concatenate([a_high, a_high, a_low], axis=axis_a)
    right = jnp.concatenate([b_high, b_low, b_high], axis=axis_b)
    return dot(left, right)


def product_nt(a, b):
    return dot3(dot_nt, a, b, 1, 1)


def product_nn(a, b):
    return dot3(dot_nn, a, b, 1, 0)


def turn_lanes(x, turn):
    return dot_nn(jnp.concatenate(split(x), axis=1), jnp.concatenate([turn, turn], axis=0))


def turn_rows(x, turn):
    return dot_nn(jnp.concatenate([turn, turn], axis=1), jnp.concatenate(split(x), axis=0))


def rows_of(value, count, dtype):
    return jnp.broadcast_to(value, (count, value.shape[1])).astype(dtype)


def places(size, width):
    place = lax.broadcasted_iota(jnp.int32, (size, width), 0)
    return place.astype(F32).astype(BF16)


def split_cell(cell, cells_i, cells_j):
    row = lax.shift_right_logical(cell, 7)
    k = lax.bitwise_and(cell, LANES - 1)
    i = jnp.zeros_like(row)
    for m in range(1, cells_i):
        i = i + (row >= m * cells_j).astype(jnp.int32)
    return i, row - i * cells_j, k


def near(x):
    return pltpu.with_memory_space_constraint(x, pltpu.VMEM)


def far(x):
    return pltpu.with_memory_space_constraint(x, pltpu.HBM)


def col(x, c):
    return jnp.broadcast_to(x[:, c : c + 1], x.shape)


def build_hot(hot_ref, lane, cell_ref, place, d, c, chunk, sizes):
    _, cells_j, cells_i = sizes
    start = pl.multiple_of(c * chunk, chunk)
    cell = cell_ref[pl.ds(d, 1), pl.ds(start, chunk)]
    i, _, k = split_cell(cell, cells_i, cells_j)
    column = (lax.bitwise_and(i, 1) * LANES + k).astype(F32)
    column = rows_of(column, 16, BF16)
    for r in range(2 * LANES // 16):
        here = jnp.concatenate([place[16 * r : 16 * r + 16]] * (chunk // LANES), axis=1)
        hot_ref[16 * r : 16 * r + 16, lane : lane + chunk] = jnp.where(
            here == column, jnp.asarray(1, BF16), jnp.asarray(0, BF16)
        )


def pick_rows(found_ref, lane, cell_ref, d, c, count, chunk, sizes, put):
    fields, cells_j, cells_i = sizes
    half_i = cells_i // 2
    rows = half_i * cells_j
    per = chunk // LANES
    start = pl.multiple_of(c * chunk, chunk)
    cell = cell_ref[pl.ds(d, 1), pl.ds(start, chunk)]
    i, j, _ = split_cell(cell, cells_i, cells_j)
    slot = start + lax.broadcasted_iota(jnp.int32, cell.shape, 1)
    row = j * half_i + lax.shift_right_logical(i, 1)
    row = jnp.where(slot < count, row, -8)
    picks = {}
    for f in range(fields):
        base = f * rows // 8 * 8
        offset = f * rows - base
        size = -(-(offset + rows) // 8) * 8
        if offset not in picks:
            place = lax.broadcasted_iota(jnp.int32, (size, chunk), 0)
            picks[offset] = place == row + offset
        value = found_ref[base : base + size, lane : lane + chunk]
        value = jnp.where(picks[offset], value, 0.0)
        value = jnp.sum(value, axis=0, keepdims=True)
        for q in range(per):
            put(f, c * per + q, value[:, q * LANES : (q + 1) * LANES])


def gather_kernel(
    count_hbm,
    cell_hbm,
    field_hbm,
    out_hbm,
    high_ref,
    low_ref,
    cell_ref,
    field_ref,
    out_ref,
    place_ref,
    hot_ref,
    found_ref,
    list_ref,
    count_ref,
    count_sem,
    cell_sem,
    field_sem,
    out_sem,
    *,
    chunk,
    group,
    sizes,
):
    fields, cells_j, cells_i = sizes
    owners, capacity = cell_ref.shape
    rows = cells_j * cells_i
    slot_rows = capacity // LANES
    steps = capacity // chunk
    loads = [
        pltpu.make_async_copy(
            field_hbm.at[pl.ds(f * rows, rows)], field_ref.at[pl.ds(f * rows, rows)], field_sem.at[f]
        )
        for f in range(fields)
    ]
    cell_load = pltpu.make_async_copy(cell_hbm, cell_ref, cell_sem)
    count_load = pltpu.make_async_copy(count_hbm, count_ref, count_sem)
    count_load.start()
    cell_load.start()
    for load in loads:
        load.start()
    mine = lax.axis_index("block")

    def send(d):
        part = out_ref.at[d, pl.ds(0, out_hbm.shape[1])]
        return pltpu.make_async_copy(part, out_hbm.at[d], out_sem.at[d])

    out_ref[...] = jnp.zeros(out_ref.shape, F32)
    send(mine).start()
    place_ref[...] = places(2 * LANES, LANES)

    count_load.wait()

    def list_owner(d, total):
        live = jnp.maximum(lax.div(count_ref[d] + (chunk - 1), chunk), 1)
        live = jnp.where(d == mine, 0, live)

        def list_chunk(c, at):
            list_ref[at] = d * steps + c
            return at + 1

        return lax.fori_loop(0, live, list_chunk, total)

    total = lax.fori_loop(0, owners, list_owner, 0)
    groups = lax.div(total + (group - 1), group)

    def place_of(n):
        entry = list_ref[jnp.minimum(n, total - 1)]
        return lax.div(entry, steps), lax.rem(entry, steps)

    def build(n):
        for g in range(group):
            d, c = place_of(n * group + g)
            build_hot(hot_ref, g * chunk, cell_ref, place_ref[...], d, c, chunk, sizes)

    cell_load.wait()
    build(0)
    for load in loads:
        load.wait()
    for parity in range(2):
        part = field_ref[pl.ds(parity, fields * rows // 2, stride=2), :]
        high, low = split(part)
        high_ref[:, parity * LANES : (parity + 1) * LANES] = high
        low_ref[:, parity * LANES : (parity + 1) * LANES] = low

    def pick(n):
        for g in range(group):
            d, c = place_of(n * group + g)

            def put(f, row, value, d=d):
                out_ref[d, pl.ds(f * slot_rows + row, 1), :] = value

            pick_rows(
                found_ref, g * chunk, cell_ref, d, c, count_ref[d], chunk, sizes, put
            )

    def body(n, carry):
        done = jnp.maximum(n - 1, 0)
        pick(done)
        hot = hot_ref[...]
        found_ref[...] = dot_nn(high_ref[...], hot) + dot_nn(low_ref[...], hot)
        build(n + 1)
        for g in range(group):
            here, _ = place_of(done * group + g)
            following, _ = place_of(done * group + g + 1)

            @pl.when((n > 0) & (here != following))
            def _(here=here):
                send(here).start()

        return carry

    lax.fori_loop(0, groups, body, 0)
    pick(groups - 1)
    for g in range(group):
        here, _ = place_of((groups - 1) * group + g)
        following, _ = place_of((groups - 1) * group + g + 1)

        @pl.when(here != following)
        def _(here=here):
            send(here).start()

    last, _ = place_of(total - 1)
    send(last).start()

    def wait_body(d, carry):
        send(d).wait()
        return carry

    lax.fori_loop(0, owners, wait_body, 0)


def gather(count, cell, field, chunk=256, group=6):
    fields, cells_j, cells_i, _ = field.shape
    owners, capacity = cell.shape
    field = field.reshape(-1, LANES)
    table = (field.shape[0] // 2, 2 * LANES)
    out = (owners, fields * capacity // LANES, LANES)
    vmem = pl.BlockSpec(memory_space=pltpu.VMEM)
    hbm = pl.BlockSpec(memory_space=pltpu.HBM)
    return pl.pallas_call(
        functools.partial(
            gather_kernel, chunk=chunk, group=group, sizes=(fields, cells_j, cells_i)
        ),
        out_shape=(
            jax.ShapeDtypeStruct(out, F32),
            pltpu.VMEM(table, BF16),
            pltpu.VMEM(table, BF16),
        ),
        in_specs=[hbm, hbm, hbm],
        out_specs=(hbm, vmem, vmem),
        scratch_shapes=[
            pltpu.VMEM(cell.shape, jnp.int32),
            pltpu.VMEM(field.shape, F32),
            pltpu.VMEM((out[0], out[1] + 8, LANES), F32),
            pltpu.VMEM((2 * LANES, LANES), BF16),
            pltpu.VMEM((2 * LANES, group * chunk), BF16),
            pltpu.VMEM((table[0], group * chunk), F32),
            pltpu.SMEM((owners * capacity // chunk,), jnp.int32),
            pltpu.SMEM((owners,), jnp.int32),
            pltpu.SemaphoreType.DMA(()),
            pltpu.SemaphoreType.DMA(()),
            pltpu.SemaphoreType.DMA((fields,)),
            pltpu.SemaphoreType.DMA((owners,)),
        ],
        compiler_params=PARAMS,
        name="gather",
    )(far(count), far(cell), far(field))


def lay_out(entries):
    lane = lax.broadcasted_iota(jnp.int32, (8, LANES), 1)
    tile = jnp.zeros((8, LANES), F32)
    for at, entry in enumerate(entries):
        tile = jnp.where(lane == at, entry, tile)
    return tile


def edge_entries(couple_ref, direction):
    row = lax.broadcasted_iota(jnp.int32, (8, LANES), 0)
    table = []
    for c in range(3):
        value = jnp.zeros((8, LANES), F32)
        for f in range(couple_ref.shape[2]):
            value = jnp.where(row == f, couple_ref[c, direction, f], value)
        table.append(value)
    return table


def prepare_i_kernel(couple_ref, i_ref, i_out, *, cells_i):
    lower, upper = i_ref[0], i_ref[1]

    def edges(matrix, direction):
        e0, e1, e2 = edge_entries(couple_ref, direction)
        table = []
        for p in range(cells_i):
            first, second = col(matrix, p * cells_i), col(matrix, p * cells_i + 1)
            table.append((first * e0 + second * e2, first * e1))
        return table

    low_edge = edges(lower, 0)
    up_edge = edges(upper, 1)
    through = []
    for p in range(cells_i):
        total = [jnp.zeros((8, LANES), F32), jnp.zeros((8, LANES), F32)]
        for q in range(p + 1):
            factor = col(upper, p * cells_i + q)
            for a in range(2):
                total[a] = total[a] + factor * low_edge[cells_i - 1 - q][a]
        through.append(total)
    last, prior = cells_i - 1, cells_i - 2
    entries = []
    for table in (through, up_edge):
        for p in range(cells_i):
            entries += [table[p][0], table[p][1]]
    entries += [-low_edge[last][0], -low_edge[last][1], -low_edge[prior][0], -low_edge[prior][1]]
    entries += [-up_edge[last][0], -up_edge[last][1], -up_edge[prior][0], -up_edge[prior][1]]
    entries += [through[last][0], through[last][1], through[prior][0], through[prior][1]]
    i_out[...] = lay_out(entries)


def prepare_i(couplings, i_tiles, cells_i):
    return pl.pallas_call(
        functools.partial(prepare_i_kernel, cells_i=cells_i),
        out_shape=pltpu.VMEM((8, LANES), F32),
        in_specs=[
            pl.BlockSpec(memory_space=pltpu.SMEM),
            pl.BlockSpec(memory_space=pltpu.VMEM),
        ],
        out_specs=pl.BlockSpec(memory_space=pltpu.VMEM),
        compiler_params=PARAMS,
        name="prepare_i",
    )(couplings, near(i_tiles))


def prepare_k_kernel(couple_ref, k_ref, k_tile, k_map, k_rows, k_carry):
    fields, length = k_ref.shape[1], k_ref.shape[2]
    row_n = lax.broadcasted_iota(jnp.int32, (length, length), 0)
    lane_n = lax.broadcasted_iota(jnp.int32, (length, length), 1)
    turn = jnp.where(row_n + lane_n == length - 1, 1.0, 0.0).astype(BF16)
    columns = jnp.zeros((length, length), F32)
    for f in range(fields):
        low, up = k_ref[0, f], k_ref[1, f]
        whole = product_nn(up, turn_rows(low, turn))
        k_map[f] = whole
        k_rows[f] = jnp.concatenate(
            [x[length - q : length - q + 1] for x in (low, whole) for q in (1, 2)]
            + [jnp.zeros((4, length), F32)],
            axis=0,
        )
        for m, matrix in enumerate((low, up, whole)):
            for q in range(2):
                value = jnp.broadcast_to(matrix[:, q : q + 1], (length, length))
                columns = jnp.where(lane_n == 16 * m + 8 * q + f, value, columns)
    columns = columns.T
    low0, low1, up0, up1, all0, all1 = (columns[8 * q : 8 * q + 8] for q in range(6))

    e0, e1, e2 = edge_entries(couple_ref, 2)
    d0, d1, d2 = edge_entries(couple_ref, 3)
    first = (low0 * e0 + low1 * e2, low0 * e1)
    through = (all0 * e0 + all1 * e2, all0 * e1)
    second = (up0 * d0 + up1 * d2, up0 * d1)
    turned = turn_lanes(jnp.concatenate(through + second, axis=0), turn)
    for a in range(4):
        k_carry[a] = turned[8 * a : 8 * a + 8]
    ends = [(pair, p) for p in (length - 1, length - 2) for pair in (0, 1)]
    k_tile[...] = lay_out(
        [-col(first[pair], p) for pair, p in ends]
        + [-col(second[pair], p) for pair, p in ends]
        + [col(through[pair], p) for pair, p in ends]
    )


def prepare_k(couplings, k_factors):
    fields, length = k_factors.shape[1], k_factors.shape[2]
    return pl.pallas_call(
        prepare_k_kernel,
        out_shape=(
            pltpu.VMEM((8, LANES), F32),
            pltpu.VMEM((fields, length, length), F32),
            pltpu.VMEM((fields, 8, length), F32),
            pltpu.VMEM((4, 8, length), F32),
        ),
        in_specs=[
            pl.BlockSpec(memory_space=pltpu.SMEM),
            pl.BlockSpec(memory_space=pltpu.VMEM),
        ],
        out_specs=(pl.BlockSpec(memory_space=pltpu.VMEM),) * 4,
        compiler_params=PARAMS,
        name="prepare_k",
    )(couplings, near(k_factors))


def mat2(a, b):
    return [
        a[0] * b[0] + a[1] * b[2],
        a[0] * b[1] + a[1] * b[3],
        a[2] * b[0] + a[3] * b[2],
        a[2] * b[1] + a[3] * b[3],
    ]


def downstream_map(tiles, base, mine):
    peers = len(tiles)
    total = [jnp.zeros((8, LANES), F32)] * 4
    for m in range(1, peers):
        entry = [col(tiles[m], base + c) for c in range(12)]
        step = mat2(mat2(entry[4:8], total), entry[0:4])
        total = [
            jnp.where(m > mine, new - back, old) for new, back, old in zip(step, entry[8:12], total)
        ]
    return total


def spread_slots(total_ref, place_ref, value_of, cell_ref, weight_ref, units, sizes, size):
    fields, cells_j, cells_i = sizes
    rows_j = 16
    chunk = size * len(units)
    per = chunk // LANES

    def joined(pick):
        return jnp.concatenate([pick(pl.ds(b, 1), pl.ds(at, size)) for b, at in units], axis=1)

    cell = joined(lambda b, at: cell_ref[b, at])
    x, y, z = (joined(lambda b, at, axis=axis: weight_ref[axis, b, at]) for axis in range(3))
    i, j, k = split_cell(cell, cells_i, cells_j)

    def hat(size, at, t):
        place = lax.broadcasted_iota(jnp.int32, (size, chunk), 0)
        return jnp.where(place == at, 1.0 - t, jnp.where(place == at + 1, t, 0.0))

    along_i = hat(cells_i, i, x)
    along_j = hat(rows_j, j, y)
    first = rows_of(k.astype(F32), 16, BF16)
    second = rows_of((k + 1).astype(F32), 16, BF16)
    remote = split(rows_of(z, 16, F32))
    close = split(rows_of(1.0 - z, 16, F32))
    zero = jnp.zeros((16, chunk), BF16)
    place = place_ref[:LANES]
    along_k = []
    for part in range(2):
        for r in range(LANES // 16):
            here = jnp.concatenate([place[16 * r : 16 * r + 16]] * per, axis=1)
            weight = jnp.where(here == second, remote[part], zero)
            along_k.append(jnp.where(here == first, close[part], weight))
    along_k = jnp.concatenate(along_k, axis=0)
    blocks = []
    for f in range(fields):
        rows = []
        for b, at in units:
            for q in range(0, size // LANES, 8):
                block = value_of(f, b, lax.div(at, LANES) + q)
                rows += [block[r : r + 1] for r in range(8)]
        value = jnp.concatenate(rows, axis=1)
        scaled = along_j * value
        blocks += [along_i * scaled[q : q + 1] for q in range(cells_j)]
    high, low = split(jnp.concatenate(blocks, axis=0))
    total_ref[...] += dot_nt(
        jnp.concatenate([high, low], axis=1), jnp.concatenate([along_k, along_k], axis=1)
    )


def scatter_own_kernel(
    count_ref,
    high_ref,
    low_ref,
    from_ref,
    cell_ref,
    weight_ref,
    total_ref,
    got_ref,
    place_ref,
    hot_ref,
    found_ref,
    *,
    sizes,
    gather_chunk,
):
    capacity = cell_ref.shape[1]
    slot_rows = capacity // LANES
    total_ref[...] = jnp.zeros(total_ref.shape, F32)
    got_ref[...] = jnp.zeros(got_ref.shape, F32)
    place_ref[...] = places(2 * LANES, LANES)
    mine = lax.axis_index("block")
    count = count_ref[mine]

    def put(f, row, value):
        got_ref[pl.ds(f * slot_rows + row, 1), :] = value

    def find_body(c, carry):
        build_hot(hot_ref, 0, from_ref, place_ref[...], mine, c, gather_chunk, sizes)
        hot = hot_ref[...]
        found_ref[...] = dot_nn(high_ref[...], hot) + dot_nn(low_ref[...], hot)
        pick_rows(found_ref, 0, from_ref, mine, c, count, gather_chunk, sizes, put)
        return carry

    lax.fori_loop(0, lax.div(count + (gather_chunk - 1), gather_chunk), find_body, 0)

    spread_slots(
        total_ref,
        place_ref,
        lambda f, b, q: got_ref[pl.ds(pl.multiple_of(f * slot_rows + q, 8), 8), :],
        cell_ref,
        weight_ref,
        [(mine, 0)],
        sizes,
        capacity,
    )


def scatter_own(count, tables, receptor, cell, weight, sizes, gather_chunk=512):
    vmem = pl.BlockSpec(memory_space=pltpu.VMEM)
    smem = pl.BlockSpec(memory_space=pltpu.SMEM)
    fields, cells_j, cells_i = sizes
    return pl.pallas_call(
        functools.partial(scatter_own_kernel, sizes=sizes, gather_chunk=gather_chunk),
        out_shape=pltpu.VMEM((fields * cells_i * cells_j, 2 * LANES), F32),
        in_specs=[smem] + [vmem] * 5,
        out_specs=vmem,
        scratch_shapes=[
            pltpu.VMEM((fields * cell.shape[1] // LANES + 8, LANES), F32),
            pltpu.VMEM((2 * LANES, LANES), BF16),
            pltpu.VMEM((2 * LANES, gather_chunk), BF16),
            pltpu.VMEM((tables[0].shape[0], gather_chunk), F32),
        ],
        compiler_params=PARAMS,
        name="scatter_own",
    )(far(count), *map(near, (*tables, receptor, cell, weight)))


def scatter_kernel(*refs, peers, chunk, base, sizes):
    factor_ref, begun_ref, got_ref, cell_ref, weight_ref, residual_ref = refs[:6]
    refs = refs[6:]
    tile_refs = refs[:peers]
    start_ref = refs[peers]
    send_refs = refs[1 + peers : 1 + 2 * peers]
    total_ref, place_ref, fold_ref, solve_ref, solve_sem = refs[1 + 2 * peers :]
    fields, cells_j, cells_i = sizes
    sources, capacity = cell_ref.shape
    rows_j = 16
    slot_rows = capacity // LANES
    solve_load = pltpu.make_async_copy(factor_ref, solve_ref, solve_sem)
    solve_load.start()
    total_ref[...] = begun_ref[...]
    place_ref[...] = places(LANES, LANES)
    own = lax.axis_index("block")

    parts = capacity // chunk
    count = (sources - 1) * parts
    group = max(g for g in range(1, 8) if count % g == 0)

    def step_body(step, carry):
        units = []
        for g in range(group):
            unit = step * group + g
            b = lax.div(unit, parts)
            b = b + (b >= own).astype(jnp.int32)
            units.append((b, pl.multiple_of(lax.rem(unit, parts) * chunk, chunk)))
        spread_slots(
            total_ref,
            place_ref,
            lambda f, b, q: got_ref[b, pl.ds(pl.multiple_of(f * slot_rows + q, 8), 8), :],
            cell_ref,
            weight_ref,
            units,
            (fields, cells_j, cells_i),
            chunk,
        )
        return carry

    lax.fori_loop(0, count // group, step_body, 0)

    count = fields * cells_j * cells_i
    fold_ref[:count] = total_ref[:, :LANES] + total_ref[:, LANES:] + residual_ref[...]
    solve_load.wait()
    mine = lax.axis_index("line")
    tiles = [ref[...] for ref in tile_refs]
    onward = downstream_map(tiles, base, mine)
    turned = mat2([col(tiles[0], base + 4 + c) for c in range(4)], onward)
    pad = jnp.zeros((rows_j - cells_j, LANES), F32)
    for f in range(fields):
        data = []
        for i in range(cells_i):
            at = pl.ds(f * cells_i * cells_j + i, cells_j, stride=cells_i)
            data.append(jnp.concatenate([fold_ref[at, :], pad], axis=0))

        def solve(direction, columns):
            result = []
            for p in range(cells_i):
                value = solve_ref[direction, f, p * cells_i] * columns[0]
                for q in range(1, p + 1):
                    value = value + solve_ref[direction, f, p * cells_i + q] * columns[q]
                result.append(value)
            return result

        first = solve(0, data)
        second = solve(1, first[::-1])
        e0, e1 = first[-1], first[-2]
        g0, g1 = second[-1], second[-2]
        m = [jnp.broadcast_to(entry[f : f + 1], (rows_j, LANES)) for entry in turned]
        h0 = g0 + m[0] * e0 + m[1] * e1
        h1 = g1 + m[2] * e0 + m[3] * e1
        for i in range(cells_i):
            at = (f * cells_i + i) * rows_j
            start_ref[at : at + rows_j] = second[cells_i - 1 - i]
        for shift in range(peers):
            ahead = mine + shift < peers
            at = f * rows_j
            send_refs[shift][at : at + rows_j] = jnp.where(ahead, e0, h0)
            at = (fields + f) * rows_j
            send_refs[shift][at : at + rows_j] = jnp.where(ahead, e1, h1)


def scatter(solve_tiles, begun, got, cell, weight, residual, tiles, base, chunk=1024):
    fields, cells_j, cells_i, _ = residual.shape
    peers = len(tiles)
    rows = fields * cells_i * 16
    vmem = pl.BlockSpec(memory_space=pltpu.VMEM)
    smem = pl.BlockSpec(memory_space=pltpu.SMEM)
    return pl.pallas_call(
        functools.partial(
            scatter_kernel,
            peers=peers,
            chunk=chunk,
            base=base,
            sizes=(fields, cells_j, cells_i),
        ),
        out_shape=(pltpu.VMEM((rows, LANES), F32),)
        + (pltpu.VMEM((2 * fields * 16, LANES), F32),) * peers,
        in_specs=[vmem] * (6 + peers),
        out_specs=(vmem,) * (1 + peers),
        scratch_shapes=[
            pltpu.VMEM((fields * cells_i * cells_j, 2 * LANES), F32),
            pltpu.VMEM((LANES, LANES), BF16),
            pltpu.VMEM((fields * cells_i * cells_j + 8 * cells_i, LANES), F32),
            pltpu.SMEM(solve_tiles.shape, F32),
            pltpu.SemaphoreType.DMA(()),
        ],
        compiler_params=PARAMS,
        name="scatter",
    )(*map(near, (solve_tiles, begun, got, cell, weight, residual.reshape(-1, LANES), *tiles)))


def middle_kernel(*refs, peers, base, fields, cells_i):
    start_ref, rows_ref, k_tile_ref = refs[:3]
    tile_refs = refs[3 : 3 + peers]
    got_refs = refs[3 + peers : 3 + 2 * peers]
    field_ref, send_hbm, end_ref, own_ref, own_sem, send_sem = refs[3 + 2 * peers :]
    own_load = pltpu.make_async_copy(tile_refs[0], own_ref, own_sem)
    own_load.start()
    rows_j = 16
    mine = lax.axis_index("line")
    tiles = [ref[...] for ref in tile_refs]
    onward = downstream_map(tiles, base, mine)
    forward = [[col(tile, base + c) for c in range(4)] for tile in tiles]
    backward = [[col(tile, base + 4 + c) for c in range(4)] for tile in tiles]
    end_ref[...] = jnp.zeros(end_ref.shape, F32)
    rows = cells_i * rows_j
    own_load.wait()
    for f in range(fields):

        def wide(entry):
            return jnp.broadcast_to(entry[f : f + 1], (rows_j, LANES))

        def advance(matrix, state, add):
            m = [wide(entry) for entry in matrix]
            return [
                m[0] * state[0] + m[1] * state[1] + add[0],
                m[2] * state[0] + m[3] * state[1] + add[1],
            ]

        got = []
        for shift in range(peers):
            low = got_refs[shift][f * rows_j : (f + 1) * rows_j]
            high = got_refs[shift][(fields + f) * rows_j : (fields + f + 1) * rows_j]
            got.append((low, high))
        zero = jnp.zeros((rows_j, LANES), F32)
        before = [zero, zero]
        for shift in range(peers - 1, 0, -1):
            new = advance(forward[shift], before, got[shift])
            before = [jnp.where(shift <= mine, n, o) for n, o in zip(new, before)]
        after = [zero, zero]
        for shift in range(1, peers):
            new = advance(backward[shift], after, got[shift])
            after = [jnp.where(shift > mine, n, o) for n, o in zip(new, after)]
        onto = advance(forward[0], before, got[0])
        after = advance(onward, onto, after)
        for p in range(cells_i):
            at = (f * cells_i + cells_i - 1 - p) * rows_j
            value = start_ref[at : at + rows_j]
            value = value - own_ref[f, 2 * p] * before[0] - own_ref[f, 2 * p + 1] * before[1]
            shift = 2 * cells_i
            value = value - own_ref[f, shift + 2 * p] * after[0]
            value = value - own_ref[f, shift + 2 * p + 1] * after[1]
            field_ref[at : at + rows_j] = value
        block = field_ref[f * rows : (f + 1) * rows]
        r_high, r_low = split(rows_ref[f])
        both = dot_nt(
            jnp.concatenate([r_high, r_low], axis=0), jnp.concatenate(split(block), axis=0)
        )
        ends = both[:8, :rows] + both[:8, rows:] + both[8:, :rows]
        for a in range(4):
            end_ref[a * fields + f : a * fields + f + 1, :] = ends[a : a + 1]
    lane = lax.broadcasted_iota(jnp.int32, (fields, LANES), 1)
    for a in range(4):
        part = end_ref[a * fields : (a + 1) * fields]
        for q in range(3):
            entry = col(k_tile_ref[0:fields], 3 * a + q)
            part = jnp.where(lane == rows_j * q + rows_j - 1, entry, part)
        end_ref[a * fields : (a + 1) * fields] = part
    sends = [
        pltpu.make_async_copy(
            end_ref.at[pl.ds(0, 4 * fields)], send_hbm.at[d], send_sem.at[d]
        )
        for d in range(send_hbm.shape[0])
    ]
    for copy in sends:
        copy.start()
    for copy in sends:
        copy.wait()


def middle(start, k_rows, k_tile, tiles, got, base, owners, fields, cells_i):
    peers = len(tiles)
    vmem = pl.BlockSpec(memory_space=pltpu.VMEM)
    smem = pl.BlockSpec(memory_space=pltpu.SMEM)
    return pl.pallas_call(
        functools.partial(middle_kernel, peers=peers, base=base, fields=fields, cells_i=cells_i),
        out_shape=(
            pltpu.VMEM(start.shape, F32),
            jax.ShapeDtypeStruct((owners, 4 * fields, LANES), F32),
        ),
        in_specs=[vmem] * (3 + 2 * peers),
        out_specs=(vmem, pl.BlockSpec(memory_space=pltpu.HBM)),
        scratch_shapes=[
            pltpu.VMEM((4 * fields + 8, LANES), F32),
            pltpu.SMEM((8, LANES), F32),
            pltpu.SemaphoreType.DMA(()),
            pltpu.SemaphoreType.DMA((owners,)),
        ],
        compiler_params=PARAMS,
        name="middle",
    )(*map(near, (start, k_rows, k_tile, *tiles, *got)))


def apply_k_kernel(field_ref, map_ref, out_ref):
    fields = map_ref.shape[0]
    rows = field_ref.shape[0] // fields
    length = map_ref.shape[1]
    row_n = lax.broadcasted_iota(jnp.int32, (length, length), 0)
    lane_n = lax.broadcasted_iota(jnp.int32, (length, length), 1)
    turn = jnp.where(row_n + lane_n == length - 1, 1.0, 0.0).astype(BF16)
    for f in range(fields):
        at = slice(f * rows, (f + 1) * rows)
        out_ref[at] = turn_lanes(product_nt(field_ref[at], map_ref[f]), turn)


def apply_k(field, k_map):
    vmem = pl.BlockSpec(memory_space=pltpu.VMEM)
    return pl.pallas_call(
        apply_k_kernel,
        out_shape=pltpu.VMEM(field.shape, F32),
        in_specs=[vmem, vmem],
        out_specs=vmem,
        compiler_params=PARAMS,
        name="apply_k",
    )(near(field), near(k_map))


def finish_kernel(start_ref, got_ref, carry_ref, out_hbm, out_ref, out_sem):
    fields, cells_j, cells_i, _ = out_hbm.shape
    rows_j = 16
    rows = cells_i * rows_j
    blocks = got_ref.shape[0]

    def send(f):
        part = out_ref.at[f, pl.ds(0, cells_j)]
        return pltpu.make_async_copy(part, out_hbm.at[f], out_sem.at[f])

    mine = lax.axis_index("block")
    zero = jnp.zeros((fields, LANES), F32)
    part = [
        [got_ref[m, fields * a : fields * (a + 1)] for a in range(4)] for m in range(blocks)
    ]
    entry = [
        [col(part[m][c // 3], rows_j * (c % 3) + rows_j - 1) for c in range(12)]
        for m in range(blocks)
    ]
    states = []
    state = [zero, zero]
    for m in range(blocks):
        states.append(state)
        p = entry[m]
        state = [
            p[0] * state[0] + p[1] * state[1] + part[m][0],
            p[2] * state[0] + p[3] * state[1] + part[m][1],
        ]
    before = [zero, zero]
    after = [zero, zero]
    state = [zero, zero]
    for m in range(blocks - 1, -1, -1):
        here = m == mine
        before = [jnp.where(here, n, o) for n, o in zip(states[m], before)]
        after = [jnp.where(here, n, o) for n, o in zip(state, after)]
        q, b = entry[m][4:8], entry[m][8:12]
        old = states[m]
        state = [
            q[0] * state[0] + q[1] * state[1] + part[m][2] - b[0] * old[0] - b[1] * old[1],
            q[2] * state[0] + q[3] * state[1] + part[m][3] - b[2] * old[0] - b[3] * old[1],
        ]
    for f in range(fields):
        carried = jnp.concatenate(
            [x[f : f + 1] for x in (before[0], before[1], after[0], after[1])]
            + [jnp.zeros((4, LANES), F32)],
            axis=0,
        )
        response = jnp.concatenate(
            [carry_ref[a, f : f + 1, :] for a in range(4)] + [jnp.zeros((4, LANES), F32)], axis=0
        )
        change = dot3(dot_tn, carried, response, 0, 0)
        value = start_ref[f * rows : (f + 1) * rows] - change
        for i in range(cells_i):
            out_ref[f, :, i, :] = value[i * rows_j : (i + 1) * rows_j]
        send(f).start()
    for f in range(fields):
        send(f).wait()


def finish(start, got, carry, shape):
    vmem = pl.BlockSpec(memory_space=pltpu.VMEM)
    smem = pl.BlockSpec(memory_space=pltpu.SMEM)
    return pl.pallas_call(
        finish_kernel,
        out_shape=jax.ShapeDtypeStruct(shape, F32),
        in_specs=[vmem, vmem, vmem],
        out_specs=pl.BlockSpec(memory_space=pltpu.HBM),
        scratch_shapes=[
            pltpu.VMEM((shape[0], 16) + shape[2:], F32),
            pltpu.SemaphoreType.DMA((shape[0],)),
        ],
        compiler_params=PARAMS,
        name="finish",
    )(near(start), near(got), near(carry))


def per_device(
    residual,
    adjoint,
    i_factors,
    k_factors,
    couplings,
    receptor_cell,
    send_count,
    donor_cell,
    donor_weight,
):
    fields, cells_i, cells_j, cells_k = adjoint.shape
    owners = receptor_cell.shape[2]
    peers = lax.axis_size("line")
    base = 4 * cells_i

    adjoint, residual = (x.transpose(0, 2, 1, 3) for x in (adjoint, residual))
    counts = send_count.reshape(owners)
    outgoing, *tables = gather(counts, receptor_cell[0, 0], adjoint)
    incoming = lax.all_to_all(outgoing, "block", split_axis=0, concat_axis=0, tiled=True)

    square = i_factors[0].reshape(2, fields, cells_i * cells_i)
    i_tiles = jnp.pad(square, ((0, 0), (0, 8 - fields), (0, LANES - cells_i * cells_i)))
    couple = couplings[0, 0].transpose(1, 0, 2)
    own = prepare_i(couple, i_tiles, cells_i)

    def shifted(value, shift):
        return lax.ppermute(value, "line", [(s, (s + shift) % peers) for s in range(peers)])

    tiles = [own] + [shifted(own, m) for m in range(1, peers)]
    k_couple, _ = lax.optimization_barrier((couple, outgoing))
    k_tile, k_map, k_rows, k_carry = prepare_k(k_couple, k_factors[0])
    counts, _ = lax.optimization_barrier((counts, k_tile))
    begun = scatter_own(
        counts,
        tables,
        receptor_cell[0, 0],
        donor_cell[0, 0],
        donor_weight[0, 0],
        (fields, cells_j, cells_i),
    )
    start, *ends = scatter(
        i_tiles,
        begun,
        incoming,
        donor_cell[0, 0],
        donor_weight[0, 0],
        residual,
        tiles,
        base,
    )
    got = [ends[0]] + [shifted(ends[m], m) for m in range(1, peers)]
    start, message = middle(
        start, k_rows, k_tile, tiles, got, base, owners, fields, cells_i
    )
    message = lax.all_to_all(message, "block", split_axis=0, concat_axis=0, tiled=True)
    start = apply_k(start, k_map)
    return finish(start, message, k_carry, residual.shape).transpose(0, 2, 1, 3)


def solution(mesh):
    return jax.shard_map(
        per_device,
        mesh=mesh,
        in_specs=(
            P(None, "line", None, "block"),
            P(None, "line", None, "block"),
            P("block", None, None, "line", None),
            P("line", None, None, "block", None),
            P("line", "block", None, None, None),
            P("line", "block", None, None),
            P("line", "block", None),
            P("line", "block", None, None),
            P("line", "block", None, None, None),
        ),
        out_specs=P(None, "line", None, "block"),
        check_vma=False,
    )
```
